32 devices in a mesh: blk: 2 (over x), rows: 16 (over z, y, core).
Axes of the slice: x: 2, y: 2, z: 4, core: 2. Of those that a mesh axis runs over, the one named last changes fastest.
Arguments:
- features: bfloat16 [8192, 128], P(('blk', 'rows')), may hold values from -6 to 6
- labels: int32 [8192], P(('blk', 'rows')), may hold values from 0 to 6
- destination: int32 [8192, 1], P(('blk', 'rows')), may hold values from 0 to 15; in each aligned block of 256 rows (0 to 255, 256 to 511, ...) at most 32 rows name the same one
- centres: bfloat16 [8192, 128], P('blk'), may hold values from -6 to 6
- tri_inverse: float32 [8192, 8192], P('blk', 'rows'), may hold values from -1 to 2, as said below
- aux_inverse: float32 [8192, 8192], P('blk', 'rows'), may hold values from -1 to 2, as said below
Outputs:
- predictions: float32 [7, 16384], P(None, ('blk', 'rows'))
The draws below stay inside these ranges and needn't reach their ends.
Inputs may be any that keep to these rules, and one draw needn't show every extreme that they name: `destination`: in each aligned block of 256 rows (the rows of one device) no value occurs more than 32 times, and some value occurs exactly 32 times. `tri_inverse`: zero below the diagonal, positive on it. `aux_inverse`: zero below the diagonal, positive on it.
All inputs are finite; a program needn't handle non-finite values.
Results may differ from the reference program's by a relative error of at most 0.0003.
Values may be sent and summed in bfloat16 or wider, within the bound.
A program may use at most 128 MiB of HBM per device.

```python
import math
import jax
import jax.numpy as jnp
import numpy as np
from jax import lax

D = 128
M = 8192
CLASSES = 7
ITERS = 2
ROWS_DEV = 256
CAP = 32
ROWS_ALL = 8192
SLOTS_ALL = 16384
N_BLK = 2
N_ROWS = 16


def triangle_draw(key):
    first_key, second_key = jax.random.split(key)
    row_ids = jnp.arange(M, dtype=jnp.int32)[:, None]
    col_ids = jnp.arange(M, dtype=jnp.int32)[None, :]
    spread = 0.6 / math.sqrt(M)
    upper = jax.random.normal(first_key, (M, M), jnp.float32) * spread
    diagonal = jax.random.uniform(second_key, (M,), jnp.float32, 0.7, 1.3)
    upper = jnp.clip(upper, -0.9, 0.9)
    return jnp.where(col_ids > row_ids, upper, 0.0) + jnp.where(col_ids == row_ids, diagonal[:, None], 0.0)


def draw_tri_inverse(key, part):
    return triangle_draw(jax.random.fold_in(key, 11))


def draw_aux_inverse(key, part):
    return triangle_draw(jax.random.fold_in(key, 23))


def place_ends(entries, stream_key, least, largest):
    index_at = [jax.random.randint(jax.random.fold_in(stream_key, axis), (), 0, length) for axis, length in enumerate(entries.shape)]
    widest = entries.shape.index(max(entries.shape))
    beside = index_at[:widest] + [(index_at[widest] + 1) % entries.shape[widest]] + index_at[widest + 1:]
    return entries.at[tuple(index_at)].set(least).at[tuple(beside)].set(largest)


def shard_levels(stream_key, dims, cuts, smallest, top_value):
    loudness, own = 1.0, jax.random.fold_in(stream_key, 6)
    for dim, blocks in cuts:
        steps = jnp.exp(jax.random.uniform(jax.random.fold_in(own, dim), (blocks,), jnp.float32, smallest / len(cuts), top_value / len(cuts)))
        loudness = loudness * jnp.repeat(steps, dims[dim] // blocks).reshape([-1 if axis == dim else 1 for axis in range(len(dims))])
    return loudness


def shared_out(stream_key, own, number, rows, number_of, top, limit, lean):
    sequence = jax.random.permutation(stream_key, number_of)
    packed, usual = load_shares(number_of, rows * top, limit, lean, True), load_shares(number_of, rows * top, limit, lean, False)
    places = jnp.arange(number_of)

    def named(tallies, offset_by):
        used = int((tallies > 0).sum())
        fixed = max(1, used // 4)
        moved = fixed + (places - fixed + offset_by * (used - fixed)) % max(1, number_of - fixed)
        return jnp.zeros((number_of,), jnp.int32).at[sequence[jnp.where(places < fixed, places, moved)]].set(jnp.asarray(tallies, jnp.int32))

    tallies = jnp.where(number % 4 == 0, named(packed, number // 4), named(usual, number - number // 4 - 1))
    mixed = jax.random.permutation(jax.random.fold_in(own, 3), number_of)
    donor, sink = mixed[0:number_of // 2 * 2:2], mixed[1:number_of // 2 * 2:2]
    room = jnp.minimum(tallies[donor] - 1, limit - tallies[sink]) // 2
    room = jnp.where((donor == sequence[0]) | (sink == sequence[0]) | (tallies[sink] == 0), 0, jnp.maximum(room, 0))
    moved = jax.random.randint(jax.random.fold_in(own, 4), (number_of // 2,), 0, 1 << 20) % (room + 1)
    tallies = tallies.at[donor].add(-moved).at[sink].add(moved)
    items = jnp.searchsorted(jnp.cumsum(tallies), jnp.arange(rows * top), side="right").astype(jnp.int32)
    listing = items.reshape(top, rows).T
    listing = listing[jax.random.permutation(jax.random.fold_in(own, 1), rows)]
    offset_by = jax.random.randint(jax.random.fold_in(own, 2), (rows, 1), 0, top)
    return jnp.take_along_axis(listing, (jnp.arange(top)[None, :] + offset_by) % top, axis=1)


def load_shares(amount, total, bound, skew, full):
    portions = [(1 << 20) // math.isqrt(rank ** skew) + 1 for rank in range(1, amount + 1)]
    largest = bound if full else min(bound, max(-(-total // amount), total * portions[0] // sum(portions)))
    least = 1 if total - largest >= amount - 1 else 0
    holding, surplus = [largest] + [least] * (amount - 1), total - largest - least * (amount - 1)
    while surplus > 0:
        movable = [i for i in range(1, amount) if holding[i] < largest] or [i for i in range(1, amount) if holding[i] < bound]
        mass, remaining = sum([portions[i] for i in movable]), surplus
        for i in movable:
            addition = min(bound - holding[i], max(1, remaining * portions[i] // mass), surplus)
            holding[i] = holding[i] + addition
            surplus = surplus - addition
    return np.array(holding)


def centred(own_key, shape, width, limit, shards=(), kind=jnp.bfloat16):
    entries = jax.random.normal(own_key, shape, jnp.float32) * width
    if len(shards) > 0:
        entries = shard_levels(own_key, shape, shards, -0.22, 0.18) * entries
    return jnp.clip(entries, min=-limit, max=limit).astype(kind)


def setup_inputs(seed: int = 0) -> dict:
    seeds = jax.random.split(jax.random.key(seed), 7)
    features = centred(seeds[0], (ROWS_ALL, D), 1.0, 6.0, ((0, 32),))
    labels = place_ends(jax.random.randint(seeds[1], (ROWS_ALL,), 0, CLASSES), jax.random.fold_in(seeds[1], 1), 0, CLASSES - 1).astype(jnp.int32)
    destination_keys = jax.random.split(jax.random.fold_in(seeds[2], 1), ROWS_ALL // ROWS_DEV)
    destination_turns = jax.random.permutation(jax.random.fold_in(seeds[2], 3), ROWS_ALL // ROWS_DEV)
    destination = jax.vmap(lambda own, number: shared_out(jax.random.fold_in(seeds[2], 2), own, number, ROWS_DEV, N_ROWS, 1, CAP, 2))(destination_keys, destination_turns).reshape((ROWS_ALL, 1))
    centres = centred(seeds[3], (M, D), 1.0, 6.0, ((0, 2),))
    tri_inverse = draw_tri_inverse(jax.random.fold_in(seeds[6], 71), 0)
    aux_inverse = draw_aux_inverse(jax.random.fold_in(seeds[6], 71), 0)
    return dict(features=features, labels=labels, destination=destination, centres=centres, tri_inverse=tri_inverse, aux_inverse=aux_inverse)


ridge_weight = 0.1
highest = lax.Precision.HIGHEST


def as_bf16(values):
    return lax.optimization_barrier(values.astype(jnp.bfloat16)).astype(jnp.float32)


def reference(features, labels, destination, centres, tri_inverse, aux_inverse):
    scale = 2.0 / D
    count_all = float(ROWS_ALL)
    centre_f = centres.astype(jnp.float32)
    centre_norm = jnp.sum(centre_f * centre_f, axis=1)
    block = math.gcd(ROWS_ALL, 1024)
    stacked = features.reshape(ROWS_ALL // block, block, D)
    class_ids = jnp.arange(CLASSES, dtype=jnp.int32)[:, None]
    targets = jnp.where(labels[None, :] == class_ids, 1.0, -1.0).astype(jnp.float32)
    stacked_targets = targets.reshape(CLASSES, ROWS_ALL // block, block).transpose(1, 0, 2)

    def tile_of(rows_x):
        rows_f = rows_x.astype(jnp.float32)
        rows_norm = jnp.sum(rows_f * rows_f, axis=1)
        inner = jnp.dot(rows_f, centre_f.T, precision=highest)
        return as_bf16(jnp.exp(-(rows_norm[:, None] + centre_norm[None, :] - 2.0 * inner) * scale))

    def gram(vector):
        low = as_bf16(vector)

        def visit(carry, rows_x):
            tile = tile_of(rows_x)
            image = as_bf16(jnp.dot(low, tile.T, precision=highest))
            return carry + jnp.dot(image, tile, precision=highest), None

        total, _ = lax.scan(visit, jnp.zeros((CLASSES, M), jnp.float32), stacked)
        return total / count_all

    def visit_targets(carry, pieces):
        rows_x, rows_targets = pieces
        return carry + jnp.dot(rows_targets, tile_of(rows_x), precision=highest), None

    kernel_targets, _ = lax.scan(visit_targets, jnp.zeros((CLASSES, M), jnp.float32), (stacked, stacked_targets))

    def forward(factor, vector):
        return jnp.dot(vector, factor.T, precision=highest)

    def backward(factor, vector):
        return jnp.dot(vector, factor, precision=highest)

    def system(vector):
        first = forward(aux_inverse, vector)
        second = forward(tri_inverse, first)
        third = backward(tri_inverse, gram(second))
        return backward(aux_inverse, third + ridge_weight * first)

    rhs = backward(aux_inverse, backward(tri_inverse, kernel_targets / count_all))
    solution = jnp.zeros((CLASSES, M), jnp.float32)
    residual = rhs
    direction = rhs
    norm_now = jnp.sum(residual * residual, axis=1, keepdims=True)
    for step in range(ITERS):
        image = system(direction)
        step_size = norm_now / jnp.sum(direction * image, axis=1, keepdims=True)
        solution = solution + step_size * direction
        residual = residual - step_size * image
        norm_next = jnp.sum(residual * residual, axis=1, keepdims=True)
        direction = residual + (norm_next / norm_now) * direction
        norm_now = norm_next
    coefficients = forward(tri_inverse, forward(aux_inverse, solution))
    low_coeff = as_bf16(coefficients)

    def score_block(rows_x):
        return jnp.dot(low_coeff, tile_of(rows_x).T, precision=highest)

    scores = lax.map(score_block, stacked).transpose(1, 0, 2).reshape(CLASSES, ROWS_ALL)

    devices = N_BLK * N_ROWS
    target = destination[:, 0].reshape(devices, ROWS_DEV)
    picks = (target[:, :, None] == jnp.arange(N_ROWS, dtype=jnp.int32)[None, None, :]).astype(jnp.int32)
    before = jnp.sum((jnp.cumsum(picks, axis=1) - picks) * picks, axis=2)
    device_id = jnp.arange(devices, dtype=jnp.int32)[:, None]
    group_of = device_id // N_ROWS
    source = device_id % N_ROWS
    slot = (((group_of * N_ROWS + target) * N_ROWS + source) * CAP + before).reshape(ROWS_ALL).astype(jnp.int32)
    predictions = jnp.zeros((CLASSES, SLOTS_ALL), jnp.float32).at[:, slot].set(scores)
    return predictions
```

```python
import functools

import jax
import jax.numpy as jnp
from jax import lax
from jax.experimental import pallas as pl
from jax.experimental.pallas import tpu as pltpu
from jax.sharding import PartitionSpec as P

CLASSES = 7
PAD = 8
LANES = 128
MESH = pl.DeviceIdType.MESH
ridge_weight = 0.1
highest = lax.Precision.HIGHEST

PLANES = 2
LINE = 16
HALF = LINE // 2
NEAR = 4
FLIPPED = (((1,), (1,)), ((), ()))
STRAIGHT = (((1,), (0,)), ((), ()))

dma = pltpu.SemaphoreType.DMA


def spot(index, chunk):
    return pl.ds(pl.multiple_of(index * chunk, chunk), chunk)


def dot(left, right, dims):
    return lax.dot_general(left, right, dims, preferred_element_type=jnp.float32)


def stacked(vector):
    high = vector.astype(jnp.bfloat16).astype(jnp.float32)
    return jnp.concatenate([high, vector - high], axis=0).astype(jnp.bfloat16)


def fold(product):
    return product[:PAD] + product[PAD:]


def tree_sum(terms):
    while len(terms) > 1:
        pairs = [terms[i] + terms[i + 1] for i in range(0, len(terms) - 1, 2)]
        terms = pairs + terms[len(pairs) * 2 :]
    return terms[0]


def diagonal(width):
    sub = lax.broadcasted_iota(jnp.int32, (PAD, width), 0)
    lane = lax.broadcasted_iota(jnp.int32, (PAD, width), 1)
    return sub == lane


def to_lanes(column, width):
    spread = jnp.where(diagonal(width), column, 0.0)
    return jnp.sum(spread, axis=0, keepdims=True)


def to_column(row):
    spread = jnp.where(diagonal(row.shape[1]), row, 0.0)
    return jnp.sum(spread, axis=1, keepdims=True)


def with_scalars(vector, column):
    lines = lax.broadcasted_iota(jnp.int32, vector.shape, 0)
    return jnp.where(lines == PAD - 1, to_lanes(column, vector.shape[1]), vector)


def ratio(above, below):
    lines = lax.broadcasted_iota(jnp.int32, above.shape, 0)
    return jnp.where(lines < CLASSES, above / below, 0.0)


def row_sum(values):
    return jnp.sum(values, axis=1, keepdims=True)


def fused_kernel(count_all, scale, feat, label, dest, cent, tri_hbm, aux_hbm, out, *scratch):
    (
        stage, tri, aux, km, cn, place, feat_in, tgt, tgt_in,
        rs_out, rs_in, ag, w_own, w_in, w_cross, p_own, p_in, r_vec,
        c_out, c_keep, c_in, f_out, f_in, f_vec, e_own, e_in, e_vec, m_out, m_in,
        load_sem, far_send, far_recv, w_send, w_relay, w_recv, x_recv, f_send, f_recv,
        one_send, one_recv,
    ) = scratch
    b, r = lax.axis_index("blk"), lax.axis_index("rows")
    z, c = r // NEAR, lax.rem(r, 2)
    mate = r + 1 - 2 * c
    across = 1 - b
    chunk = ag.shape[3]
    own_rows = feat.shape[0]
    cols = tri.shape[2]
    low_plane, low_line = b == 0, r < HALF
    active = jnp.logical_or(low_plane, r >= HALF)
    pending = []

    def settle():
        for action in pending:
            action()
        pending.clear()

    def remote(source, target, send_sem, recv_sem, device):
        return pltpu.make_async_remote_copy(
            src_ref=source, dst_ref=target, send_sem=send_sem, recv_sem=recv_sem,
            device_id=device, device_id_type=MESH,
        )

    def loop(count, body):
        def step(i, carry):
            body(i)
            return carry

        lax.fori_loop(0, count, step, 0)

    def group(j):
        return lax.rem(z + j, 2) + 2 * lax.rem(z // 2 + j // 2, 2)

    barrier = pltpu.get_barrier_semaphore()

    def hello(k):
        number = lax.rem(b * LINE + r + k + 1, PLANES * LINE)
        pl.semaphore_signal(
            barrier, inc=1, device_id=(number // LINE, lax.rem(number, LINE)), device_id_type=MESH
        )

    loop(PLANES * LINE - 1, hello)
    loads = [
        pltpu.make_async_copy(source, stage.at[i], load_sem.at[i])
        for i, source in enumerate((tri_hbm, aux_hbm))
    ]
    for load in loads:
        load.start()

    class_rows = lax.broadcasted_iota(jnp.int32, (PAD, own_rows), 0)
    hits = jnp.where(label[...] == class_rows, 1.0, -1.0)
    tgt[...] = jnp.where(class_rows < CLASSES, hits, 0.0)

    def squares_of_centres(q):
        values = cent[spot(q, chunk), :].astype(jnp.float32)
        values = values * values
        high = values.astype(jnp.bfloat16)
        low = (values - high.astype(jnp.float32)).astype(jnp.bfloat16)
        ones = jnp.ones((PAD, values.shape[1]), jnp.bfloat16)
        cn[q] = dot(ones, high, FLIPPED) + dot(ones, low, FLIPPED)

    def build(source, half):
        values = source[...].astype(jnp.float32)
        norm = row_sum(values * values)

        def visit(q):
            inner = dot(source[...], cent[spot(q, chunk), :], FLIPPED)
            distance = norm + cn[q][:1] - 2.0 * inner
            km[q, spot(half, own_rows), :] = jnp.exp(-distance * scale).astype(jnp.bfloat16)

        loop(LINE, visit)

    pl.semaphore_wait(barrier, PLANES * LINE - 1)
    shares = [
        remote(feat, feat_in, one_send.at[0], one_recv.at[0], (across, r)),
        remote(tgt, tgt_in, one_send.at[1], one_recv.at[1], (across, r)),
    ]
    for share in shares:
        share.start()
    loop(LINE, squares_of_centres)
    build(feat, b)
    for share in shares:
        share.wait_recv()
    build(feat_in, across)
    for share in shares:
        share.wait_send()
    mine, other = tgt[...], tgt_in[...]
    targets = jnp.concatenate(
        [jnp.where(low_plane, mine, other), jnp.where(low_plane, other, mine)], axis=1
    ).astype(jnp.bfloat16)

    def split(index, target):
        loads[index].wait()

        def visit(i):
            piece = spot(i, chunk)
            values = stage[index, piece, :]
            high = values.astype(jnp.bfloat16)
            target[0, piece, :] = high
            target[1, piece, :] = (values - high.astype(jnp.float32)).astype(jnp.bfloat16)

        loop(LINE, visit)

    def find_places():
        to = dest[...].astype(jnp.float32)
        sub = lax.broadcasted_iota(jnp.int32, (own_rows, own_rows), 0)
        lane = lax.broadcasted_iota(jnp.int32, (own_rows, own_rows), 1)
        to_row = jnp.sum(jnp.where(sub == lane, to, 0.0), axis=0, keepdims=True)
        same = jnp.logical_and(to == to_row, lane < sub)
        before = row_sum(jnp.where(same, 1.0, 0.0))
        position = to * LANES + before

        def visit(q):
            lanes = lax.broadcasted_iota(jnp.int32, (own_rows, own_rows), 1) + q * own_rows
            hit = jnp.where(lanes.astype(jnp.float32) == position, 1.0, 0.0)
            place[:, spot(q, own_rows)] = hit.astype(jnp.bfloat16)

        loop(place.shape[1] // own_rows, visit)

    def scatter(phase, term, sources_all, meanwhile=None):
        def copy(q):
            return remote(
                rs_out.at[phase, q], rs_in.at[phase, r],
                far_send.at[2 * phase, q], far_recv.at[2 * phase, r], (b, q),
            )

        def send():
            def visit(step):
                first = group(NEAR - 1 - step) * NEAR
                for i in range(NEAR):
                    rs_out[phase, first + i] = term(first + i)
                for i in range(NEAR):

                    @pl.when(first + i != r)
                    def _():
                        copy(first + i).start()

            loop(NEAR, visit)
            rs_in[phase, r] = rs_out[phase, r]

        def left():
            def visit(q):
                @pl.when(q != r)
                def _():
                    copy(q).wait_send()

            loop(LINE, visit)

        def gated(action):
            if sources_all:
                action()
            else:
                pl.when(active)(action)

        gated(send)
        settle()
        if meanwhile is not None:
            meanwhile()

        def arrive(q):
            wanted = q != r
            if not sources_all:
                wanted = jnp.logical_and(wanted, jnp.logical_or(low_plane, q >= HALF))

            @pl.when(wanted)
            def _():
                remote(
                    rs_out.at[phase, q], rs_in.at[phase, q],
                    far_send.at[2 * phase, q], far_recv.at[2 * phase, q], (b, r),
                ).wait_recv()

        loop(LINE, arrive)
        pending.append(lambda: gated(left))
        upper = tree_sum([rs_in[phase, q] for q in range(HALF, LINE)])
        if sources_all:
            return upper + tree_sum([rs_in[phase, q] for q in range(HALF)])
        ag[phase, r] = upper

        @pl.when(low_plane)
        def _():
            ag[phase, r] += tree_sum([rs_in[phase, q] for q in range(HALF)])

        return ag[phase, r]

    def gather(phase, mine, width, use, meanwhile=None):
        ag[phase, r] = mine

        def copy(q):
            return remote(
                ag.at[phase, r], ag.at[phase, r],
                far_send.at[2 * phase + 1, q], far_recv.at[2 * phase + 1, r], (b, q),
            )

        def send(step):
            first = group(NEAR - 1 - step) * NEAR
            for i in range(NEAR):

                @pl.when(first + i != r)
                def _():
                    copy(first + i).start()

        loop(NEAR, send)
        settle()
        if meanwhile is not None:
            meanwhile()

        def visit(j, carry):
            first = group(j) * NEAR
            for i in range(NEAR):
                source = first + i

                @pl.when(source != r)
                def _():
                    remote(
                        ag.at[phase, source], ag.at[phase, source],
                        far_send.at[2 * phase + 1, source], far_recv.at[2 * phase + 1, source],
                        (b, r),
                    ).wait_recv()

            for i in range(NEAR):
                carry = carry + use(first + i, stacked(ag[phase, first + i]))
            return carry

        total = lax.fori_loop(0, NEAR, visit, jnp.zeros((2 * PAD, width), jnp.float32))

        def left():
            def visit(q):
                @pl.when(q != r)
                def _():
                    copy(q).wait_send()

            loop(LINE, visit)

        pending.append(left)
        return fold(total)

    def scalars(phase):
        rows = [ag[phase, q] for q in range(LINE)]
        return to_column(tree_sum(rows)[PAD - 1 :])

    def swap(own, landing, index):
        copy = remote(own, landing, one_send.at[index], one_recv.at[index], (across, r))
        copy.start()
        settle()
        copy.wait_recv()
        pending.append(copy.wait_send)

    def factor_rows(factor):
        def use(q, low):
            return dot(low, factor[0, spot(q, chunk), :], STRAIGHT) + dot(
                low, factor[1, spot(q, chunk), :], STRAIGHT
            )

        return use

    def factor_chunk(factor, low):
        def term(q):
            return fold(
                dot(low, factor[0, spot(q, chunk), :], FLIPPED)
                + dot(low, factor[1, spot(q, chunk), :], FLIPPED)
            )

        return term

    def turn(it, product):
        w_own[it] = product
        base = b * HALF

        def inside(q):
            return remote(
                w_own.at[it], w_in.at[it, r - base], w_send.at[it, q], w_recv.at[it, r - base], (b, q)
            )

        def outside(q):
            return remote(
                w_own.at[it], w_cross.at[it, r - HALF],
                w_send.at[it, q], x_recv.at[it, r - HALF], (1, q),
            )

        def relay(t):
            return remote(
                w_in.at[it, t], w_in.at[it, t], w_relay.at[it, t], w_recv.at[it, t], (b, mate)
            )

        def near(act):
            def visit(i):
                q = base + i

                @pl.when(q != r)
                def _():
                    act(inside(q))

            return lambda: loop(HALF, visit)

        def far(act):
            return lambda: loop(HALF // 2, lambda m: act(inside(HALF + 2 * m + c)))

        def over(act):
            return lambda: loop(HALF, lambda i: act(outside(HALF + i)))

        holder = jnp.logical_and(r >= base, r < base + HALF)
        first_low = jnp.logical_and(low_plane, low_line)
        first_high = jnp.logical_and(low_plane, r >= HALF)

        @pl.when(holder)
        def _():
            w_in[it, r - base] = w_own[it]

        def start(copy):
            copy.start()

        def left(copy):
            copy.wait_send()

        pl.when(first_low)(far(start))
        pl.when(holder)(near(start))
        pl.when(first_high)(over(start))
        settle()

        def arrival(t):
            remote(
                w_own.at[it], w_in.at[it, t], w_send.at[it, t], w_recv.at[it, t], (b, r)
            ).wait_recv()

        @pl.when(first_high)
        def _():
            def visit(m):
                arrival(2 * m + c)
                relay(2 * m + c).start()

            loop(HALF // 2, visit)

        p_own[it] = jnp.zeros(p_own.shape[1:], jnp.float32)

        @pl.when(active)
        def _():
            def visit(i, carry):
                t = 2 * lax.rem(i, HALF // 2) + lax.rem(c + i // (HALF // 2), 2)
                direct = jnp.logical_and(holder, base + t != r)
                relayed = jnp.logical_and(first_high, lax.rem(t, 2) != c)

                @pl.when(jnp.logical_or(direct, relayed))
                def _():
                    arrival(t)

                @pl.when(b == 1)
                def _():
                    remote(
                        w_own.at[it], w_cross.at[it, t], w_send.at[it, t], x_recv.at[it, t], (b, r)
                    ).wait_recv()
                    w_in[it, t] += w_cross[it, t]

                low = stacked(w_in[it, t])
                rows = spot(t, cols)
                return carry + dot(low, aux[0, rows, :], STRAIGHT) + dot(low, aux[1, rows, :], STRAIGHT)

            total = lax.fori_loop(0, HALF, visit, jnp.zeros((2 * PAD, cols), jnp.float32))
            p_own[it] = fold(total)

        def all_left():
            pl.when(first_low)(far(left))
            pl.when(holder)(near(left))
            pl.when(first_high)(over(left))
            pl.when(first_high)(lambda: loop(HALF // 2, lambda m: relay(2 * m + c).wait_send()))

        pending.append(all_left)

    def spread(it, vector):
        pair = remote(
            c_out.at[it], c_in.at[it], one_send.at[4 + it], one_recv.at[4 + it], (b, mate)
        )
        low = stacked(vector)
        term = factor_chunk(aux, low)

        def targets_of(act, keep):
            def visit(t):
                here = b * HALF + t

                @pl.when(here != r)
                def _():
                    act(
                        remote(
                            f_out.at[it, t], f_in.at[it, r],
                            f_send.at[0, t], f_recv.at[it, r], (b, here),
                        )
                    )

                if keep:

                    @pl.when(here == r)
                    def _():
                        f_in[it, r] = f_out[it, t]

                @pl.when(b == 1)
                def _():
                    act(
                        remote(
                            f_out.at[it, t], f_in.at[it, r],
                            f_send.at[1, t], f_recv.at[it, r], (0, here),
                        )
                    )

            return visit

        @pl.when(active)
        def _():
            def theirs(t):
                c_out[it, t] = term(2 * t + 1 - c)

            loop(HALF, theirs)
            pair.start()

            def ours(t):
                c_keep[t] = term(2 * t + c)

            loop(HALF, ours)
            pair.wait_recv()
            sends = targets_of(lambda copy: copy.start(), True)

            def visit(t):
                f_out[it, t] = c_keep[t] + c_in[it, t]
                sends(t)

            loop(HALF, visit)

        settle()

        def left():
            @pl.when(active)
            def _():
                pair.wait_send()
                loop(HALF, targets_of(lambda copy: copy.wait_send(), False))

        pending.append(left)

        @pl.when(active)
        def _():
            def arrive(q):
                elsewhere = jnp.logical_or(q != r, jnp.logical_and(low_plane, r >= HALF))

                @pl.when(jnp.logical_and(elsewhere, jnp.logical_or(low_line, q >= HALF)))
                def _():
                    remote(
                        f_out.at[it, 0], f_in.at[it, q],
                        f_send.at[0, 0], f_recv.at[it, q], (b, r),
                    ).wait_recv()

            loop(LINE, arrive)
            for side in range(2):
                columns = slice(side * chunk, (side + 1) * chunk)
                f_vec[it, :, columns] = tree_sum([f_in[it, q] for q in range(HALF + side, LINE, 2)])

            @pl.when(low_line)
            def _():
                for side in range(2):
                    columns = slice(side * chunk, (side + 1) * chunk)
                    f_vec[it, :, columns] += tree_sum([f_in[it, q] for q in range(side, HALF, 2)])

    def onto_centres(low):
        return lambda q: dot(low, km[q], STRAIGHT)

    def onto_rows(q, low):
        return dot(low, km[q], FLIPPED)

    f_vec[0] = jnp.zeros(f_vec.shape[1:], jnp.float32)
    f_vec[1] = jnp.zeros(f_vec.shape[1:], jnp.float32)
    start = scatter(0, onto_centres(targets), True, lambda: split(0, tri)) / count_all
    turned = gather(0, start, cols, factor_rows(tri), lambda: split(1, aux))
    turn(0, turned)
    swap(p_own.at[0], p_in.at[0], 2)
    residual = p_own[0] + p_in[0]
    r_vec[...] = residual
    norm = row_sum(residual * residual)
    spread(0, residual)
    mine = scatter(1, factor_chunk(tri, stacked(f_vec[0])), False, find_places)
    image = gather(1, with_scalars(mine, norm), 2 * own_rows, onto_rows)
    norm_first = scalars(1)

    def curve_of(it, partial, forward):
        own = with_scalars(partial, ridge_weight * row_sum(forward * forward))
        e_own[it] = own
        swap(e_own.at[it], e_in.at[it], 6 + it)
        theirs = e_in[it]
        ridge = jnp.where(low_plane, own, theirs)[PAD - 1 :]
        return own + theirs, to_column(ridge)

    exact, ridge = curve_of(0, image, f_vec[0])
    e_vec[...] = exact
    low = exact.astype(jnp.bfloat16)
    curve = row_sum(low.astype(jnp.float32) * exact) / count_all + ridge
    gram = scatter(2, onto_centres(low), True) / count_all
    turned = gather(2, with_scalars(gram, curve), cols, factor_rows(tri))
    step_first = ratio(norm_first, scalars(2))
    holds = jnp.logical_or(b == 1, low_line)
    turn(1, jnp.where(holds, turned + ridge_weight * f_vec[0], turned))
    swap(p_own.at[1], p_in.at[1], 3)
    residual = r_vec[...] - step_first * (p_own[1] + p_in[1])
    norm = row_sum(residual * residual)
    spread(1, residual)
    mine = scatter(3, factor_chunk(tri, stacked(f_vec[1])), False)
    image = gather(3, with_scalars(mine, norm), 2 * own_rows, onto_rows)
    norm_next = scalars(3)
    weight = ratio(norm_next, norm_first)
    exact, ridge = curve_of(1, image, f_vec[1] + weight * f_vec[0])
    exact = exact + weight * e_vec[...]
    low = exact.astype(jnp.bfloat16).astype(jnp.float32)
    curve = row_sum(low * exact) / count_all + ridge

    wide = LANES // 4
    settle()
    e_own[1] = exact
    ours = spot(b, own_rows)
    pieces = jnp.concatenate(
        [stacked(e_own[1, :, ours]), stacked(step_first * e_vec[:, ours])], axis=0
    )

    def move(q):
        return remote(
            m_out.at[q], m_in.at[r], far_send.at[8, q], far_recv.at[8, r], (b, q)
        )

    curve_row = to_lanes(curve, LANES)
    last = lax.broadcasted_iota(jnp.int32, (PAD, LANES), 0) == PAD - 1

    def put(step):
        first = group(NEAR - 1 - step) * NEAR
        both = dot(pieces, place[:, spot(first // NEAR, NEAR * LANES)], STRAIGHT)
        second, early = fold(both[: 2 * PAD]), fold(both[2 * PAD :])
        for i in range(NEAR):
            lanes = slice(i * LANES, (i + 1) * LANES)
            tile = second[:, lanes] + pltpu.roll(early[:, lanes], wide, 1)
            m_out[first + i] = jnp.where(last, curve_row, tile)
        for i in range(NEAR):

            @pl.when(first + i != r)
            def _():
                move(first + i).start()

    loop(NEAR, put)
    m_in[r] = m_out[r]
    settle()

    def arrive(q):
        @pl.when(q != r)
        def _():
            remote(
                m_out.at[q], m_in.at[q], far_send.at[8, q], far_recv.at[8, q], (b, r)
            ).wait_recv()

    loop(LINE, arrive)
    tiles = [m_in[q] for q in range(LINE)]
    step_next = ratio(norm_next, to_column(tree_sum(tiles)[PAD - 1 :]))
    band = lax.broadcasted_iota(jnp.int32, (PAD, LANES), 1) // wide
    for four in range(LINE // 4):
        total = None
        for i in range(4):
            tile = tiles[four * 4 + i]
            value = pltpu.roll(tile, LANES - wide, 1) + step_next * tile
            if i > 0:
                value = pltpu.roll(value, i * wide, 1)
            total = value if total is None else jnp.where(band == i, value, total)
        out[:, four * LANES : (four + 1) * LANES] = total[:CLASSES]

    def moved(q):
        @pl.when(q != r)
        def _():
            move(q).wait_send()

    loop(LINE, moved)


def fused(features, labels, destination, centres, tri_inverse, aux_inverse):
    own_rows, width = features.shape
    rows, cols = tri_inverse.shape
    chunk = rows // LINE
    slots = LINE * max(2, 2 * own_rows // LINE)

    def floats(*shape):
        return pltpu.VMEM(shape, jnp.float32)

    def halves(*shape):
        return pltpu.VMEM(shape, jnp.bfloat16)

    scratch = [
        floats(2, rows, cols),
        halves(2, rows, cols),
        halves(2, rows, cols),
        halves(LINE, PLANES * own_rows, chunk),
        floats(LINE, PAD, chunk),
        halves(own_rows, LINE * LANES),
        halves(own_rows, width),
        floats(PAD, own_rows),
        floats(PAD, own_rows),
        floats(4, LINE, PAD, chunk),
        floats(4, LINE, PAD, chunk),
        floats(4, LINE, PAD, chunk),
        floats(2, PAD, cols),
        floats(2, HALF, PAD, cols),
        floats(2, HALF, PAD, cols),
        floats(2, PAD, cols),
        floats(2, PAD, cols),
        floats(PAD, cols),
        floats(2, HALF, PAD, chunk),
        floats(HALF, PAD, chunk),
        floats(2, HALF, PAD, chunk),
        floats(2, HALF, PAD, chunk),
        floats(2, LINE, PAD, chunk),
        floats(2, PAD, cols),
        floats(2, PAD, PLANES * own_rows),
        floats(2, PAD, PLANES * own_rows),
        floats(PAD, PLANES * own_rows),
        floats(LINE, PAD, LANES),
        floats(LINE, PAD, LANES),
        dma((2,)),
        dma((9, LINE)),
        dma((9, LINE)),
        dma((2, LINE)),
        dma((2, HALF)),
        dma((2, HALF)),
        dma((2, HALF)),
        dma((2, HALF)),
        dma((2, LINE)),
        dma((8,)),
        dma((8,)),
    ]
    whole = pl.BlockSpec(memory_space=pltpu.VMEM)
    away = pl.BlockSpec(memory_space=pltpu.MemorySpace.HBM)
    return pl.pallas_call(
        functools.partial(fused_kernel, float(own_rows * PLANES * LINE), 2.0 / width),
        out_shape=jax.ShapeDtypeStruct((CLASSES, slots), jnp.float32),
        in_specs=[whole] * 4 + [away] * 2,
        out_specs=whole,
        scratch_shapes=scratch,
        compiler_params=pltpu.CompilerParams(
            collective_id=0, has_side_effects=True, vmem_limit_bytes=56 * 1024 * 1024
        ),
    )(features, labels[None, :], destination, centres, tri_inverse, aux_inverse)


def three_parts(x):
    high = x.astype(jnp.bfloat16).astype(jnp.float32)
    rest = x - high
    mid = rest.astype(jnp.bfloat16).astype(jnp.float32)
    return high, mid, rest - mid


def exact_product(dims, vector, block):
    parts = jnp.concatenate(three_parts(vector), axis=0).astype(jnp.bfloat16)
    total = None
    for part in reversed(block):
        product = dot(parts, part.astype(jnp.bfloat16), dims)
        product = product[2 * PAD :] + product[PAD : 2 * PAD] + product[:PAD]
        total = product if total is None else total + product
    return total


def forward_kernel(u_ref, block_ref, o_ref):
    o_ref[...] = exact_product(FLIPPED, u_ref[...], three_parts(block_ref[...]))


def backward_kernel(u_ref, block_ref, o_ref):
    product = exact_product(STRAIGHT, u_ref[...], three_parts(block_ref[...]))

    @pl.when(pl.program_id(0) == 0)
    def _():
        o_ref[...] = product

    @pl.when(pl.program_id(0) > 0)
    def _():
        o_ref[...] += product


STEP = 512

def factor_forward(block, vector):
    rows, cols = block.shape
    return pl.pallas_call(
        forward_kernel,
        grid=(rows // STEP,),
        in_specs=[
            pl.BlockSpec((PAD, cols), lambda i: (0, 0)),
            pl.BlockSpec((STEP, cols), lambda i: (i, 0)),
        ],
        out_specs=pl.BlockSpec((PAD, STEP), lambda i: (0, i)),
        out_shape=jax.ShapeDtypeStruct((PAD, rows), jnp.float32),
    )(vector, block)


def factor_backward(block, vector):
    rows, cols = block.shape
    return pl.pallas_call(
        backward_kernel,
        grid=(rows // STEP,),
        in_specs=[
            pl.BlockSpec((PAD, STEP), lambda i: (0, i)),
            pl.BlockSpec((STEP, cols), lambda i: (i, 0)),
        ],
        out_specs=pl.BlockSpec((PAD, cols), lambda i: (0, 0)),
        out_shape=jax.ShapeDtypeStruct((PAD, cols), jnp.float32),
    )(vector, block)


def square_norms(rows_x):
    return jnp.einsum("nd,nd->n", rows_x, rows_x, preferred_element_type=jnp.float32)


def plane_sum(x):
    return lax.psum(x, "rows")


def joint_sum(kind, nb, nr, block, *operands):
    x = operands[0]
    if kind == "plane":
        out = plane_sum(x)
        lines = jnp.arange(PAD, dtype=jnp.int32)[:, None]
        return out, factor_backward(block, jnp.where(lines < CLASSES, out, 0.0))
    if kind == "turn":
        width = x.shape[1] * nr // nb
        full = lax.all_gather(lax.psum(x, "blk") + operands[1], "rows", axis=1, tiled=True)
        out = lax.dynamic_slice_in_dim(full, lax.axis_index("blk") * width, width, 1)
        return out, factor_backward(block, out)
    if kind == "slice":
        size = x.shape[1] * nb // nr
        full = lax.all_gather(lax.psum(x, "rows"), "blk", axis=1, tiled=True)
        out = lax.dynamic_slice_in_dim(full, lax.axis_index("rows") * size, size, 1)
    else:
        out = operands[1] + operands[2] * lax.psum(x, "blk")
    return out, factor_forward(block, out)


def to_low(values):
    return lax.reduce_precision(values, 8, 7).astype(jnp.bfloat16)


def with_row(vector, scalars):
    return vector + jnp.pad(scalars[None, :], ((PAD - 1, 0), (0, vector.shape[1] - PAD)))


def on_device(nb, nr, features, labels, destination, centres, tri_inverse, aux_inverse):
    own_rows, width = features.shape
    capacity = max(2, 2 * own_rows // nr)
    scale = 2.0 / width
    count_all = float(own_rows * nb * nr)
    b = lax.axis_index("blk")
    class_rows = jnp.arange(PAD, dtype=jnp.int32)[:, None]
    real = class_rows < CLASSES

    tags = jnp.pad(labels.astype(jnp.bfloat16), (0, -own_rows % (16 * width)))
    tags = tags.reshape(-1, width)
    shared = lax.all_gather(jnp.concatenate([features, tags], axis=0), "blk", axis=0)
    rows_x = shared[:, :own_rows].reshape(nb * own_rows, width)
    tags = shared[:, own_rows:].reshape(nb, -1)[:, :own_rows].reshape(nb * own_rows)
    centre_norm = square_norms(centres)
    rows_norm = square_norms(rows_x)
    inner = lax.dot_general(
        rows_x, centres, (((1,), (1,)), ((), ())), preferred_element_type=jnp.float32
    )
    kmat = jnp.exp(-(rows_norm[:, None] + centre_norm[None, :] - 2.0 * inner) * scale).astype(
        jnp.bfloat16
    )
    hits = tags.astype(jnp.float32)[None, :] == class_rows.astype(jnp.float32)
    targets = jnp.where(real, jnp.where(hits, 1.0, -1.0), 0.0).astype(jnp.bfloat16)

    def clean(vector):
        return jnp.where(real, vector, 0.0)

    def onto_rows(low):
        return lax.dot_general(
            low, kmat, (((1,), (1,)), ((), ())), preferred_element_type=jnp.float32
        )

    def images(second):
        high = to_low(second)
        rest = second - high.astype(jnp.float32)
        mid = to_low(rest)
        low = to_low(rest - mid.astype(jnp.float32))
        three = onto_rows(jnp.concatenate([high, mid, low], axis=0))
        both = jnp.concatenate([three[:PAD], three[PAD : 2 * PAD] + three[2 * PAD :]], axis=0)
        both = lax.psum(both, "blk")
        image = to_low(both[:PAD])
        exact = both[:PAD] + both[PAD:]
        curve = jnp.sum(image.astype(jnp.float32) * exact, axis=1) / count_all
        return image, curve

    def ratio(above, below):
        return jnp.where(real, (above / below)[:, None], 0.0)

    def normal(vector):
        return jnp.sum(vector * vector, axis=1)

    start = jnp.dot(targets, kmat, preferred_element_type=jnp.float32) / count_all
    start = joint_sum("plane", nb, nr, tri_inverse, start)[1]
    start = joint_sum("turn", nb, nr, aux_inverse, start, jnp.zeros_like(start))[1]
    zeros = jnp.zeros_like(start)
    rhs, start = joint_sum("pair", nb, nr, aux_inverse, start, zeros, zeros + 1.0)
    first, start = joint_sum("slice", nb, nr, tri_inverse, start)
    joined = plane_sum(with_row(start, normal(rhs)))
    norm_first = joined[PAD - 1, :PAD]
    second = clean(joined)
    image, curve = images(second)
    curve = curve + ridge_weight * normal(first)
    gram = jnp.dot(image, kmat, preferred_element_type=jnp.float32) / count_all
    joined, turned = joint_sum("plane", nb, nr, tri_inverse, with_row(gram, curve))
    step_first = ratio(norm_first, joined[PAD - 1, :PAD])
    turned = joint_sum("turn", nb, nr, aux_inverse, turned, ridge_weight * first)[1]
    residual, start = joint_sum("pair", nb, nr, aux_inverse, turned, rhs, zeros - step_first)
    first_next, start = joint_sum("slice", nb, nr, tri_inverse, start)
    joined = plane_sum(with_row(start, normal(residual)))
    norm_next = joined[PAD - 1, :PAD]
    turn_weight = ratio(norm_next, norm_first)
    first_next = first_next + turn_weight * first
    second_next = clean(joined) + turn_weight * second
    image, curve = images(second_next)
    curve = curve + ridge_weight * normal(first_next)
    curve = lax.psum(jnp.pad(curve[:, None], ((0, 0), (0, 127))), "rows")[:, 0]
    step_next = ratio(norm_next, curve)
    coefficients = step_first * second + step_next * second_next
    scores = lax.psum(onto_rows(to_low(coefficients)), "blk")
    scores = lax.dynamic_slice_in_dim(scores, b * own_rows, own_rows, 1)

    target = destination[:, 0]
    row_ids = jnp.arange(own_rows, dtype=jnp.int32)
    same = (target[:, None] == target[None, :]) & (row_ids[None, :] < row_ids[:, None])
    before = jnp.sum(same.astype(jnp.int32), axis=1)
    slots = nr * capacity
    spread = (
        (target * capacity + before)[:, None] == jnp.arange(slots, dtype=jnp.int32)[None, :]
    ).astype(jnp.float32)
    placed = jnp.dot(scores, spread, precision=highest, preferred_element_type=jnp.float32)
    placed = placed.reshape(PAD, nr, capacity).transpose(1, 0, 2)
    lanes = -capacity % 128
    placed = jnp.pad(placed, ((0, 0), (0, 0), (0, lanes)))
    moved = lax.all_to_all(placed, "rows", split_axis=0, concat_axis=0, tiled=True)
    moved = moved[:, :CLASSES, :capacity]
    return moved.transpose(1, 0, 2).reshape(CLASSES, slots)


def solution(mesh):
    nb, nr = mesh.shape["blk"], mesh.shape["rows"]
    body = fused if (nb, nr) == (PLANES, LINE) else functools.partial(on_device, nb, nr)
    return jax.shard_map(
        body,
        mesh=mesh,
        in_specs=(
            P(("blk", "rows"), None),
            P(("blk", "rows")),
            P(("blk", "rows"), None),
            P("blk", None),
            P("blk", "rows"),
            P("blk", "rows"),
        ),
        out_specs=P(None, ("blk", "rows")),
        check_vma=False,
    )
```

```python
import functools

import jax
import jax.numpy as jnp
from jax import lax
from jax.experimental import pallas as pl
from jax.experimental.pallas import tpu as pltpu
from jax.sharding import PartitionSpec as P

CLASSES = 7
PAD = 8
LANES = 128
LOG2_E = 1.4426950408889634
MESH = pl.DeviceIdType.MESH
ridge_weight = 0.1
highest = lax.Precision.HIGHEST

PLANES = 2
LINE = 16
HALF = LINE // 2
NEAR = 4
FLIPPED = (((1,), (1,)), ((), ()))
STRAIGHT = (((1,), (0,)), ((), ()))

dma = pltpu.SemaphoreType.DMA


def spot(index, chunk):
    return pl.ds(pl.multiple_of(index * chunk, chunk), chunk)


def dot(left, right, dims):
    return lax.dot_general(left, right, dims, preferred_element_type=jnp.float32)


def stacked(vector):
    high = vector.astype(jnp.bfloat16).astype(jnp.float32)
    return jnp.concatenate([high, vector - high], axis=0).astype(jnp.bfloat16)


def fold(product):
    return product[:PAD] + product[PAD:]


def tree_sum(terms):
    while len(terms) > 1:
        pairs = [terms[i] + terms[i + 1] for i in range(0, len(terms) - 1, 2)]
        terms = pairs + terms[len(pairs) * 2 :]
    return terms[0]


def diagonal(width):
    sub = lax.broadcasted_iota(jnp.int32, (PAD, width), 0)
    lane = lax.broadcasted_iota(jnp.int32, (PAD, width), 1)
    return sub == lane


def to_lanes(column, width):
    spread = jnp.where(diagonal(width), column, 0.0)
    return jnp.sum(spread, axis=0, keepdims=True)


def to_column(row):
    spread = jnp.where(diagonal(row.shape[1]), row, 0.0)
    return jnp.sum(spread, axis=1, keepdims=True)


def with_scalars(vector, column):
    lines = lax.broadcasted_iota(jnp.int32, vector.shape, 0)
    return jnp.where(lines == PAD - 1, to_lanes(column, vector.shape[1]), vector)


def ratio(above, below):
    lines = lax.broadcasted_iota(jnp.int32, above.shape, 0)
    return jnp.where(lines < CLASSES, above / below, 0.0)


def row_sum(values):
    return jnp.sum(values, axis=1, keepdims=True)


def fused_kernel(count_all, scale, feat, label, dest, cent, tri_hbm, aux_hbm, out, *scratch):
    (
        stage, tri, aux, km, cn, place, feat_in, tgt, tgt_in,
        rs_out, rs_in, ag, w_own, w_in, w_cross, p_own, p_in, r_vec,
        c_out, c_keep, c_in, f_out, f_in, f_vec, e_own, e_in, e_vec, m_out, m_in,
        load_sem, far_send, far_recv, c_send, c_recv, one_send, one_recv,
    ) = scratch
    b, r = lax.axis_index("blk"), lax.axis_index("rows")
    z, c = r // NEAR, lax.rem(r, 2)
    mate = r + 1 - 2 * c
    across = 1 - b
    chunk = ag.shape[3]
    own_rows = feat.shape[0]
    cols = tri.shape[2]
    low_plane, low_line = b == 0, r < HALF
    active = jnp.logical_or(low_plane, r >= HALF)
    pending = []

    def settle():
        for action in pending:
            action()
        pending.clear()

    def remote(source, target, send_sem, recv_sem, device):
        return pltpu.make_async_remote_copy(
            src_ref=source, dst_ref=target, send_sem=send_sem, recv_sem=recv_sem,
            device_id=device, device_id_type=MESH,
        )

    def loop(count, body):
        def step(i, carry):
            body(i)
            return carry

        lax.fori_loop(0, count, step, 0)

    def group(j):
        return lax.rem(z + j, 2) + 2 * lax.rem(z // 2 + j // 2, 2)

    barrier = pltpu.get_barrier_semaphore()

    def hello(k):
        pl.semaphore_signal(
            barrier, inc=1, device_id=(b, lax.rem(r + k + 1, LINE)), device_id_type=MESH
        )

    pl.semaphore_signal(barrier, inc=1, device_id=(across, r), device_id_type=MESH)
    loop(LINE - 1, hello)
    loads = [
        pltpu.make_async_copy(source, stage.at[i], load_sem.at[i])
        for i, source in enumerate((tri_hbm, aux_hbm))
    ]
    for load in loads:
        load.start()

    class_rows = lax.broadcasted_iota(jnp.int32, (PAD, own_rows), 0)
    hits = jnp.where(label[...] == class_rows, 1.0, -1.0)
    tgt[...] = jnp.where(class_rows < CLASSES, hits, 0.0)

    to_power = scale * LOG2_E

    def squares_of_centres(q):
        values = cent[spot(q, chunk), :].astype(jnp.float32)
        values = values * values
        high = values.astype(jnp.bfloat16)
        low = (values - high.astype(jnp.float32)).astype(jnp.bfloat16)
        ones = jnp.ones((PAD, values.shape[1]), jnp.bfloat16)
        return (dot(ones, high, FLIPPED) + dot(ones, low, FLIPPED))[:1] * to_power

    def square_norm(source):
        values = source[...].astype(jnp.float32)
        return row_sum(values * values) * to_power

    def build(source, norm, norms, half, q):
        inner = dot(source[...], cent[spot(q, chunk), :], FLIPPED)
        power = inner * (2.0 * to_power) - norm - norms
        km[q, spot(half, own_rows), :] = jnp.exp2(power).astype(jnp.bfloat16)

    own_norm = square_norm(feat)

    def own_half(q):
        for i in range(NEAR):
            norms = squares_of_centres(q * NEAR + i)
            cn[q * NEAR + i] = jnp.broadcast_to(norms, (PAD, chunk))
            build(feat, own_norm, norms, b, q * NEAR + i)

    loop(LINE // NEAR, own_half)
    pl.semaphore_wait(barrier, LINE)
    shares = [
        remote(feat, feat_in, one_send.at[0], one_recv.at[0], (across, r)),
        remote(tgt, tgt_in, one_send.at[1], one_recv.at[1], (across, r)),
    ]
    for share in shares:
        share.start()

    def split(index, target):
        loads[index].wait()

        def visit(i):
            piece = spot(i, chunk)
            values = stage[index, piece, :]
            high = values.astype(jnp.bfloat16)
            target[0, piece, :] = high
            target[1, piece, :] = (values - high.astype(jnp.float32)).astype(jnp.bfloat16)

        loop(LINE, visit)

    def find_places():
        to_row = dest[...].astype(jnp.float32)
        sub = lax.broadcasted_iota(jnp.int32, (own_rows, own_rows), 0)
        lane = lax.broadcasted_iota(jnp.int32, (own_rows, own_rows), 1)
        to = row_sum(jnp.where(sub == lane, to_row, 0.0))
        same = jnp.logical_and(to == to_row, lane < sub)
        before = row_sum(jnp.where(same, 1.0, 0.0))
        position = to * LANES + before

        def visit(q):
            lanes = lax.broadcasted_iota(jnp.int32, (own_rows, own_rows), 1) + q * own_rows
            hit = jnp.where(lanes.astype(jnp.float32) == position, 1.0, 0.0)
            place[:, spot(q, own_rows)] = hit.astype(jnp.bfloat16)

        loop(place.shape[1] // own_rows, visit)

    def scatter(phase, term, sources_all, meanwhile=None):
        def copy(q):
            return remote(
                rs_out.at[phase, q], rs_in.at[phase, r],
                far_send.at[0, q], far_recv.at[0, r], (b, q),
            )

        def send():
            def visit(step):
                first = group(NEAR - 1 - step) * NEAR
                for i in range(NEAR):
                    rs_out[phase, first + i] = term(first + i)
                for i in range(NEAR):

                    @pl.when(first + i != r)
                    def _():
                        copy(first + i).start()

            loop(NEAR, visit)
            rs_in[phase, r] = rs_out[phase, r]

        def left():
            def visit(q):
                @pl.when(q != r)
                def _():
                    copy(q).wait_send()

            loop(LINE, visit)

        def gated(action):
            if sources_all:
                action()
            else:
                pl.when(active)(action)

        gated(send)
        settle()
        if meanwhile is not None:
            meanwhile()

        def arrive(q):
            wanted = q != r
            if not sources_all:
                wanted = jnp.logical_and(wanted, jnp.logical_or(low_plane, q >= HALF))

            @pl.when(wanted)
            def _():
                remote(
                    rs_out.at[phase, q], rs_in.at[phase, q],
                    far_send.at[0, q], far_recv.at[0, q], (b, r),
                ).wait_recv()

        loop(LINE, arrive)
        pending.append(lambda: gated(left))
        upper = tree_sum([rs_in[phase, q] for q in range(HALF, LINE)])
        if sources_all:
            return upper + tree_sum([rs_in[phase, q] for q in range(HALF)])
        ag[phase, r] = upper

        @pl.when(low_plane)
        def _():
            ag[phase, r] += tree_sum([rs_in[phase, q] for q in range(HALF)])

        return ag[phase, r]

    def gather(phase, mine, width, use, meanwhile=None):
        ag[phase, r] = mine

        def copy(q):
            return remote(
                ag.at[phase, r], ag.at[phase, r],
                far_send.at[1, q], far_recv.at[1 + 3 * (phase % 2), r], (b, q),
            )

        def send(step):
            first = group(NEAR - 1 - step) * NEAR
            for i in range(NEAR):

                @pl.when(first + i != r)
                def _():
                    copy(first + i).start()

        loop(NEAR, send)
        settle()
        if meanwhile is not None:
            meanwhile()

        def visit(j, carry):
            first = group(j) * NEAR
            for i in range(NEAR):
                source = first + i

                @pl.when(source != r)
                def _():
                    remote(
                        ag.at[phase, source], ag.at[phase, source],
                        far_send.at[1, source], far_recv.at[1 + 3 * (phase % 2), source],
                        (b, r),
                    ).wait_recv()

            for i in range(NEAR):
                carry = carry + use(first + i, stacked(ag[phase, first + i]))
            return carry

        total = lax.fori_loop(0, NEAR, visit, jnp.zeros((2 * PAD, width), jnp.float32))

        def left():
            def visit(q):
                @pl.when(q != r)
                def _():
                    copy(q).wait_send()

            loop(LINE, visit)

        pending.append(left)
        return fold(total)

    def scalars(phase):
        rows = [ag[phase, q] for q in range(LINE)]
        return to_column(tree_sum(rows)[PAD - 1 :])

    def swap(own, landing, index):
        copy = remote(own, landing, one_send.at[index], one_recv.at[index], (across, r))
        copy.start()
        settle()
        copy.wait_recv()
        pending.append(copy.wait_send)

    def factor_rows(factor):
        def use(q, low):
            return dot(low, factor[0, spot(q, chunk), :], STRAIGHT) + dot(
                low, factor[1, spot(q, chunk), :], STRAIGHT
            )

        return use

    def factor_chunk(factor, low):
        def term(q):
            return fold(
                dot(low, factor[0, spot(q, chunk), :], FLIPPED)
                + dot(low, factor[1, spot(q, chunk), :], FLIPPED)
            )

        return term

    def turn(it, product):
        w_own[it] = product
        base = b * HALF

        def inside(q):
            return remote(
                w_own.at[it], w_in.at[it, r - base],
                far_send.at[0, q], far_recv.at[2, r - base], (b, q),
            )

        def outside(q):
            return remote(
                w_own.at[it], w_cross.at[it, r - HALF],
                far_send.at[0, q], far_recv.at[2, r], (1, q),
            )

        def relay(t):
            return remote(
                w_in.at[it, t], w_in.at[it, t], far_send.at[0, t], far_recv.at[2, t], (b, mate)
            )

        def near(act):
            def visit(i):
                q = base + i

                @pl.when(q != r)
                def _():
                    act(inside(q))

            return lambda: loop(HALF, visit)

        def far(act):
            return lambda: loop(HALF // 2, lambda m: act(inside(HALF + 2 * m + c)))

        def over(act):
            return lambda: loop(HALF, lambda i: act(outside(HALF + i)))

        holder = jnp.logical_and(r >= base, r < base + HALF)
        first_low = jnp.logical_and(low_plane, low_line)
        first_high = jnp.logical_and(low_plane, r >= HALF)

        @pl.when(holder)
        def _():
            w_in[it, r - base] = w_own[it]

        def start(copy):
            copy.start()

        def left(copy):
            copy.wait_send()

        pl.when(first_low)(far(start))
        pl.when(holder)(near(start))
        pl.when(first_high)(over(start))
        settle()

        def arrival(t):
            remote(
                w_own.at[it], w_in.at[it, t], far_send.at[0, t], far_recv.at[2, t], (b, r)
            ).wait_recv()

        @pl.when(first_high)
        def _():
            def visit(m):
                arrival(2 * m + c)
                relay(2 * m + c).start()

            loop(HALF // 2, visit)

        p_own[it] = jnp.zeros(p_own.shape[1:], jnp.float32)

        @pl.when(active)
        def _():
            def ready(t):
                direct = jnp.logical_and(holder, base + t != r)
                relayed = jnp.logical_and(first_high, lax.rem(t, 2) != c)

                @pl.when(jnp.logical_or(direct, relayed))
                def _():
                    arrival(t)

                @pl.when(b == 1)
                def _():
                    remote(
                        w_own.at[it], w_cross.at[it, t],
                        far_send.at[0, t], far_recv.at[2, HALF + t], (b, r),
                    ).wait_recv()
                    w_in[it, t] += w_cross[it, t]

            def visit(i, carry):
                both = [
                    2 * lax.rem(2 * i + k, HALF // 2) + lax.rem(c + 2 * i // (HALF // 2), 2)
                    for k in range(2)
                ]
                for t in both:
                    ready(t)
                for t in both:
                    low = stacked(w_in[it, t])
                    rows = spot(t, cols)
                    carry = carry + dot(low, aux[0, rows, :], STRAIGHT)
                    carry = carry + dot(low, aux[1, rows, :], STRAIGHT)
                return carry

            total = lax.fori_loop(0, HALF // 2, visit, jnp.zeros((2 * PAD, cols), jnp.float32))
            p_own[it] = fold(total)

        def all_left():
            pl.when(first_low)(far(left))
            pl.when(holder)(near(left))
            pl.when(first_high)(over(left))
            pl.when(first_high)(lambda: loop(HALF // 2, lambda m: relay(2 * m + c).wait_send()))

        pending.append(all_left)

    def spread(it, vector):
        first_part = 1 - lax.rem(z, 2)

        def pair(part):
            return remote(
                c_out.at[it, part], c_in.at[it, part],
                c_send.at[part], c_recv.at[part], (b, mate),
            )

        low = stacked(vector)
        term = factor_chunk(aux, low)

        def targets_of(act, keep):
            def visit(t):
                here = b * HALF + t

                @pl.when(here != r)
                def _():
                    act(
                        remote(
                            f_out.at[it, t], f_in.at[it, r],
                            far_send.at[1, here], far_recv.at[3, r], (b, here),
                        )
                    )

                if keep:

                    @pl.when(here == r)
                    def _():
                        f_in[it, r] = f_out[it, t]

                @pl.when(b == 1)
                def _():
                    act(
                        remote(
                            f_out.at[it, t], f_in.at[it, r],
                            far_send.at[1, t], far_recv.at[3, r], (0, here),
                        )
                    )

            return visit

        @pl.when(active)
        def _():
            sends = targets_of(lambda copy: copy.start(), True)

            def theirs(step):
                part = lax.rem(first_part + step, 2)
                for i in range(NEAR):
                    c_out[it, part, i] = term(2 * (part * NEAR + i) + 1 - c)
                pair(part).start()

            def ours(step):
                part = lax.rem(first_part + step, 2)
                for i in range(NEAR):
                    c_keep[i] = term(2 * (part * NEAR + i) + c)
                pair(part).wait_recv()
                for i in range(NEAR):
                    f_out[it, part * NEAR + i] = c_keep[i] + c_in[it, part, i]
                for i in range(NEAR):
                    sends(part * NEAR + i)

            loop(2, theirs)
            loop(2, ours)

        settle()

        def left():
            @pl.when(active)
            def _():
                loop(2, lambda part: pair(part).wait_send())
                loop(HALF, targets_of(lambda copy: copy.wait_send(), False))

        pending.append(left)

        @pl.when(active)
        def _():
            def arrive(q):
                elsewhere = jnp.logical_or(q != r, jnp.logical_and(low_plane, r >= HALF))

                @pl.when(jnp.logical_and(elsewhere, jnp.logical_or(low_line, q >= HALF)))
                def _():
                    remote(
                        f_out.at[it, 0], f_in.at[it, q],
                        far_send.at[1, q], far_recv.at[3, q], (b, r),
                    ).wait_recv()

            loop(LINE, arrive)
            for side in range(2):
                columns = slice(side * chunk, (side + 1) * chunk)
                f_vec[it, :, columns] = tree_sum([f_in[it, q] for q in range(HALF + side, LINE, 2)])

            @pl.when(low_line)
            def _():
                for side in range(2):
                    columns = slice(side * chunk, (side + 1) * chunk)
                    f_vec[it, :, columns] += tree_sum([f_in[it, q] for q in range(side, HALF, 2)])

    def onto_centres(low):
        return lambda q: dot(low, km[q], STRAIGHT)

    def onto_rows(q, low):
        return dot(low, km[q], FLIPPED)

    f_vec[0] = jnp.zeros(f_vec.shape[1:], jnp.float32)
    f_vec[1] = jnp.zeros(f_vec.shape[1:], jnp.float32)
    split(0, tri)
    for share in shares:
        share.wait_recv()
        pending.append(share.wait_send)
    mine, other = tgt[...], tgt_in[...]
    targets = jnp.concatenate(
        [jnp.where(low_plane, mine, other), jnp.where(low_plane, other, mine)], axis=1
    ).astype(jnp.bfloat16)
    other_norm = square_norm(feat_in)

    def first_term(q):
        build(feat_in, other_norm, cn[q][:1], across, q)
        return dot(targets, km[q], STRAIGHT)

    start = scatter(0, first_term, True) / count_all
    turned = gather(0, start, cols, factor_rows(tri), lambda: split(1, aux))
    turn(0, turned)
    swap(p_own.at[0], p_in.at[0], 2)
    residual = p_own[0] + p_in[0]
    r_vec[...] = residual
    norm = row_sum(residual * residual)
    spread(0, residual)
    mine = scatter(1, factor_chunk(tri, stacked(f_vec[0])), False, find_places)
    image = gather(1, with_scalars(mine, norm), 2 * own_rows, onto_rows)
    norm_first = scalars(1)

    def curve_of(it, partial, forward):
        own = with_scalars(partial, ridge_weight * row_sum(forward * forward))
        e_own[it] = own
        swap(e_own.at[it], e_in.at[it], 3)
        theirs = e_in[it]
        ridge = jnp.where(low_plane, own, theirs)[PAD - 1 :]
        return own + theirs, to_column(ridge)

    exact, ridge = curve_of(0, image, f_vec[0])
    e_vec[...] = exact
    low = exact.astype(jnp.bfloat16)
    curve = row_sum(low.astype(jnp.float32) * exact) / count_all + ridge
    gram = scatter(2, onto_centres(low), True) / count_all
    turned = gather(2, with_scalars(gram, curve), cols, factor_rows(tri))
    step_first = ratio(norm_first, scalars(2))
    holds = jnp.logical_or(b == 1, low_line)
    turn(1, jnp.where(holds, turned + ridge_weight * f_vec[0], turned))
    swap(p_own.at[1], p_in.at[1], 2)
    residual = r_vec[...] - step_first * (p_own[1] + p_in[1])
    norm = row_sum(residual * residual)
    spread(1, residual)
    mine = scatter(3, factor_chunk(tri, stacked(f_vec[1])), False)
    image = gather(3, with_scalars(mine, norm), 2 * own_rows, onto_rows)
    norm_next = scalars(3)
    weight = ratio(norm_next, norm_first)
    exact, ridge = curve_of(1, image, f_vec[1] + weight * f_vec[0])
    exact = exact + weight * e_vec[...]
    low = exact.astype(jnp.bfloat16).astype(jnp.float32)
    curve = row_sum(low * exact) / count_all + ridge

    wide = LANES // 4
    settle()
    e_own[1] = exact
    ours = spot(b, own_rows)
    pieces = jnp.concatenate(
        [stacked(e_own[1, :, ours]), stacked(step_first * e_vec[:, ours])], axis=0
    )

    def move(q):
        return remote(
            m_out.at[q], m_in.at[r], far_send.at[0, q], far_recv.at[0, r], (b, q)
        )

    curve_row = to_lanes(curve, LANES)
    last = lax.broadcasted_iota(jnp.int32, (PAD, LANES), 0) == PAD - 1

    def put(step):
        first = group(NEAR - 1 - step) * NEAR
        both = dot(pieces, place[:, spot(first // NEAR, NEAR * LANES)], STRAIGHT)
        second, early = fold(both[: 2 * PAD]), fold(both[2 * PAD :])
        for i in range(NEAR):
            lanes = slice(i * LANES, (i + 1) * LANES)
            tile = second[:, lanes] + pltpu.roll(early[:, lanes], wide, 1)
            m_out[first + i] = jnp.where(last, curve_row, tile)
        for i in range(NEAR):

            @pl.when(first + i != r)
            def _():
                move(first + i).start()

    loop(NEAR, put)
    m_in[r] = m_out[r]
    settle()

    def arrive(q):
        @pl.when(q != r)
        def _():
            remote(
                m_out.at[q], m_in.at[q], far_send.at[0, q], far_recv.at[0, q], (b, r)
            ).wait_recv()

    loop(LINE, arrive)
    tiles = [m_in[q] for q in range(LINE)]
    step_next = ratio(norm_next, to_column(tree_sum(tiles)[PAD - 1 :]))
    band = lax.broadcasted_iota(jnp.int32, (PAD, LANES), 1) // wide
    for four in range(LINE // 4):
        total = None
        for i in range(4):
            tile = tiles[four * 4 + i]
            value = pltpu.roll(tile, LANES - wide, 1) + step_next * tile
            if i > 0:
                value = pltpu.roll(value, i * wide, 1)
            total = value if total is None else jnp.where(band == i, value, total)
        out[:, four * LANES : (four + 1) * LANES] = total[:CLASSES]

    def moved(q):
        @pl.when(q != r)
        def _():
            move(q).wait_send()

    loop(LINE, moved)


def fused(features, labels, destination, centres, tri_inverse, aux_inverse):
    own_rows, width = features.shape
    rows, cols = tri_inverse.shape
    chunk = rows // LINE
    slots = LINE * max(2, 2 * own_rows // LINE)

    def floats(*shape):
        return pltpu.VMEM(shape, jnp.float32)

    def halves(*shape):
        return pltpu.VMEM(shape, jnp.bfloat16)

    scratch = [
        floats(2, rows, cols),
        halves(2, rows, cols),
        halves(2, rows, cols),
        halves(LINE, PLANES * own_rows, chunk),
        floats(LINE, PAD, chunk),
        halves(own_rows, LINE * LANES),
        halves(own_rows, width),
        floats(PAD, own_rows),
        floats(PAD, own_rows),
        floats(4, LINE, PAD, chunk),
        floats(4, LINE, PAD, chunk),
        floats(4, LINE, PAD, chunk),
        floats(2, PAD, cols),
        floats(2, HALF, PAD, cols),
        floats(2, HALF, PAD, cols),
        floats(2, PAD, cols),
        floats(2, PAD, cols),
        floats(PAD, cols),
        floats(2, 2, NEAR, PAD, chunk),
        floats(NEAR, PAD, chunk),
        floats(2, 2, NEAR, PAD, chunk),
        floats(2, HALF, PAD, chunk),
        floats(2, LINE, PAD, chunk),
        floats(2, PAD, cols),
        floats(2, PAD, PLANES * own_rows),
        floats(2, PAD, PLANES * own_rows),
        floats(PAD, PLANES * own_rows),
        floats(LINE, PAD, LANES),
        floats(LINE, PAD, LANES),
        dma((2,)),
        dma((2, LINE)),
        dma((5, LINE)),
        dma((2,)),
        dma((2,)),
        dma((4,)),
        dma((4,)),
    ]
    whole = pl.BlockSpec(memory_space=pltpu.VMEM)
    away = pl.BlockSpec(memory_space=pltpu.MemorySpace.HBM)
    return pl.pallas_call(
        functools.partial(fused_kernel, float(own_rows * PLANES * LINE), 2.0 / width),
        out_shape=jax.ShapeDtypeStruct((CLASSES, slots), jnp.float32),
        in_specs=[whole] * 4 + [away] * 2,
        out_specs=whole,
        scratch_shapes=scratch,
        compiler_params=pltpu.CompilerParams(
            collective_id=0, has_side_effects=True, vmem_limit_bytes=56 * 1024 * 1024
        ),
    )(features, labels[None, :], destination.reshape(1, own_rows), centres, tri_inverse, aux_inverse)


def three_parts(x):
    high = x.astype(jnp.bfloat16).astype(jnp.float32)
    rest = x - high
    mid = rest.astype(jnp.bfloat16).astype(jnp.float32)
    return high, mid, rest - mid


def exact_product(dims, vector, block):
    parts = jnp.concatenate(three_parts(vector), axis=0).astype(jnp.bfloat16)
    total = None
    for part in reversed(block):
        product = dot(parts, part.astype(jnp.bfloat16), dims)
        product = product[2 * PAD :] + product[PAD : 2 * PAD] + product[:PAD]
        total = product if total is None else total + product
    return total


def forward_kernel(u_ref, block_ref, o_ref):
    o_ref[...] = exact_product(FLIPPED, u_ref[...], three_parts(block_ref[...]))


def backward_kernel(u_ref, block_ref, o_ref):
    product = exact_product(STRAIGHT, u_ref[...], three_parts(block_ref[...]))

    @pl.when(pl.program_id(0) == 0)
    def _():
        o_ref[...] = product

    @pl.when(pl.program_id(0) > 0)
    def _():
        o_ref[...] += product


STEP = 512

def factor_forward(block, vector):
    rows, cols = block.shape
    return pl.pallas_call(
        forward_kernel,
        grid=(rows // STEP,),
        in_specs=[
            pl.BlockSpec((PAD, cols), lambda i: (0, 0)),
            pl.BlockSpec((STEP, cols), lambda i: (i, 0)),
        ],
        out_specs=pl.BlockSpec((PAD, STEP), lambda i: (0, i)),
        out_shape=jax.ShapeDtypeStruct((PAD, rows), jnp.float32),
    )(vector, block)


def factor_backward(block, vector):
    rows, cols = block.shape
    return pl.pallas_call(
        backward_kernel,
        grid=(rows // STEP,),
        in_specs=[
            pl.BlockSpec((PAD, STEP), lambda i: (0, i)),
            pl.BlockSpec((STEP, cols), lambda i: (i, 0)),
        ],
        out_specs=pl.BlockSpec((PAD, cols), lambda i: (0, 0)),
        out_shape=jax.ShapeDtypeStruct((PAD, cols), jnp.float32),
    )(vector, block)


def square_norms(rows_x):
    return jnp.einsum("nd,nd->n", rows_x, rows_x, preferred_element_type=jnp.float32)


def plane_sum(x):
    return lax.psum(x, "rows")


def joint_sum(kind, nb, nr, block, *operands):
    x = operands[0]
    if kind == "plane":
        out = plane_sum(x)
        lines = jnp.arange(PAD, dtype=jnp.int32)[:, None]
        return out, factor_backward(block, jnp.where(lines < CLASSES, out, 0.0))
    if kind == "turn":
        width = x.shape[1] * nr // nb
        full = lax.all_gather(lax.psum(x, "blk") + operands[1], "rows", axis=1, tiled=True)
        out = lax.dynamic_slice_in_dim(full, lax.axis_index("blk") * width, width, 1)
        return out, factor_backward(block, out)
    if kind == "slice":
        size = x.shape[1] * nb // nr
        full = lax.all_gather(lax.psum(x, "rows"), "blk", axis=1, tiled=True)
        out = lax.dynamic_slice_in_dim(full, lax.axis_index("rows") * size, size, 1)
    else:
        out = operands[1] + operands[2] * lax.psum(x, "blk")
    return out, factor_forward(block, out)


def to_low(values):
    return lax.reduce_precision(values, 8, 7).astype(jnp.bfloat16)


def with_row(vector, scalars):
    return vector + jnp.pad(scalars[None, :], ((PAD - 1, 0), (0, vector.shape[1] - PAD)))


def on_device(nb, nr, features, labels, destination, centres, tri_inverse, aux_inverse):
    own_rows, width = features.shape
    capacity = max(2, 2 * own_rows // nr)
    scale = 2.0 / width
    count_all = float(own_rows * nb * nr)
    b = lax.axis_index("blk")
    class_rows = jnp.arange(PAD, dtype=jnp.int32)[:, None]
    real = class_rows < CLASSES

    tags = jnp.pad(labels.astype(jnp.bfloat16), (0, -own_rows % (16 * width)))
    tags = tags.reshape(-1, width)
    shared = lax.all_gather(jnp.concatenate([features, tags], axis=0), "blk", axis=0)
    rows_x = shared[:, :own_rows].reshape(nb * own_rows, width)
    tags = shared[:, own_rows:].reshape(nb, -1)[:, :own_rows].reshape(nb * own_rows)
    centre_norm = square_norms(centres)
    rows_norm = square_norms(rows_x)
    inner = lax.dot_general(
        rows_x, centres, (((1,), (1,)), ((), ())), preferred_element_type=jnp.float32
    )
    kmat = jnp.exp(-(rows_norm[:, None] + centre_norm[None, :] - 2.0 * inner) * scale).astype(
        jnp.bfloat16
    )
    hits = tags.astype(jnp.float32)[None, :] == class_rows.astype(jnp.float32)
    targets = jnp.where(real, jnp.where(hits, 1.0, -1.0), 0.0).astype(jnp.bfloat16)

    def clean(vector):
        return jnp.where(real, vector, 0.0)

    def onto_rows(low):
        return lax.dot_general(
            low, kmat, (((1,), (1,)), ((), ())), preferred_element_type=jnp.float32
        )

    def images(second):
        high = to_low(second)
        rest = second - high.astype(jnp.float32)
        mid = to_low(rest)
        low = to_low(rest - mid.astype(jnp.float32))
        three = onto_rows(jnp.concatenate([high, mid, low], axis=0))
        both = jnp.concatenate([three[:PAD], three[PAD : 2 * PAD] + three[2 * PAD :]], axis=0)
        both = lax.psum(both, "blk")
        image = to_low(both[:PAD])
        exact = both[:PAD] + both[PAD:]
        curve = jnp.sum(image.astype(jnp.float32) * exact, axis=1) / count_all
        return image, curve

    def ratio(above, below):
        return jnp.where(real, (above / below)[:, None], 0.0)

    def normal(vector):
        return jnp.sum(vector * vector, axis=1)

    start = jnp.dot(targets, kmat, preferred_element_type=jnp.float32) / count_all
    start = joint_sum("plane", nb, nr, tri_inverse, start)[1]
    start = joint_sum("turn", nb, nr, aux_inverse, start, jnp.zeros_like(start))[1]
    zeros = jnp.zeros_like(start)
    rhs, start = joint_sum("pair", nb, nr, aux_inverse, start, zeros, zeros + 1.0)
    first, start = joint_sum("slice", nb, nr, tri_inverse, start)
    joined = plane_sum(with_row(start, normal(rhs)))
    norm_first = joined[PAD - 1, :PAD]
    second = clean(joined)
    image, curve = images(second)
    curve = curve + ridge_weight * normal(first)
    gram = jnp.dot(image, kmat, preferred_element_type=jnp.float32) / count_all
    joined, turned = joint_sum("plane", nb, nr, tri_inverse, with_row(gram, curve))
    step_first = ratio(norm_first, joined[PAD - 1, :PAD])
    turned = joint_sum("turn", nb, nr, aux_inverse, turned, ridge_weight * first)[1]
    residual, start = joint_sum("pair", nb, nr, aux_inverse, turned, rhs, zeros - step_first)
    first_next, start = joint_sum("slice", nb, nr, tri_inverse, start)
    joined = plane_sum(with_row(start, normal(residual)))
    norm_next = joined[PAD - 1, :PAD]
    turn_weight = ratio(norm_next, norm_first)
    first_next = first_next + turn_weight * first
    second_next = clean(joined) + turn_weight * second
    image, curve = images(second_next)
    curve = curve + ridge_weight * normal(first_next)
    curve = lax.psum(jnp.pad(curve[:, None], ((0, 0), (0, 127))), "rows")[:, 0]
    step_next = ratio(norm_next, curve)
    coefficients = step_first * second + step_next * second_next
    scores = lax.psum(onto_rows(to_low(coefficients)), "blk")
    scores = lax.dynamic_slice_in_dim(scores, b * own_rows, own_rows, 1)

    target = destination[:, 0]
    row_ids = jnp.arange(own_rows, dtype=jnp.int32)
    same = (target[:, None] == target[None, :]) & (row_ids[None, :] < row_ids[:, None])
    before = jnp.sum(same.astype(jnp.int32), axis=1)
    slots = nr * capacity
    spread = (
        (target * capacity + before)[:, None] == jnp.arange(slots, dtype=jnp.int32)[None, :]
    ).astype(jnp.float32)
    placed = jnp.dot(scores, spread, precision=highest, preferred_element_type=jnp.float32)
    placed = placed.reshape(PAD, nr, capacity).transpose(1, 0, 2)
    lanes = -capacity % 128
    placed = jnp.pad(placed, ((0, 0), (0, 0), (0, lanes)))
    moved = lax.all_to_all(placed, "rows", split_axis=0, concat_axis=0, tiled=True)
    moved = moved[:, :CLASSES, :capacity]
    return moved.transpose(1, 0, 2).reshape(CLASSES, slots)


def solution(mesh):
    nb, nr = mesh.shape["blk"], mesh.shape["rows"]
    body = fused if (nb, nr) == (PLANES, LINE) else functools.partial(on_device, nb, nr)
    return jax.shard_map(
        body,
        mesh=mesh,
        in_specs=(
            P(("blk", "rows"), None),
            P(("blk", "rows")),
            P(("blk", "rows"), None),
            P("blk", None),
            P("blk", "rows"),
            P("blk", "rows"),
        ),
        out_specs=P(None, ("blk", "rows")),
        check_vma=False,
    )
```

```python
import functools

import jax
import jax.numpy as jnp
from jax import lax
from jax.experimental import pallas as pl
from jax.experimental.pallas import tpu as pltpu
from jax.sharding import PartitionSpec as P

CLASSES = 7
PAD = 8
LANES = 128
LOG2_E = 1.4426950408889634
MESH = pl.DeviceIdType.MESH
ridge_weight = 0.1
highest = lax.Precision.HIGHEST

PLANES = 2
LINE = 16
HALF = LINE // 2
NEAR = 4
FLIPPED = (((1,), (1,)), ((), ()))
STRAIGHT = (((1,), (0,)), ((), ()))

dma = pltpu.SemaphoreType.DMA


def spot(index, chunk):
    return pl.ds(pl.multiple_of(index * chunk, chunk), chunk)


def dot(left, right, dims):
    return lax.dot_general(left, right, dims, preferred_element_type=jnp.float32)


def stacked(vector):
    high = vector.astype(jnp.bfloat16).astype(jnp.float32)
    return jnp.concatenate([high, vector - high], axis=0).astype(jnp.bfloat16)


def fold(product):
    return product[:PAD] + product[PAD:]


def tree_sum(terms):
    while len(terms) > 1:
        pairs = [terms[i] + terms[i + 1] for i in range(0, len(terms) - 1, 2)]
        terms = pairs + terms[len(pairs) * 2 :]
    return terms[0]


def diagonal(width, first):
    sub = lax.broadcasted_iota(jnp.int32, (PAD, width), 0)
    lane = lax.broadcasted_iota(jnp.int32, (PAD, width), 1)
    return sub + first == lane


def to_lanes(column, width, first=0):
    spread = jnp.where(diagonal(width, first), column, 0.0)
    return jnp.sum(spread, axis=0, keepdims=True)


def to_column(row, first=0):
    spread = jnp.where(diagonal(row.shape[1], first), row, 0.0)
    return jnp.sum(spread, axis=1, keepdims=True)


def three_parts(x):
    high = x.astype(jnp.bfloat16).astype(jnp.float32)
    rest = x - high
    mid = rest.astype(jnp.bfloat16).astype(jnp.float32)
    return high, mid, rest - mid


def with_split_scalars(vector, column):
    parts = [to_lanes(part, vector.shape[1], k * PAD) for k, part in enumerate(three_parts(column))]
    lines = lax.broadcasted_iota(jnp.int32, vector.shape, 0)
    return jnp.where(lines == PAD - 1, tree_sum(parts), vector)


def packed(vector):
    half = vector.shape[1] // 2
    return jnp.concatenate([vector[:, :half], vector[:, half:]], axis=0).astype(jnp.bfloat16)


def unpacked(tile):
    wide = tile.astype(jnp.float32)
    return jnp.concatenate([wide[:PAD], wide[PAD:]], axis=1).astype(jnp.bfloat16)


def with_scalars(vector, column):
    lines = lax.broadcasted_iota(jnp.int32, vector.shape, 0)
    return jnp.where(lines == PAD - 1, to_lanes(column, vector.shape[1]), vector)


def ratio(above, below):
    lines = lax.broadcasted_iota(jnp.int32, above.shape, 0)
    return jnp.where(lines < CLASSES, above / below, 0.0)


def row_sum(values):
    return jnp.sum(values, axis=1, keepdims=True)


def fused_kernel(count_all, scale, feat, label, dest, cent, tri_hbm, aux_hbm, out, *scratch):
    (
        stage, tri, aux, km, cn, place, feat_in, tgt, tgt_in,
        rs_out, rs_in, ag, ag_low, w_own, w_in, w_cross, p_own, p_in, r_vec, g_own,
        f_out, f_in, f_vec, e_own, e_in, e_vec, m_out, m_in,
        load_sem, far_send, line_recv, group_recv, turn_recv, one_send, one_recv,
    ) = scratch
    b, r = lax.axis_index("blk"), lax.axis_index("rows")
    z, c = r // NEAR, lax.rem(r, 2)
    mate = r + 1 - 2 * c
    across = 1 - b
    chunk = ag.shape[3]
    own_rows = feat.shape[0]
    cols = tri.shape[2]
    low_plane, low_line = b == 0, r < HALF
    active = jnp.logical_or(low_plane, r >= HALF)
    pending = []

    def settle():
        for action in pending:
            action()
        pending.clear()

    def remote(source, target, send_sem, recv_sem, device):
        return pltpu.make_async_remote_copy(
            src_ref=source, dst_ref=target, send_sem=send_sem, recv_sem=recv_sem,
            device_id=device, device_id_type=MESH,
        )

    def await_arrivals(like, sem):
        remote(like, like, sem, sem, (b, r)).wait_recv()

    def await_sent(like, sem):
        remote(like, like, sem, sem, (b, r)).wait_send()

    def loop(count, body):
        def step(i, carry):
            body(i)
            return carry

        lax.fori_loop(0, count, step, 0)

    def turned_by(i, count):
        return lax.rem(r + i, count)

    def group(j):
        return lax.rem(z + j, 2) + 2 * lax.rem(z // 2 + j // 2, 2)

    barrier = pltpu.get_barrier_semaphore()

    def hello(k):
        pl.semaphore_signal(
            barrier, inc=1, device_id=(b, lax.rem(r + k + 1, LINE)), device_id_type=MESH
        )

    pl.semaphore_signal(barrier, inc=1, device_id=(across, r), device_id_type=MESH)
    loop(LINE - 1, hello)
    loads = [
        pltpu.make_async_copy(source, stage.at[i], load_sem.at[i])
        for i, source in enumerate((tri_hbm, aux_hbm))
    ]
    for load in loads:
        load.start()

    class_rows = lax.broadcasted_iota(jnp.int32, (PAD, own_rows), 0)
    hits = jnp.where(label[...] == class_rows, 1.0, -1.0)
    tgt[...] = jnp.where(class_rows < CLASSES, hits, 0.0)

    to_power = scale * LOG2_E

    def squares_of_centres(q):
        values = cent[spot(q, chunk), :].astype(jnp.float32)
        values = values * values
        high = values.astype(jnp.bfloat16)
        low = (values - high.astype(jnp.float32)).astype(jnp.bfloat16)
        ones = jnp.ones((PAD, values.shape[1]), jnp.bfloat16)
        return (dot(ones, high, FLIPPED) + dot(ones, low, FLIPPED))[:1] * to_power

    def square_norm(source):
        values = source[...].astype(jnp.float32)
        return row_sum(values * values) * to_power

    def build(source, norm, norms, half, q):
        inner = dot(source[...], cent[spot(q, chunk), :], FLIPPED)
        power = inner * (2.0 * to_power) - norm - norms
        km[q, spot(half, own_rows), :] = jnp.exp2(power).astype(jnp.bfloat16)

    own_norm = square_norm(feat)

    def own_half(q):
        for i in range(NEAR):
            norms = squares_of_centres(q * NEAR + i)
            cn[q * NEAR + i] = jnp.broadcast_to(norms, (PAD, chunk))
            build(feat, own_norm, norms, b, q * NEAR + i)

    loop(LINE // NEAR, own_half)
    pl.semaphore_wait(barrier, LINE)
    shares = [
        remote(feat, feat_in, one_send.at[0], one_recv.at[0], (across, r)),
        remote(tgt, tgt_in, one_send.at[1], one_recv.at[1], (across, r)),
    ]
    for share in shares:
        share.start()

    def split(index, target):
        loads[index].wait()

        def visit(i):
            piece = spot(i, chunk)
            values = stage[index, piece, :]
            high = values.astype(jnp.bfloat16)
            target[0, piece, :] = high
            target[1, piece, :] = (values - high.astype(jnp.float32)).astype(jnp.bfloat16)

        loop(LINE, visit)

    def find_places():
        to_row = dest[...].astype(jnp.float32)
        sub = lax.broadcasted_iota(jnp.int32, (own_rows, own_rows), 0)
        lane = lax.broadcasted_iota(jnp.int32, (own_rows, own_rows), 1)
        to = row_sum(jnp.where(sub == lane, to_row, 0.0))
        same = jnp.logical_and(to == to_row, lane < sub)
        before = row_sum(jnp.where(same, 1.0, 0.0))
        position = to * LANES + before

        def visit(q):
            lanes = lax.broadcasted_iota(jnp.int32, (own_rows, own_rows), 1) + q * own_rows
            hit = jnp.where(lanes.astype(jnp.float32) == position, 1.0, 0.0)
            place[:, spot(q, own_rows)] = hit.astype(jnp.bfloat16)

        loop(place.shape[1] // own_rows, visit)

    def scatter(phase, term, sources_all, meanwhile=None):
        def copy(q):
            return remote(
                rs_out.at[phase, q], rs_in.at[phase, r],
                far_send.at[0], line_recv.at[0], (b, q),
            )

        def send():
            def visit(step):
                first = group(NEAR - 1 - step) * NEAR
                for i in range(NEAR):
                    rs_out[phase, first + i] = term(first + i)
                for i in range(NEAR):
                    q = first + turned_by(i, NEAR)

                    @pl.when(q != r)
                    def _():
                        copy(q).start()

            loop(NEAR, visit)
            rs_in[phase, r] = rs_out[phase, r]

        def left():
            await_sent(rs_out.at[phase, pl.ds(0, LINE - 1)], far_send.at[0])

        def gated(action):
            if sources_all:
                action()
            else:
                pl.when(active)(action)

        gated(send)
        settle()
        if meanwhile is not None:
            meanwhile()

        def arrive(count):
            return lambda: await_arrivals(rs_in.at[phase, pl.ds(0, count)], line_recv.at[0])

        if sources_all:
            arrive(LINE - 1)()
        else:
            pl.when(low_plane)(arrive(LINE - 1))
            pl.when(jnp.logical_and(b == 1, r >= HALF))(arrive(HALF - 1))
            pl.when(jnp.logical_and(b == 1, low_line))(arrive(HALF))
        pending.append(lambda: gated(left))
        upper = tree_sum([rs_in[phase, q] for q in range(HALF, LINE)])
        if sources_all:
            return upper + tree_sum([rs_in[phase, q] for q in range(HALF)])
        ag[phase, r] = upper

        @pl.when(low_plane)
        def _():
            ag[phase, r] += tree_sum([rs_in[phase, q] for q in range(HALF)])

        return ag[phase, r]

    def gather(phase, mine, width, use, rounded=False):
        if rounded:
            held = ag_low.at[phase // 2]
            held[r] = packed(mine)
        else:
            held = ag.at[phase]
            held[r] = mine

        def copy(q):
            return remote(
                held.at[r], held.at[r],
                far_send.at[1], group_recv.at[phase % 2, z], (b, q),
            )

        def send(step):
            first = group(NEAR - 1 - step) * NEAR
            for i in range(NEAR):
                q = first + turned_by(i, NEAR)

                @pl.when(q != r)
                def _():
                    copy(q).start()

        loop(NEAR, send)
        settle()
        if phase == 0:
            split(1, aux)

        def visit(j, carry):
            first = group(j) * NEAR
            def arrive(count):
                return lambda: await_arrivals(
                    held.at[pl.ds(first, count)], group_recv.at[phase % 2, group(j)]
                )

            pl.when(j == 0)(arrive(NEAR - 1))
            pl.when(j > 0)(arrive(NEAR))
            for i in range(NEAR):
                low = unpacked(held[first + i]) if rounded else stacked(held[first + i])
                carry = carry + use(first + i, low)
            return carry

        lines = PAD if rounded else 2 * PAD
        total = lax.fori_loop(0, NEAR, visit, jnp.zeros((lines, width), jnp.float32))

        def left():
            await_sent(held.at[pl.ds(0, LINE - 1)], far_send.at[1])

        pending.append(left)
        return total if rounded else fold(total)

    def scalars(phase):
        rows = [ag[phase, q] for q in range(LINE)]
        return tree_sum(rows)[PAD - 1 :]

    def scalars_rounded(phase):
        rows = [ag_low[phase // 2, q].astype(jnp.float32) for q in range(LINE)]
        row = tree_sum(rows)[PAD - 1 : PAD]
        return tree_sum([to_column(row, k * PAD) for k in range(3)])

    def swap(own, landing, index):
        copy = remote(own, landing, one_send.at[index], one_recv.at[index], (across, r))
        copy.start()
        settle()
        copy.wait_recv()
        pending.append(copy.wait_send)

    def factor_rows(factor):
        def use(q, low):
            return dot(low, factor[0, spot(q, chunk), :], STRAIGHT) + dot(
                low, factor[1, spot(q, chunk), :], STRAIGHT
            )

        return use

    def factor_chunk(factor, low):
        def term(q):
            return fold(
                dot(low, factor[0, spot(q, chunk), :], FLIPPED)
                + dot(low, factor[1, spot(q, chunk), :], FLIPPED)
            )

        return term

    def turn(it, product):
        w_own[it] = product
        base = b * HALF

        def inside(q):
            return remote(
                w_own.at[it], w_in.at[it, r - base],
                far_send.at[0], turn_recv.at[r - base], (b, q),
            )

        def outside(q):
            return remote(
                w_own.at[it], w_cross.at[it, r - HALF],
                far_send.at[0], turn_recv.at[r], (1, q),
            )

        def relay(t):
            return remote(
                w_in.at[it, t], w_in.at[it, t], far_send.at[0], turn_recv.at[t], (b, mate)
            )

        def near(act):
            def visit(i):
                q = base + turned_by(i, HALF)

                @pl.when(q != r)
                def _():
                    act(inside(q))

            return lambda: loop(HALF, visit)

        def far(act):
            return lambda: loop(HALF // 2, lambda m: act(inside(HALF + lax.rem(2 * m + r, HALF))))

        def over(act):
            return lambda: loop(HALF, lambda i: act(outside(HALF + turned_by(i, HALF))))

        holder = jnp.logical_and(r >= base, r < base + HALF)
        first_low = jnp.logical_and(low_plane, low_line)
        first_high = jnp.logical_and(low_plane, r >= HALF)

        @pl.when(holder)
        def _():
            w_in[it, r - base] = w_own[it]

        def start(copy):
            copy.start()

        pl.when(first_low)(far(start))
        pl.when(holder)(near(start))
        pl.when(first_high)(over(start))
        settle()

        def arrival(t):
            remote(
                w_own.at[it], w_in.at[it, t], far_send.at[0], turn_recv.at[t], (b, r)
            ).wait_recv()

        @pl.when(first_high)
        def _():
            def visit(m):
                arrival(2 * m + c)
                relay(2 * m + c).start()

            loop(HALF // 2, visit)

        p_own[it] = jnp.zeros(p_own.shape[1:], jnp.float32)

        @pl.when(active)
        def _():
            def ready(t):
                direct = jnp.logical_and(holder, base + t != r)
                relayed = jnp.logical_and(first_high, lax.rem(t, 2) != c)

                @pl.when(jnp.logical_or(direct, relayed))
                def _():
                    arrival(t)

                @pl.when(b == 1)
                def _():
                    remote(
                        w_own.at[it], w_cross.at[it, t],
                        far_send.at[0], turn_recv.at[HALF + t], (b, r),
                    ).wait_recv()
                    w_in[it, t] += w_cross[it, t]

            def visit(i, carry):
                both = [
                    2 * lax.rem(2 * i + k, HALF // 2) + lax.rem(c + 2 * i // (HALF // 2), 2)
                    for k in range(2)
                ]
                for t in both:
                    ready(t)
                for t in both:
                    low = stacked(w_in[it, t])
                    rows = spot(t, cols)
                    carry = carry + dot(low, aux[0, rows, :], STRAIGHT)
                    carry = carry + dot(low, aux[1, rows, :], STRAIGHT)
                return carry

            total = lax.fori_loop(0, HALF // 2, visit, jnp.zeros((2 * PAD, cols), jnp.float32))
            p_own[it] = fold(total)

        def left(count):
            return lambda: await_sent(f_in.at[it, pl.ds(0, count)], far_send.at[0])

        def all_left():
            pl.when(first_low)(left(HALF - 1 + HALF // 2))
            pl.when(first_high)(left(HALF + HALF // 2))
            pl.when(jnp.logical_and(b == 1, r >= HALF))(left(HALF - 1))

        pending.append(all_left)

    def spread(it, vector):
        first_part = (z == 2 * b).astype(jnp.int32)
        low = stacked(vector)
        term = factor_chunk(aux, low)

        def deliver(t):
            here = b * HALF + t

            def copy(plane):
                return remote(
                    f_out.at[it, t], f_in.at[it, r], far_send.at[1], line_recv.at[1], (plane, here)
                )

            @pl.when(here != r)
            def _():
                copy(b).start()

            @pl.when(here == r)
            def _():
                f_in[it, r] = f_out[it, t]

            @pl.when(b == 1)
            def _():
                copy(0).start()

        @pl.when(active)
        def _():
            def visit(step):
                part = lax.rem(first_part + step // 2, 2)
                first = part * NEAR + 2 * lax.rem(step + r // 2, 2)
                for i in range(2):
                    for side in range(2):
                        columns = slice(side * chunk, (side + 1) * chunk)
                        f_out[it, first + i, :, columns] = term(2 * (first + i) + side)
                for i in range(2):
                    deliver(first + turned_by(i, 2))

            loop(NEAR, visit)

        settle()

        def left(count):
            return lambda: await_sent(f_in.at[it, pl.ds(0, count)], far_send.at[1])

        def arrive(count):
            return lambda: await_arrivals(f_in.at[it, pl.ds(0, count)], line_recv.at[1])

        first_low = jnp.logical_and(low_plane, low_line)
        first_high = jnp.logical_and(low_plane, r >= HALF)
        second = jnp.logical_and(b == 1, r >= HALF)

        def all_left():
            pl.when(first_low)(left(HALF - 1))
            pl.when(first_high)(left(HALF))
            pl.when(second)(left(2 * HALF - 1))

        pending.append(all_left)
        pl.when(first_low)(arrive(LINE - 1))
        pl.when(first_high)(arrive(HALF))
        pl.when(second)(arrive(HALF - 1))

        @pl.when(active)
        def _():
            f_vec[it] = tree_sum([f_in[it, q] for q in range(HALF, LINE)])

        @pl.when(first_low)
        def _():
            f_vec[it] += tree_sum([f_in[it, q] for q in range(HALF)])

    def onto_centres(low):
        return lambda q: dot(low, km[q], STRAIGHT)

    def onto_rows(q, low):
        return dot(low, km[q], FLIPPED)

    f_vec[0] = jnp.zeros(f_vec.shape[1:], jnp.float32)
    f_vec[1] = jnp.zeros(f_vec.shape[1:], jnp.float32)
    split(0, tri)
    for share in shares:
        share.wait_recv()
        pending.append(share.wait_send)
    mine, other = tgt[...], tgt_in[...]
    targets = jnp.concatenate(
        [jnp.where(low_plane, mine, other), jnp.where(low_plane, other, mine)], axis=1
    ).astype(jnp.bfloat16)
    other_norm = square_norm(feat_in)

    def first_term(q):
        build(feat_in, other_norm, cn[q][:1], across, q)
        return dot(targets, km[q], STRAIGHT)

    start = scatter(0, first_term, True) / count_all
    turned = gather(0, start, cols, factor_rows(tri))
    turn(0, turned)
    swap(p_own.at[0], p_in.at[0], 2)
    residual = p_own[0] + p_in[0]
    r_vec[...] = residual
    norm = row_sum(residual * residual)
    spread(0, residual)
    mine = scatter(1, factor_chunk(tri, stacked(f_vec[0])), False, find_places)
    g_own[...] = mine
    image = gather(1, with_split_scalars(mine, norm), 2 * own_rows, onto_rows, True)
    e_own[0] = image
    swap(e_own.at[0], e_in.at[0], 3)
    e_vec[...] = e_own[0] + e_in[0]
    gram = scatter(2, onto_centres(e_vec[...].astype(jnp.bfloat16)), True) / count_all
    ridge = jnp.where(low_plane, ridge_weight, 0.0) * row_sum(f_vec[0] * f_vec[0])
    curve = row_sum(gram * g_own[...]) + ridge
    turned = gather(2, with_scalars(gram, curve), cols, factor_rows(tri))
    holds = jnp.logical_or(b == 1, low_line)
    turn(1, jnp.where(holds, turned + ridge_weight * f_vec[0], turned))
    p_own[1, PAD - 1 :, :chunk] = scalars(2)
    swap(p_own.at[1], p_in.at[1], 2)
    norm_first = scalars_rounded(1)
    both = p_own[1] + p_in[1]
    step_first = ratio(norm_first, to_column(both[PAD - 1 :]))
    residual = r_vec[...] - step_first * both
    norm = row_sum(residual * residual)
    spread(1, residual)
    mine = scatter(3, factor_chunk(tri, stacked(f_vec[1])), False)
    image = gather(3, with_split_scalars(mine, norm), 2 * own_rows, onto_rows, True)
    norm_next = scalars_rounded(3)
    weight = ratio(norm_next, norm_first)
    forward = f_vec[1] + weight * f_vec[0]
    e_own[1] = with_scalars(image, ridge_weight * row_sum(forward * forward))
    swap(e_own.at[1], e_in.at[1], 3)
    ridge = jnp.where(low_plane, e_own[1, PAD - 1 :, :chunk], e_in[1, PAD - 1 :, :chunk])
    exact = e_own[1] + e_in[1] + weight * e_vec[...]
    low = exact.astype(jnp.bfloat16).astype(jnp.float32)
    curve = row_sum(low * exact) / count_all + to_column(ridge)

    wide = LANES // 4
    settle()
    e_own[1] = exact
    ours = spot(b, own_rows)
    pieces = jnp.concatenate(
        [stacked(e_own[1, :, ours]), stacked(step_first * e_vec[:, ours])], axis=0
    )

    def move(q):
        return remote(
            m_out.at[q], m_in.at[r], far_send.at[0], line_recv.at[0], (b, q)
        )

    curve_row = to_lanes(curve, LANES)
    last = lax.broadcasted_iota(jnp.int32, (PAD, LANES), 0) == PAD - 1

    def put(step):
        first = group(NEAR - 1 - step) * NEAR
        both = dot(pieces, place[:, spot(first // NEAR, NEAR * LANES)], STRAIGHT)
        second, early = fold(both[: 2 * PAD]), fold(both[2 * PAD :])
        for i in range(NEAR):
            lanes = slice(i * LANES, (i + 1) * LANES)
            tile = second[:, lanes] + pltpu.roll(early[:, lanes], wide, 1)
            m_out[first + i] = jnp.where(last, curve_row, tile)
        for i in range(NEAR):
            q = first + turned_by(i, NEAR)

            @pl.when(q != r)
            def _():
                move(q).start()

    loop(NEAR, put)
    m_in[r] = m_out[r]
    settle()

    await_arrivals(m_in.at[pl.ds(0, LINE - 1)], line_recv.at[0])
    tiles = [m_in[q] for q in range(LINE)]
    step_next = ratio(norm_next, to_column(tree_sum(tiles)[PAD - 1 :]))
    band = lax.broadcasted_iota(jnp.int32, (PAD, LANES), 1) // wide
    for four in range(LINE // 4):
        total = None
        for i in range(4):
            tile = tiles[four * 4 + i]
            value = pltpu.roll(tile, LANES - wide, 1) + step_next * tile
            if i > 0:
                value = pltpu.roll(value, i * wide, 1)
            total = value if total is None else jnp.where(band == i, value, total)
        out[:, four * LANES : (four + 1) * LANES] = total[:CLASSES]

    await_sent(m_out.at[pl.ds(0, LINE - 1)], far_send.at[0])


def fused(features, labels, destination, centres, tri_inverse, aux_inverse):
    own_rows, width = features.shape
    rows, cols = tri_inverse.shape
    chunk = rows // LINE
    slots = LINE * max(2, 2 * own_rows // LINE)

    def floats(*shape):
        return pltpu.VMEM(shape, jnp.float32)

    def halves(*shape):
        return pltpu.VMEM(shape, jnp.bfloat16)

    scratch = [
        floats(2, rows, cols),
        halves(2, rows, cols),
        halves(2, rows, cols),
        halves(LINE, PLANES * own_rows, chunk),
        floats(LINE, PAD, chunk),
        halves(own_rows, LINE * LANES),
        halves(own_rows, width),
        floats(PAD, own_rows),
        floats(PAD, own_rows),
        floats(4, LINE, PAD, chunk),
        floats(4, LINE, PAD, chunk),
        floats(4, LINE, PAD, chunk),
        halves(2, LINE, 2 * PAD, chunk // 2),
        floats(2, PAD, cols),
        floats(2, HALF, PAD, cols),
        floats(2, HALF, PAD, cols),
        floats(2, PAD, cols),
        floats(2, PAD, cols),
        floats(PAD, cols),
        floats(PAD, chunk),
        floats(2, HALF, PAD, cols),
        floats(2, LINE, PAD, cols),
        floats(2, PAD, cols),
        floats(2, PAD, PLANES * own_rows),
        floats(2, PAD, PLANES * own_rows),
        floats(PAD, PLANES * own_rows),
        floats(LINE, PAD, LANES),
        floats(LINE, PAD, LANES),
        dma((2,)),
        dma((2,)),
        dma((2,)),
        dma((2, LINE // NEAR)),
        dma((LINE,)),
        dma((4,)),
        dma((4,)),
    ]
    whole = pl.BlockSpec(memory_space=pltpu.VMEM)
    away = pl.BlockSpec(memory_space=pltpu.MemorySpace.HBM)
    return pl.pallas_call(
        functools.partial(fused_kernel, float(own_rows * PLANES * LINE), 2.0 / width),
        out_shape=jax.ShapeDtypeStruct((CLASSES, slots), jnp.float32),
        in_specs=[whole] * 4 + [away] * 2,
        out_specs=whole,
        scratch_shapes=scratch,
        compiler_params=pltpu.CompilerParams(
            collective_id=0, has_side_effects=True, vmem_limit_bytes=56 * 1024 * 1024
        ),
    )(features, labels[None, :], destination.reshape(1, own_rows), centres, tri_inverse, aux_inverse)


def exact_product(dims, vector, block):
    parts = jnp.concatenate(three_parts(vector), axis=0).astype(jnp.bfloat16)
    total = None
    for part in reversed(block):
        product = dot(parts, part.astype(jnp.bfloat16), dims)
        product = product[2 * PAD :] + product[PAD : 2 * PAD] + product[:PAD]
        total = product if total is None else total + product
    return total


def forward_kernel(u_ref, block_ref, o_ref):
    o_ref[...] = exact_product(FLIPPED, u_ref[...], three_parts(block_ref[...]))


def backward_kernel(u_ref, block_ref, o_ref):
    product = exact_product(STRAIGHT, u_ref[...], three_parts(block_ref[...]))

    @pl.when(pl.program_id(0) == 0)
    def _():
        o_ref[...] = product

    @pl.when(pl.program_id(0) > 0)
    def _():
        o_ref[...] += product


STEP = 512

def factor_forward(block, vector):
    rows, cols = block.shape
    return pl.pallas_call(
        forward_kernel,
        grid=(rows // STEP,),
        in_specs=[
            pl.BlockSpec((PAD, cols), lambda i: (0, 0)),
            pl.BlockSpec((STEP, cols), lambda i: (i, 0)),
        ],
        out_specs=pl.BlockSpec((PAD, STEP), lambda i: (0, i)),
        out_shape=jax.ShapeDtypeStruct((PAD, rows), jnp.float32),
    )(vector, block)


def factor_backward(block, vector):
    rows, cols = block.shape
    return pl.pallas_call(
        backward_kernel,
        grid=(rows // STEP,),
        in_specs=[
            pl.BlockSpec((PAD, STEP), lambda i: (0, i)),
            pl.BlockSpec((STEP, cols), lambda i: (i, 0)),
        ],
        out_specs=pl.BlockSpec((PAD, cols), lambda i: (0, 0)),
        out_shape=jax.ShapeDtypeStruct((PAD, cols), jnp.float32),
    )(vector, block)


def square_norms(rows_x):
    return jnp.einsum("nd,nd->n", rows_x, rows_x, preferred_element_type=jnp.float32)


def plane_sum(x):
    return lax.psum(x, "rows")


def joint_sum(kind, nb, nr, block, *operands):
    x = operands[0]
    if kind == "plane":
        out = plane_sum(x)
        lines = jnp.arange(PAD, dtype=jnp.int32)[:, None]
        return out, factor_backward(block, jnp.where(lines < CLASSES, out, 0.0))
    if kind == "turn":
        width = x.shape[1] * nr // nb
        full = lax.all_gather(lax.psum(x, "blk") + operands[1], "rows", axis=1, tiled=True)
        out = lax.dynamic_slice_in_dim(full, lax.axis_index("blk") * width, width, 1)
        return out, factor_backward(block, out)
    if kind == "slice":
        size = x.shape[1] * nb // nr
        full = lax.all_gather(lax.psum(x, "rows"), "blk", axis=1, tiled=True)
        out = lax.dynamic_slice_in_dim(full, lax.axis_index("rows") * size, size, 1)
    else:
        out = operands[1] + operands[2] * lax.psum(x, "blk")
    return out, factor_forward(block, out)


def to_low(values):
    return lax.reduce_precision(values, 8, 7).astype(jnp.bfloat16)


def with_row(vector, scalars):
    return vector + jnp.pad(scalars[None, :], ((PAD - 1, 0), (0, vector.shape[1] - PAD)))


def on_device(nb, nr, features, labels, destination, centres, tri_inverse, aux_inverse):
    own_rows, width = features.shape
    capacity = max(2, 2 * own_rows // nr)
    scale = 2.0 / width
    count_all = float(own_rows * nb * nr)
    b = lax.axis_index("blk")
    class_rows = jnp.arange(PAD, dtype=jnp.int32)[:, None]
    real = class_rows < CLASSES

    tags = jnp.pad(labels.astype(jnp.bfloat16), (0, -own_rows % (16 * width)))
    tags = tags.reshape(-1, width)
    shared = lax.all_gather(jnp.concatenate([features, tags], axis=0), "blk", axis=0)
    rows_x = shared[:, :own_rows].reshape(nb * own_rows, width)
    tags = shared[:, own_rows:].reshape(nb, -1)[:, :own_rows].reshape(nb * own_rows)
    centre_norm = square_norms(centres)
    rows_norm = square_norms(rows_x)
    inner = lax.dot_general(
        rows_x, centres, (((1,), (1,)), ((), ())), preferred_element_type=jnp.float32
    )
    kmat = jnp.exp(-(rows_norm[:, None] + centre_norm[None, :] - 2.0 * inner) * scale).astype(
        jnp.bfloat16
    )
    hits = tags.astype(jnp.float32)[None, :] == class_rows.astype(jnp.float32)
    targets = jnp.where(real, jnp.where(hits, 1.0, -1.0), 0.0).astype(jnp.bfloat16)

    def clean(vector):
        return jnp.where(real, vector, 0.0)

    def onto_rows(low):
        return lax.dot_general(
            low, kmat, (((1,), (1,)), ((), ())), preferred_element_type=jnp.float32
        )

    def images(second):
        high = to_low(second)
        rest = second - high.astype(jnp.float32)
        mid = to_low(rest)
        low = to_low(rest - mid.astype(jnp.float32))
        three = onto_rows(jnp.concatenate([high, mid, low], axis=0))
        both = jnp.concatenate([three[:PAD], three[PAD : 2 * PAD] + three[2 * PAD :]], axis=0)
        both = lax.psum(both, "blk")
        image = to_low(both[:PAD])
        exact = both[:PAD] + both[PAD:]
        curve = jnp.sum(image.astype(jnp.float32) * exact, axis=1) / count_all
        return image, curve

    def ratio(above, below):
        return jnp.where(real, (above / below)[:, None], 0.0)

    def normal(vector):
        return jnp.sum(vector * vector, axis=1)

    start = jnp.dot(targets, kmat, preferred_element_type=jnp.float32) / count_all
    start = joint_sum("plane", nb, nr, tri_inverse, start)[1]
    start = joint_sum("turn", nb, nr, aux_inverse, start, jnp.zeros_like(start))[1]
    zeros = jnp.zeros_like(start)
    rhs, start = joint_sum("pair", nb, nr, aux_inverse, start, zeros, zeros + 1.0)
    first, start = joint_sum("slice", nb, nr, tri_inverse, start)
    joined = plane_sum(with_row(start, normal(rhs)))
    norm_first = joined[PAD - 1, :PAD]
    second = clean(joined)
    image, curve = images(second)
    curve = curve + ridge_weight * normal(first)
    gram = jnp.dot(image, kmat, preferred_element_type=jnp.float32) / count_all
    joined, turned = joint_sum("plane", nb, nr, tri_inverse, with_row(gram, curve))
    step_first = ratio(norm_first, joined[PAD - 1, :PAD])
    turned = joint_sum("turn", nb, nr, aux_inverse, turned, ridge_weight * first)[1]
    residual, start = joint_sum("pair", nb, nr, aux_inverse, turned, rhs, zeros - step_first)
    first_next, start = joint_sum("slice", nb, nr, tri_inverse, start)
    joined = plane_sum(with_row(start, normal(residual)))
    norm_next = joined[PAD - 1, :PAD]
    turn_weight = ratio(norm_next, norm_first)
    first_next = first_next + turn_weight * first
    second_next = clean(joined) + turn_weight * second
    image, curve = images(second_next)
    curve = curve + ridge_weight * normal(first_next)
    curve = lax.psum(jnp.pad(curve[:, None], ((0, 0), (0, 127))), "rows")[:, 0]
    step_next = ratio(norm_next, curve)
    coefficients = step_first * second + step_next * second_next
    scores = lax.psum(onto_rows(to_low(coefficients)), "blk")
    scores = lax.dynamic_slice_in_dim(scores, b * own_rows, own_rows, 1)

    target = destination[:, 0]
    row_ids = jnp.arange(own_rows, dtype=jnp.int32)
    same = (target[:, None] == target[None, :]) & (row_ids[None, :] < row_ids[:, None])
    before = jnp.sum(same.astype(jnp.int32), axis=1)
    slots = nr * capacity
    spread = (
        (target * capacity + before)[:, None] == jnp.arange(slots, dtype=jnp.int32)[None, :]
    ).astype(jnp.float32)
    placed = jnp.dot(scores, spread, precision=highest, preferred_element_type=jnp.float32)
    placed = placed.reshape(PAD, nr, capacity).transpose(1, 0, 2)
    lanes = -capacity % 128
    placed = jnp.pad(placed, ((0, 0), (0, 0), (0, lanes)))
    moved = lax.all_to_all(placed, "rows", split_axis=0, concat_axis=0, tiled=True)
    moved = moved[:, :CLASSES, :capacity]
    return moved.transpose(1, 0, 2).reshape(CLASSES, slots)


def solution(mesh):
    nb, nr = mesh.shape["blk"], mesh.shape["rows"]
    body = fused if (nb, nr) == (PLANES, LINE) else functools.partial(on_device, nb, nr)
    return jax.shard_map(
        body,
        mesh=mesh,
        in_specs=(
            P(("blk", "rows"), None),
            P(("blk", "rows")),
            P(("blk", "rows"), None),
            P("blk", None),
            P("blk", "rows"),
            P("blk", "rows"),
        ),
        out_specs=P(None, ("blk", "rows")),
        check_vma=False,
    )
```

```python
import functools

import jax
import jax.numpy as jnp
from jax import lax
from jax.experimental import pallas as pl
from jax.experimental.pallas import tpu as pltpu
from jax.sharding import PartitionSpec as P

CLASSES = 7
PAD = 8
LANES = 128
LOG2_E = 1.4426950408889634
MESH = pl.DeviceIdType.MESH
ridge_weight = 0.1
highest = lax.Precision.HIGHEST

PLANES = 2
LINE = 16
HALF = LINE // 2
NEAR = 4
FLIPPED = (((1,), (1,)), ((), ()))
STRAIGHT = (((1,), (0,)), ((), ()))

dma = pltpu.SemaphoreType.DMA


def spot(index, chunk):
    return pl.ds(pl.multiple_of(index * chunk, chunk), chunk)


def dot(left, right, dims):
    return lax.dot_general(left, right, dims, preferred_element_type=jnp.float32)


def stacked(vector):
    high = vector.astype(jnp.bfloat16).astype(jnp.float32)
    return jnp.concatenate([high, vector - high], axis=0).astype(jnp.bfloat16)


def fold(product):
    return product[:PAD] + product[PAD:]


def tree_sum(terms):
    while len(terms) > 1:
        pairs = [terms[i] + terms[i + 1] for i in range(0, len(terms) - 1, 2)]
        terms = pairs + terms[len(pairs) * 2 :]
    return terms[0]


def diagonal(width, first):
    sub = lax.broadcasted_iota(jnp.int32, (PAD, width), 0)
    lane = lax.broadcasted_iota(jnp.int32, (PAD, width), 1)
    return sub + first == lane


def to_lanes(column, width, first=0):
    spread = jnp.where(diagonal(width, first), column, 0.0)
    return jnp.sum(spread, axis=0, keepdims=True)


def to_column(row, first=0):
    spread = jnp.where(diagonal(row.shape[1], first), row, 0.0)
    return jnp.sum(spread, axis=1, keepdims=True)


def three_parts(x):
    high = x.astype(jnp.bfloat16).astype(jnp.float32)
    rest = x - high
    mid = rest.astype(jnp.bfloat16).astype(jnp.float32)
    return high, mid, rest - mid


def with_split_scalars(vector, column):
    parts = [to_lanes(part, vector.shape[1], k * PAD) for k, part in enumerate(three_parts(column))]
    lines = lax.broadcasted_iota(jnp.int32, vector.shape, 0)
    return jnp.where(lines == PAD - 1, tree_sum(parts), vector)


def packed(vector):
    half = vector.shape[1] // 2
    return jnp.concatenate([vector[:, :half], vector[:, half:]], axis=0).astype(jnp.bfloat16)


def unpacked(tile):
    wide = tile.astype(jnp.float32)
    return jnp.concatenate([wide[:PAD], wide[PAD:]], axis=1).astype(jnp.bfloat16)


def with_scalars(vector, column):
    lines = lax.broadcasted_iota(jnp.int32, vector.shape, 0)
    return jnp.where(lines == PAD - 1, to_lanes(column, vector.shape[1]), vector)


def ratio(above, below):
    lines = lax.broadcasted_iota(jnp.int32, above.shape, 0)
    return jnp.where(lines < CLASSES, above / below, 0.0)


def row_sum(values):
    return jnp.sum(values, axis=1, keepdims=True)


def fused_kernel(count_all, scale, *refs):
    arrays, out, scratch = refs[:6], refs[6], refs[7:]
    (
        feat, label, cent, dest, stage, tri, aux, km, cn, place, feat_in, tgt, tgt_in,
        rs_out, rs_in, ag, ag_low, w_own, w_in, w_cross, p_own, p_in, r_vec, g_own,
        f_out, f_in, f_vec, c_out, c_in, far_out, far_in, e_own, e_in, e_vec, m_out, m_in,
        load_sem, far_send, line_recv, group_recv, turn_recv, mate_send, mate_recv, one_send, one_recv,
    ) = scratch
    b, r = lax.axis_index("blk"), lax.axis_index("rows")
    z, c = r // NEAR, lax.rem(r, 2)
    mate = r + 1 - 2 * c
    across = 1 - b
    chunk = ag.shape[3]
    own_rows = feat.shape[0]
    cols = tri.shape[2]
    low_plane, low_line = b == 0, r < HALF
    active = jnp.logical_or(low_plane, r >= HALF)
    pending = []

    def settle():
        for action in pending:
            action()
        pending.clear()

    def remote(source, target, send_sem, recv_sem, device):
        return pltpu.make_async_remote_copy(
            src_ref=source, dst_ref=target, send_sem=send_sem, recv_sem=recv_sem,
            device_id=device, device_id_type=MESH,
        )

    def await_arrivals(like, sem):
        remote(like, like, sem, sem, (b, r)).wait_recv()

    def await_sent(like, sem):
        remote(like, like, sem, sem, (b, r)).wait_send()

    def loop(count, body):
        def step(i, carry):
            body(i)
            return carry

        lax.fori_loop(0, count, step, 0)

    def turned_by(i, count):
        return lax.rem(r + i, count)

    def group(j):
        return lax.rem(z + j, 2) + 2 * lax.rem(z // 2 + j // 2, 2)

    barrier = pltpu.get_barrier_semaphore()

    def hello(k):
        pl.semaphore_signal(
            barrier, inc=1, device_id=(b, lax.rem(r + k + 1, LINE)), device_id_type=MESH
        )

    pl.semaphore_signal(barrier, inc=1, device_id=(across, r), device_id_type=MESH)
    loop(LINE - 1, hello)
    into = (feat, label, cent, dest, stage.at[0], stage.at[1])
    loads = [
        pltpu.make_async_copy(source, target, load_sem.at[i])
        for i, (source, target) in enumerate(zip(arrays, into))
    ]
    for load in loads:
        load.start()
    for load in loads[:4]:
        load.wait()
    loads = loads[4:]

    class_rows = lax.broadcasted_iota(jnp.int32, (PAD, own_rows), 0)
    hits = jnp.where(label[...] == class_rows, 1.0, -1.0)
    tgt[...] = jnp.where(class_rows < CLASSES, hits, 0.0)

    to_power = scale * LOG2_E

    def squares_of_centres(q):
        values = cent[spot(q, chunk), :].astype(jnp.float32)
        values = values * values
        high = values.astype(jnp.bfloat16)
        low = (values - high.astype(jnp.float32)).astype(jnp.bfloat16)
        ones = jnp.ones((PAD, values.shape[1]), jnp.bfloat16)
        return (dot(ones, high, FLIPPED) + dot(ones, low, FLIPPED))[:1] * to_power

    def square_norm(source):
        values = source[...].astype(jnp.float32)
        return row_sum(values * values) * to_power

    def build(source, norm, norms, half, q):
        inner = dot(source[...], cent[spot(q, chunk), :], FLIPPED)
        power = inner * (2.0 * to_power) - norm - norms
        km[q, spot(half, own_rows), :] = jnp.exp2(power).astype(jnp.bfloat16)

    own_norm = square_norm(feat)

    def own_half(q):
        for i in range(NEAR):
            norms = squares_of_centres(q * NEAR + i)
            cn[q * NEAR + i] = jnp.broadcast_to(norms, (PAD, chunk))
            build(feat, own_norm, norms, b, q * NEAR + i)

    loop(LINE // NEAR, own_half)
    pl.semaphore_wait(barrier, LINE)
    shares = [
        remote(feat, feat_in, one_send.at[0], one_recv.at[0], (across, r)),
        remote(tgt, tgt_in, one_send.at[1], one_recv.at[1], (across, r)),
    ]
    for share in shares:
        share.start()

    def split(index, target):
        loads[index].wait()

        def visit(i):
            piece = spot(i, chunk)
            values = stage[index, piece, :]
            high = values.astype(jnp.bfloat16)
            target[0, piece, :] = high
            target[1, piece, :] = (values - high.astype(jnp.float32)).astype(jnp.bfloat16)

        loop(LINE, visit)

    def find_places():
        to_row = dest[...].astype(jnp.float32)
        sub = lax.broadcasted_iota(jnp.int32, (own_rows, own_rows), 0)
        lane = lax.broadcasted_iota(jnp.int32, (own_rows, own_rows), 1)
        to = row_sum(jnp.where(sub == lane, to_row, 0.0))
        same = jnp.logical_and(to == to_row, lane < sub)
        before = row_sum(jnp.where(same, 1.0, 0.0))
        position = to * LANES + before

        def visit(q):
            lanes = lax.broadcasted_iota(jnp.int32, (own_rows, own_rows), 1) + q * own_rows
            hit = jnp.where(lanes.astype(jnp.float32) == position, 1.0, 0.0)
            place[:, spot(q, own_rows)] = hit.astype(jnp.bfloat16)

        loop(place.shape[1] // own_rows, visit)

    def scatter(phase, term, sources_all, meanwhile=None):
        def copy(q):
            return remote(
                rs_out.at[phase, q], rs_in.at[phase, r],
                far_send.at[0], line_recv.at[0], (b, q),
            )

        def send():
            def visit(step):
                first = group(NEAR - 1 - step) * NEAR
                for i in range(NEAR):
                    rs_out[phase, first + i] = term(first + i)
                for i in range(NEAR):
                    q = first + turned_by(i, NEAR)

                    @pl.when(q != r)
                    def _():
                        copy(q).start()

            loop(NEAR, visit)
            rs_in[phase, r] = rs_out[phase, r]

        def left():
            await_sent(rs_out.at[phase, pl.ds(0, LINE - 1)], far_send.at[0])

        def gated(action):
            if sources_all:
                action()
            else:
                pl.when(active)(action)

        gated(send)
        settle()
        if meanwhile is not None:
            meanwhile()

        def arrive(count):
            return lambda: await_arrivals(rs_in.at[phase, pl.ds(0, count)], line_recv.at[0])

        if sources_all:
            arrive(LINE - 1)()
        else:
            pl.when(low_plane)(arrive(LINE - 1))
            pl.when(jnp.logical_and(b == 1, r >= HALF))(arrive(HALF - 1))
            pl.when(jnp.logical_and(b == 1, low_line))(arrive(HALF))
        pending.append(lambda: gated(left))
        upper = tree_sum([rs_in[phase, q] for q in range(HALF, LINE)])
        if sources_all:
            return upper + tree_sum([rs_in[phase, q] for q in range(HALF)])
        ag[phase, r] = upper

        @pl.when(low_plane)
        def _():
            ag[phase, r] += tree_sum([rs_in[phase, q] for q in range(HALF)])

        return ag[phase, r]

    def gather(phase, mine, width, use, rounded=False):
        if rounded:
            held = ag_low.at[phase // 2]
            held[r] = packed(mine)
        else:
            held = ag.at[phase]
            held[r] = mine

        def copy(q):
            return remote(
                held.at[r], held.at[r],
                far_send.at[1], group_recv.at[phase % 2, z], (b, q),
            )

        def send(step):
            first = group(NEAR - 1 - step) * NEAR
            for i in range(NEAR):
                q = first + turned_by(i, NEAR)

                @pl.when(q != r)
                def _():
                    copy(q).start()

        loop(NEAR, send)
        settle()
        if phase == 0:
            split(1, aux)

        def visit(j, carry):
            first = group(j) * NEAR
            def arrive(count):
                return lambda: await_arrivals(
                    held.at[pl.ds(first, count)], group_recv.at[phase % 2, group(j)]
                )

            pl.when(j == 0)(arrive(NEAR - 1))
            pl.when(j > 0)(arrive(NEAR))
            for i in range(NEAR):
                low = unpacked(held[first + i]) if rounded else stacked(held[first + i])
                carry = carry + use(first + i, low)
            return carry

        lines = PAD if rounded else 2 * PAD
        total = lax.fori_loop(0, NEAR, visit, jnp.zeros((lines, width), jnp.float32))

        def left():
            await_sent(held.at[pl.ds(0, LINE - 1)], far_send.at[1])

        pending.append(left)
        return total if rounded else fold(total)

    def scalars(phase):
        rows = [ag[phase, q] for q in range(LINE)]
        return tree_sum(rows)[PAD - 1 :]

    def scalars_rounded(phase):
        rows = [ag_low[phase // 2, q].astype(jnp.float32) for q in range(LINE)]
        row = tree_sum(rows)[PAD - 1 : PAD]
        return tree_sum([to_column(row, k * PAD) for k in range(3)])

    def swap(own, landing, index):
        copy = remote(own, landing, one_send.at[index], one_recv.at[index], (across, r))
        copy.start()
        settle()
        copy.wait_recv()
        pending.append(copy.wait_send)

    def factor_rows(factor):
        def use(q, low):
            return dot(low, factor[0, spot(q, chunk), :], STRAIGHT) + dot(
                low, factor[1, spot(q, chunk), :], STRAIGHT
            )

        return use

    def factor_chunk(factor, low):
        def term(q):
            return fold(
                dot(low, factor[0, spot(q, chunk), :], FLIPPED)
                + dot(low, factor[1, spot(q, chunk), :], FLIPPED)
            )

        return term

    def turn(it, product):
        w_own[it] = product
        base = b * HALF

        def inside(q):
            return remote(
                w_own.at[it], w_in.at[it, r - base],
                far_send.at[0], turn_recv.at[r - base], (b, q),
            )

        def outside(q):
            return remote(
                w_own.at[it], w_cross.at[it, r - HALF],
                far_send.at[0], turn_recv.at[r], (1, q),
            )

        def relay(t):
            return remote(
                w_in.at[it, t], w_in.at[it, t], far_send.at[0], turn_recv.at[t], (b, mate)
            )

        def near(act):
            def visit(i):
                q = base + turned_by(i, HALF)

                @pl.when(q != r)
                def _():
                    act(inside(q))

            return lambda: loop(HALF, visit)

        def far(act):
            return lambda: loop(HALF // 2, lambda m: act(inside(HALF + lax.rem(2 * m + r, HALF))))

        def over(act):
            return lambda: loop(HALF, lambda i: act(outside(HALF + turned_by(i, HALF))))

        holder = jnp.logical_and(r >= base, r < base + HALF)
        first_low = jnp.logical_and(low_plane, low_line)
        first_high = jnp.logical_and(low_plane, r >= HALF)

        @pl.when(holder)
        def _():
            w_in[it, r - base] = w_own[it]

        def start(copy):
            copy.start()

        pl.when(first_low)(far(start))
        pl.when(holder)(near(start))
        pl.when(first_high)(over(start))
        settle()

        def arrival(t):
            remote(
                w_own.at[it], w_in.at[it, t], far_send.at[0], turn_recv.at[t], (b, r)
            ).wait_recv()

        @pl.when(first_high)
        def _():
            def visit(m):
                arrival(2 * m + c)
                relay(2 * m + c).start()

            loop(HALF // 2, visit)

        p_own[it] = jnp.zeros(p_own.shape[1:], jnp.float32)

        @pl.when(active)
        def _():
            def ready(t):
                direct = jnp.logical_and(holder, base + t != r)
                relayed = jnp.logical_and(first_high, lax.rem(t, 2) != c)

                @pl.when(jnp.logical_or(direct, relayed))
                def _():
                    arrival(t)

                @pl.when(b == 1)
                def _():
                    remote(
                        w_own.at[it], w_cross.at[it, t],
                        far_send.at[0], turn_recv.at[HALF + t], (b, r),
                    ).wait_recv()
                    w_in[it, t] += w_cross[it, t]

            def visit(i, carry):
                both = [
                    2 * lax.rem(2 * i + k, HALF // 2) + lax.rem(c + 2 * i // (HALF // 2), 2)
                    for k in range(2)
                ]
                for t in both:
                    ready(t)
                for t in both:
                    low = stacked(w_in[it, t])
                    rows = spot(t, cols)
                    carry = carry + dot(low, aux[0, rows, :], STRAIGHT)
                    carry = carry + dot(low, aux[1, rows, :], STRAIGHT)
                return carry

            total = lax.fori_loop(0, HALF // 2, visit, jnp.zeros((2 * PAD, cols), jnp.float32))
            p_own[it] = fold(total)

        def left(count):
            return lambda: await_sent(f_in.at[it, pl.ds(0, count)], far_send.at[0])

        def all_left():
            pl.when(first_low)(left(HALF - 1 + HALF // 2))
            pl.when(first_high)(left(HALF + HALF // 2))
            pl.when(jnp.logical_and(b == 1, r >= HALF))(left(HALF - 1))

        pending.append(all_left)

    def spread(it, vector):
        first_part = (z == 2 * b).astype(jnp.int32)
        low = stacked(vector)
        term = factor_chunk(aux, low)

        def deliver(t):
            here = b * HALF + t

            def copy(plane):
                return remote(
                    f_out.at[it, t], f_in.at[it, r], far_send.at[1], line_recv.at[1], (plane, here)
                )

            @pl.when(here != r)
            def _():
                copy(b).start()

            @pl.when(here == r)
            def _():
                f_in[it, r] = f_out[it, t]

            @pl.when(b == 1)
            def _():
                copy(0).start()

        first_low = jnp.logical_and(low_plane, low_line)
        first_high = jnp.logical_and(low_plane, r >= HALF)
        second = jnp.logical_and(b == 1, r >= HALF)

        @pl.when(first_high)
        def _():
            def mated(step):
                return remote(
                    c_out.at[it, step], c_in.at[it, step],
                    mate_send.at[0], mate_recv.at[step], (b, mate),
                )

            def theirs(step):
                for i in range(2):
                    c_out[it, step, i] = term(2 * (2 * step + i) + 1 - c)
                mated(step).start()

            def ours(step):
                kept = [term(2 * (2 * step + i) + c) for i in range(2)]
                mated(step).wait_recv()
                for i in range(2):
                    far_out[it, 2 * step + i] = kept[i] + c_in[it, step, i]
                for i in range(2):
                    t = 2 * step + turned_by(i, 2)
                    remote(
                        far_out.at[it, t], far_in.at[it, r - HALF],
                        far_send.at[1], line_recv.at[1], (0, t),
                    ).start()

            loop(NEAR, theirs)
            loop(NEAR, ours)

        @pl.when(jnp.logical_or(first_low, second))
        def _():
            def visit(step):
                part = lax.rem(first_part + step // 2, 2)
                first = part * NEAR + 2 * lax.rem(step + r // 2, 2)
                for i in range(2):
                    for side in range(2):
                        columns = slice(side * chunk, (side + 1) * chunk)
                        f_out[it, first + i, :, columns] = term(2 * (first + i) + side)
                for i in range(2):
                    deliver(first + turned_by(i, 2))

            loop(NEAR, visit)

        settle()

        def left(count):
            return lambda: await_sent(f_in.at[it, pl.ds(0, count)], far_send.at[1])

        def arrive(count):
            return lambda: await_arrivals(f_in.at[it, pl.ds(0, count)], line_recv.at[1])

        def all_left():
            pl.when(first_low)(left(HALF - 1))
            pl.when(first_high)(left(HALF // 2))
            pl.when(first_high)(lambda: await_sent(c_out.at[it], mate_send.at[0]))
            pl.when(second)(left(2 * HALF - 1))

        pending.append(all_left)
        pl.when(first_low)(arrive(HALF - 1 + HALF // 2))
        pl.when(first_high)(arrive(HALF))
        pl.when(second)(arrive(HALF - 1))

        @pl.when(r >= HALF)
        def _():
            f_vec[it] = tree_sum([f_in[it, q] for q in range(HALF, LINE)])

        @pl.when(first_low)
        def _():
            near = tree_sum([f_in[it, q] for q in range(HALF)])
            sides = [tree_sum([far_in[it, q] for q in range(side, HALF, 2)]) for side in range(2)]
            f_vec[it] = near + jnp.concatenate(sides, axis=1)

    def onto_centres(low):
        return lambda q: dot(low, km[q], STRAIGHT)

    def onto_rows(q, low):
        return dot(low, km[q], FLIPPED)

    f_vec[0] = jnp.zeros(f_vec.shape[1:], jnp.float32)
    f_vec[1] = jnp.zeros(f_vec.shape[1:], jnp.float32)
    split(0, tri)
    for share in shares:
        share.wait_recv()
        pending.append(share.wait_send)
    mine, other = tgt[...], tgt_in[...]
    targets = jnp.concatenate(
        [jnp.where(low_plane, mine, other), jnp.where(low_plane, other, mine)], axis=1
    ).astype(jnp.bfloat16)
    other_norm = square_norm(feat_in)

    def first_term(q):
        build(feat_in, other_norm, cn[q][:1], across, q)
        return dot(targets, km[q], STRAIGHT)

    start = scatter(0, first_term, True) / count_all
    turned = gather(0, start, cols, factor_rows(tri))
    turn(0, turned)
    swap(p_own.at[0], p_in.at[0], 2)
    residual = p_own[0] + p_in[0]
    r_vec[...] = residual
    norm = row_sum(residual * residual)
    spread(0, residual)
    mine = scatter(1, factor_chunk(tri, stacked(f_vec[0])), False, find_places)
    g_own[...] = mine
    image = gather(1, with_split_scalars(mine, norm), 2 * own_rows, onto_rows, True)
    e_own[0] = image
    swap(e_own.at[0], e_in.at[0], 3)
    e_vec[...] = e_own[0] + e_in[0]
    gram = scatter(2, onto_centres(e_vec[...].astype(jnp.bfloat16)), True) / count_all
    ridge = jnp.where(low_plane, ridge_weight, 0.0) * row_sum(f_vec[0] * f_vec[0])
    curve = row_sum(gram * g_own[...]) + ridge
    turned = gather(2, with_scalars(gram, curve), cols, factor_rows(tri))
    holds = jnp.logical_or(b == 1, low_line)
    turn(1, jnp.where(holds, turned + ridge_weight * f_vec[0], turned))
    p_own[1, PAD - 1 :, :chunk] = scalars(2)
    swap(p_own.at[1], p_in.at[1], 2)
    norm_first = scalars_rounded(1)
    both = p_own[1] + p_in[1]
    step_first = ratio(norm_first, to_column(both[PAD - 1 :]))
    residual = r_vec[...] - step_first * both
    norm = row_sum(residual * residual)
    spread(1, residual)
    mine = scatter(3, factor_chunk(tri, stacked(f_vec[1])), False)
    image = gather(3, with_split_scalars(mine, norm), 2 * own_rows, onto_rows, True)
    norm_next = scalars_rounded(3)
    weight = ratio(norm_next, norm_first)
    forward = f_vec[1] + weight * f_vec[0]
    e_own[1] = with_scalars(image, ridge_weight * row_sum(forward * forward))
    swap(e_own.at[1], e_in.at[1], 3)
    ridge = jnp.where(low_plane, e_own[1, PAD - 1 :, :chunk], e_in[1, PAD - 1 :, :chunk])
    exact = e_own[1] + e_in[1] + weight * e_vec[...]
    low = exact.astype(jnp.bfloat16).astype(jnp.float32)
    curve = row_sum(low * exact) / count_all + to_column(ridge)

    wide = LANES // 4
    settle()
    e_own[1] = exact
    ours = spot(b, own_rows)
    pieces = jnp.concatenate(
        [stacked(e_own[1, :, ours]), stacked(step_first * e_vec[:, ours])], axis=0
    )

    def move(q):
        return remote(
            m_out.at[q], m_in.at[r], far_send.at[0], line_recv.at[0], (b, q)
        )

    curve_row = to_lanes(curve, LANES)
    last = lax.broadcasted_iota(jnp.int32, (PAD, LANES), 0) == PAD - 1

    def put(step):
        first = group(NEAR - 1 - step) * NEAR
        both = dot(pieces, place[:, spot(first // NEAR, NEAR * LANES)], STRAIGHT)
        second, early = fold(both[: 2 * PAD]), fold(both[2 * PAD :])
        for i in range(NEAR):
            lanes = slice(i * LANES, (i + 1) * LANES)
            tile = second[:, lanes] + pltpu.roll(early[:, lanes], wide, 1)
            m_out[first + i] = jnp.where(last, curve_row, tile)
        for i in range(NEAR):
            q = first + turned_by(i, NEAR)

            @pl.when(q != r)
            def _():
                move(q).start()

    loop(NEAR, put)
    m_in[r] = m_out[r]
    settle()

    await_arrivals(m_in.at[pl.ds(0, LINE - 1)], line_recv.at[0])
    tiles = [m_in[q] for q in range(LINE)]
    step_next = ratio(norm_next, to_column(tree_sum(tiles)[PAD - 1 :]))
    band = lax.broadcasted_iota(jnp.int32, (PAD, LANES), 1) // wide
    for four in range(LINE // 4):
        total = None
        for i in range(4):
            tile = tiles[four * 4 + i]
            value = pltpu.roll(tile, LANES - wide, 1) + step_next * tile
            if i > 0:
                value = pltpu.roll(value, i * wide, 1)
            total = value if total is None else jnp.where(band == i, value, total)
        out[:, four * LANES : (four + 1) * LANES] = total[:CLASSES]

    await_sent(m_out.at[pl.ds(0, LINE - 1)], far_send.at[0])


def fused(features, labels, destination, centres, tri_inverse, aux_inverse):
    own_rows, width = features.shape
    rows, cols = tri_inverse.shape
    chunk = rows // LINE
    slots = LINE * max(2, 2 * own_rows // LINE)

    def floats(*shape):
        return pltpu.VMEM(shape, jnp.float32)

    def halves(*shape):
        return pltpu.VMEM(shape, jnp.bfloat16)

    scratch = [
        halves(own_rows, width),
        pltpu.VMEM((1, own_rows), jnp.int32),
        halves(rows, width),
        pltpu.VMEM((1, own_rows), jnp.int32),
        floats(2, rows, cols),
        halves(2, rows, cols),
        halves(2, rows, cols),
        halves(LINE, PLANES * own_rows, chunk),
        floats(LINE, PAD, chunk),
        halves(own_rows, LINE * LANES),
        halves(own_rows, width),
        floats(PAD, own_rows),
        floats(PAD, own_rows),
        floats(4, LINE, PAD, chunk),
        floats(4, LINE, PAD, chunk),
        floats(4, LINE, PAD, chunk),
        halves(2, LINE, 2 * PAD, chunk // 2),
        floats(2, PAD, cols),
        floats(2, HALF, PAD, cols),
        floats(2, HALF, PAD, cols),
        floats(2, PAD, cols),
        floats(2, PAD, cols),
        floats(PAD, cols),
        floats(PAD, chunk),
        floats(2, HALF, PAD, cols),
        floats(2, LINE, PAD, cols),
        floats(2, PAD, cols),
        floats(2, NEAR, 2, PAD, chunk),
        floats(2, NEAR, 2, PAD, chunk),
        floats(2, HALF, PAD, chunk),
        floats(2, HALF, PAD, chunk),
        floats(2, PAD, PLANES * own_rows),
        floats(2, PAD, PLANES * own_rows),
        floats(PAD, PLANES * own_rows),
        floats(LINE, PAD, LANES),
        floats(LINE, PAD, LANES),
        dma((6,)),
        dma((2,)),
        dma((2,)),
        dma((2, LINE // NEAR)),
        dma((LINE,)),
        dma((1,)),
        dma((NEAR,)),
        dma((4,)),
        dma((4,)),
    ]
    whole = pl.BlockSpec(memory_space=pltpu.VMEM)
    away = pl.BlockSpec(memory_space=pltpu.MemorySpace.HBM)
    return pl.pallas_call(
        functools.partial(fused_kernel, float(own_rows * PLANES * LINE), 2.0 / width),
        out_shape=jax.ShapeDtypeStruct((CLASSES, slots), jnp.float32),
        in_specs=[away] * 6,
        out_specs=whole,
        scratch_shapes=scratch,
        compiler_params=pltpu.CompilerParams(
            collective_id=0, has_side_effects=True, vmem_limit_bytes=56 * 1024 * 1024
        ),
    )(
        features,
        labels[None, :],
        centres,
        destination.reshape(1, own_rows),
        tri_inverse,
        aux_inverse,
    )


def exact_product(dims, vector, block):
    parts = jnp.concatenate(three_parts(vector), axis=0).astype(jnp.bfloat16)
    total = None
    for part in reversed(block):
        product = dot(parts, part.astype(jnp.bfloat16), dims)
        product = product[2 * PAD :] + product[PAD : 2 * PAD] + product[:PAD]
        total = product if total is None else total + product
    return total


def forward_kernel(u_ref, block_ref, o_ref):
    o_ref[...] = exact_product(FLIPPED, u_ref[...], three_parts(block_ref[...]))


def backward_kernel(u_ref, block_ref, o_ref):
    product = exact_product(STRAIGHT, u_ref[...], three_parts(block_ref[...]))

    @pl.when(pl.program_id(0) == 0)
    def _():
        o_ref[...] = product

    @pl.when(pl.program_id(0) > 0)
    def _():
        o_ref[...] += product


STEP = 512

def factor_forward(block, vector):
    rows, cols = block.shape
    return pl.pallas_call(
        forward_kernel,
        grid=(rows // STEP,),
        in_specs=[
            pl.BlockSpec((PAD, cols), lambda i: (0, 0)),
            pl.BlockSpec((STEP, cols), lambda i: (i, 0)),
        ],
        out_specs=pl.BlockSpec((PAD, STEP), lambda i: (0, i)),
        out_shape=jax.ShapeDtypeStruct((PAD, rows), jnp.float32),
    )(vector, block)


def factor_backward(block, vector):
    rows, cols = block.shape
    return pl.pallas_call(
        backward_kernel,
        grid=(rows // STEP,),
        in_specs=[
            pl.BlockSpec((PAD, STEP), lambda i: (0, i)),
            pl.BlockSpec((STEP, cols), lambda i: (i, 0)),
        ],
        out_specs=pl.BlockSpec((PAD, cols), lambda i: (0, 0)),
        out_shape=jax.ShapeDtypeStruct((PAD, cols), jnp.float32),
    )(vector, block)


def square_norms(rows_x):
    return jnp.einsum("nd,nd->n", rows_x, rows_x, preferred_element_type=jnp.float32)


def plane_sum(x):
    return lax.psum(x, "rows")


def joint_sum(kind, nb, nr, block, *operands):
    x = operands[0]
    if kind == "plane":
        out = plane_sum(x)
        lines = jnp.arange(PAD, dtype=jnp.int32)[:, None]
        return out, factor_backward(block, jnp.where(lines < CLASSES, out, 0.0))
    if kind == "turn":
        width = x.shape[1] * nr // nb
        full = lax.all_gather(lax.psum(x, "blk") + operands[1], "rows", axis=1, tiled=True)
        out = lax.dynamic_slice_in_dim(full, lax.axis_index("blk") * width, width, 1)
        return out, factor_backward(block, out)
    if kind == "slice":
        size = x.shape[1] * nb // nr
        full = lax.all_gather(lax.psum(x, "rows"), "blk", axis=1, tiled=True)
        out = lax.dynamic_slice_in_dim(full, lax.axis_index("rows") * size, size, 1)
    else:
        out = operands[1] + operands[2] * lax.psum(x, "blk")
    return out, factor_forward(block, out)


def to_low(values):
    return lax.reduce_precision(values, 8, 7).astype(jnp.bfloat16)


def with_row(vector, scalars):
    return vector + jnp.pad(scalars[None, :], ((PAD - 1, 0), (0, vector.shape[1] - PAD)))


def on_device(nb, nr, features, labels, destination, centres, tri_inverse, aux_inverse):
    own_rows, width = features.shape
    capacity = max(2, 2 * own_rows // nr)
    scale = 2.0 / width
    count_all = float(own_rows * nb * nr)
    b = lax.axis_index("blk")
    class_rows = jnp.arange(PAD, dtype=jnp.int32)[:, None]
    real = class_rows < CLASSES

    tags = jnp.pad(labels.astype(jnp.bfloat16), (0, -own_rows % (16 * width)))
    tags = tags.reshape(-1, width)
    shared = lax.all_gather(jnp.concatenate([features, tags], axis=0), "blk", axis=0)
    rows_x = shared[:, :own_rows].reshape(nb * own_rows, width)
    tags = shared[:, own_rows:].reshape(nb, -1)[:, :own_rows].reshape(nb * own_rows)
    centre_norm = square_norms(centres)
    rows_norm = square_norms(rows_x)
    inner = lax.dot_general(
        rows_x, centres, (((1,), (1,)), ((), ())), preferred_element_type=jnp.float32
    )
    kmat = jnp.exp(-(rows_norm[:, None] + centre_norm[None, :] - 2.0 * inner) * scale).astype(
        jnp.bfloat16
    )
    hits = tags.astype(jnp.float32)[None, :] == class_rows.astype(jnp.float32)
    targets = jnp.where(real, jnp.where(hits, 1.0, -1.0), 0.0).astype(jnp.bfloat16)

    def clean(vector):
        return jnp.where(real, vector, 0.0)

    def onto_rows(low):
        return lax.dot_general(
            low, kmat, (((1,), (1,)), ((), ())), preferred_element_type=jnp.float32
        )

    def images(second):
        high = to_low(second)
        rest = second - high.astype(jnp.float32)
        mid = to_low(rest)
        low = to_low(rest - mid.astype(jnp.float32))
        three = onto_rows(jnp.concatenate([high, mid, low], axis=0))
        both = jnp.concatenate([three[:PAD], three[PAD : 2 * PAD] + three[2 * PAD :]], axis=0)
        both = lax.psum(both, "blk")
        image = to_low(both[:PAD])
        exact = both[:PAD] + both[PAD:]
        curve = jnp.sum(image.astype(jnp.float32) * exact, axis=1) / count_all
        return image, curve

    def ratio(above, below):
        return jnp.where(real, (above / below)[:, None], 0.0)

    def normal(vector):
        return jnp.sum(vector * vector, axis=1)

    start = jnp.dot(targets, kmat, preferred_element_type=jnp.float32) / count_all
    start = joint_sum("plane", nb, nr, tri_inverse, start)[1]
    start = joint_sum("turn", nb, nr, aux_inverse, start, jnp.zeros_like(start))[1]
    zeros = jnp.zeros_like(start)
    rhs, start = joint_sum("pair", nb, nr, aux_inverse, start, zeros, zeros + 1.0)
    first, start = joint_sum("slice", nb, nr, tri_inverse, start)
    joined = plane_sum(with_row(start, normal(rhs)))
    norm_first = joined[PAD - 1, :PAD]
    second = clean(joined)
    image, curve = images(second)
    curve = curve + ridge_weight * normal(first)
    gram = jnp.dot(image, kmat, preferred_element_type=jnp.float32) / count_all
    joined, turned = joint_sum("plane", nb, nr, tri_inverse, with_row(gram, curve))
    step_first = ratio(norm_first, joined[PAD - 1, :PAD])
    turned = joint_sum("turn", nb, nr, aux_inverse, turned, ridge_weight * first)[1]
    residual, start = joint_sum("pair", nb, nr, aux_inverse, turned, rhs, zeros - step_first)
    first_next, start = joint_sum("slice", nb, nr, tri_inverse, start)
    joined = plane_sum(with_row(start, normal(residual)))
    norm_next = joined[PAD - 1, :PAD]
    turn_weight = ratio(norm_next, norm_first)
    first_next = first_next + turn_weight * first
    second_next = clean(joined) + turn_weight * second
    image, curve = images(second_next)
    curve = curve + ridge_weight * normal(first_next)
    curve = lax.psum(jnp.pad(curve[:, None], ((0, 0), (0, 127))), "rows")[:, 0]
    step_next = ratio(norm_next, curve)
    coefficients = step_first * second + step_next * second_next
    scores = lax.psum(onto_rows(to_low(coefficients)), "blk")
    scores = lax.dynamic_slice_in_dim(scores, b * own_rows, own_rows, 1)

    target = destination[:, 0]
    row_ids = jnp.arange(own_rows, dtype=jnp.int32)
    same = (target[:, None] == target[None, :]) & (row_ids[None, :] < row_ids[:, None])
    before = jnp.sum(same.astype(jnp.int32), axis=1)
    slots = nr * capacity
    spread = (
        (target * capacity + before)[:, None] == jnp.arange(slots, dtype=jnp.int32)[None, :]
    ).astype(jnp.float32)
    placed = jnp.dot(scores, spread, precision=highest, preferred_element_type=jnp.float32)
    placed = placed.reshape(PAD, nr, capacity).transpose(1, 0, 2)
    lanes = -capacity % 128
    placed = jnp.pad(placed, ((0, 0), (0, 0), (0, lanes)))
    moved = lax.all_to_all(placed, "rows", split_axis=0, concat_axis=0, tiled=True)
    moved = moved[:, :CLASSES, :capacity]
    return moved.transpose(1, 0, 2).reshape(CLASSES, slots)


def solution(mesh):
    nb, nr = mesh.shape["blk"], mesh.shape["rows"]
    body = fused if (nb, nr) == (PLANES, LINE) else functools.partial(on_device, nb, nr)
    return jax.shard_map(
        body,
        mesh=mesh,
        in_specs=(
            P(("blk", "rows"), None),
            P(("blk", "rows")),
            P(("blk", "rows"), None),
            P("blk", None),
            P("blk", "rows"),
            P("blk", "rows"),
        ),
        out_specs=P(None, ("blk", "rows")),
        check_vma=False,
    )
```

```python
import functools

import jax
import jax.numpy as jnp
from jax import lax
from jax.experimental import pallas as pl
from jax.experimental.pallas import tpu as pltpu
from jax.sharding import PartitionSpec as P

CLASSES = 7
PAD = 8
LANES = 128
MESH = pl.DeviceIdType.MESH
ridge_weight = 0.1
highest = lax.Precision.HIGHEST

PLANES = 2
LINE = 16
HALF = LINE // 2
NEAR = 4
FLIPPED = (((1,), (1,)), ((), ()))
STRAIGHT = (((1,), (0,)), ((), ()))

dma = pltpu.SemaphoreType.DMA


def spot(index, chunk):
    return pl.ds(pl.multiple_of(index * chunk, chunk), chunk)


def dot(left, right, dims):
    return lax.dot_general(left, right, dims, preferred_element_type=jnp.float32)


def stacked(vector):
    high = vector.astype(jnp.bfloat16).astype(jnp.float32)
    return jnp.concatenate([high, vector - high], axis=0).astype(jnp.bfloat16)


def fold(product):
    return product[:PAD] + product[PAD:]


def tree_sum(terms):
    while len(terms) > 1:
        pairs = [terms[i] + terms[i + 1] for i in range(0, len(terms) - 1, 2)]
        terms = pairs + terms[len(pairs) * 2 :]
    return terms[0]


def diagonal(width, first):
    sub = lax.broadcasted_iota(jnp.int32, (PAD, width), 0)
    lane = lax.broadcasted_iota(jnp.int32, (PAD, width), 1)
    return sub + first == lane


def to_lanes(column, width, first=0):
    spread = jnp.where(diagonal(width, first), column, 0.0)
    return jnp.sum(spread, axis=0, keepdims=True)


def to_column(row, first=0):
    spread = jnp.where(diagonal(row.shape[1], first), row, 0.0)
    return jnp.sum(spread, axis=1, keepdims=True)


def three_parts(x):
    high = x.astype(jnp.bfloat16).astype(jnp.float32)
    rest = x - high
    mid = rest.astype(jnp.bfloat16).astype(jnp.float32)
    return high, mid, rest - mid


def with_last(vector, row):
    lines = lax.broadcasted_iota(jnp.int32, vector.shape, 0)
    return jnp.where(lines == PAD - 1, row, vector)


def rows_of(columns, width):
    return tree_sum([to_lanes(column, width, k * PAD) for k, column in enumerate(columns)])


def packed(vector):
    half = vector.shape[1] // 2
    return jnp.concatenate([vector[:, :half], vector[:, half:]], axis=0).astype(jnp.bfloat16)


def unpacked(tile):
    wide = tile.astype(jnp.float32)
    return jnp.concatenate([wide[:PAD], wide[PAD:]], axis=1).astype(jnp.bfloat16)


def ratio(above, below):
    lines = lax.broadcasted_iota(jnp.int32, above.shape, 0)
    return jnp.where(lines < CLASSES, above / below, 0.0)


def row_sum(values):
    return jnp.sum(values, axis=1, keepdims=True)


def fused_kernel(count_all, scale, *refs):
    arrays, out, scratch = refs[:6], refs[6], refs[7:]
    (
        feat, label, cent, dest, stage, tri, aux, km, cn, place, feat_in, tgt, tgt_in,
        rs_out, rs_in, ag, ag_low, w_own, w_in, w_cross, p_own, p_in, r_vec, g_own,
        f_out, f_in, f_vec, c_out, c_in, far_out, far_in, e_own, e_in, e_vec, m_out, m_in,
        load_sem, far_send, line_recv, group_recv, turn_recv, mate_send, mate_recv, ready, one_send, one_recv,
    ) = scratch
    b, r = lax.axis_index("blk"), lax.axis_index("rows")
    z, c = r // NEAR, lax.rem(r, 2)
    mate = r + 1 - 2 * c
    across = 1 - b
    chunk = ag.shape[3]
    own_rows = feat.shape[0]
    cols = tri.shape[2]
    low_plane, low_line = b == 0, r < HALF
    active = jnp.logical_or(low_plane, r >= HALF)
    pending = []

    def settle():
        for action in pending:
            action()
        pending.clear()

    def remote(source, target, send_sem, recv_sem, device):
        return pltpu.make_async_remote_copy(
            src_ref=source, dst_ref=target, send_sem=send_sem, recv_sem=recv_sem,
            device_id=device, device_id_type=MESH,
        )

    def await_arrivals(like, sem):
        remote(like, like, sem, sem, (b, r)).wait_recv()

    def await_sent(like, sem):
        remote(like, like, sem, sem, (b, r)).wait_send()

    def loop(count, body):
        def step(i, carry):
            body(i)
            return carry

        lax.fori_loop(0, count, step, 0)

    def turned_by(i, count):
        return lax.rem(r + i, count)

    def group(j):
        return lax.rem(z + j, 2) + 2 * lax.rem(z // 2 + j // 2, 2)

    barrier = pltpu.get_barrier_semaphore()

    def hello(k):
        pl.semaphore_signal(
            barrier, inc=1, device_id=(b, lax.rem(r + k * NEAR, LINE)), device_id_type=MESH
        )

    def beside(k):
        return (b, z * NEAR + lax.rem(r + k, NEAR))

    pl.semaphore_signal(barrier, inc=1, device_id=(across, r), device_id_type=MESH)
    for k in range(1, NEAR):
        hello(k)
        pl.semaphore_signal(barrier, inc=1, device_id=beside(k), device_id_type=MESH)
    into = (feat, label, cent, dest, stage.at[0], stage.at[1])
    loads = [
        pltpu.make_async_copy(source, target, load_sem.at[i])
        for i, (source, target) in enumerate(zip(arrays, into))
    ]
    for load in loads:
        load.start()
    for load in loads[:4]:
        load.wait()
    loads = loads[4:]

    class_rows = lax.broadcasted_iota(jnp.int32, (PAD, own_rows), 0)
    hits = jnp.where(label[...] == class_rows, 1.0, -1.0)
    tgt[...] = jnp.where(class_rows < CLASSES, hits, 0.0)

    def squares_of_centres(q):
        values = cent[spot(q, chunk), :].astype(jnp.float32)
        values = values * values
        high = values.astype(jnp.bfloat16)
        low = (values - high.astype(jnp.float32)).astype(jnp.bfloat16)
        ones = jnp.ones((PAD, values.shape[1]), jnp.bfloat16)
        return (dot(ones, high, FLIPPED) + dot(ones, low, FLIPPED))[:1] * scale

    def square_norm(source):
        values = source[...].astype(jnp.float32)
        return row_sum(values * values) * scale

    def build(source, norm, norms, half, q):
        inner = dot(source[...], cent[spot(q, chunk), :], FLIPPED)
        power = inner * (2.0 * scale) - norm - norms
        km[q, spot(half, own_rows), :] = jnp.exp(power).astype(jnp.bfloat16)

    own_norm = square_norm(feat)

    def own_half(q):
        for i in range(NEAR):
            norms = squares_of_centres(q * NEAR + i)
            cn[q * NEAR + i] = jnp.broadcast_to(norms, (PAD, chunk))
            build(feat, own_norm, norms, b, q * NEAR + i)

    loop(LINE // NEAR, own_half)
    pl.semaphore_wait(barrier, 2 * NEAR - 1)
    shares = [
        remote(feat, feat_in, one_send.at[0], one_recv.at[0], (across, r)),
        remote(tgt, tgt_in, one_send.at[1], one_recv.at[1], (across, r)),
    ]
    for share in shares:
        share.start()
    for k in range(1, NEAR):
        pl.semaphore_signal(ready, inc=1, device_id=beside(k), device_id_type=MESH)

    def split(index, target):
        loads[index].wait()

        def visit(i):
            piece = spot(i, chunk)
            values = stage[index, piece, :]
            high = values.astype(jnp.bfloat16)
            target[0, piece, :] = high
            target[1, piece, :] = (values - high.astype(jnp.float32)).astype(jnp.bfloat16)

        loop(LINE, visit)

    def find_places():
        to_row = dest[...].astype(jnp.float32)
        sub = lax.broadcasted_iota(jnp.int32, (own_rows, own_rows), 0)
        lane = lax.broadcasted_iota(jnp.int32, (own_rows, own_rows), 1)
        to = row_sum(jnp.where(sub == lane, to_row, 0.0))
        same = jnp.logical_and(to == to_row, lane < sub)
        before = row_sum(jnp.where(same, 1.0, 0.0))
        position = to * LANES + before

        def visit(q):
            lanes = lax.broadcasted_iota(jnp.int32, (own_rows, own_rows), 1) + q * own_rows
            hit = jnp.where(lanes.astype(jnp.float32) == position, 1.0, 0.0)
            place[:, spot(q, own_rows)] = hit.astype(jnp.bfloat16)

        loop(place.shape[1] // own_rows, visit)

    def scatter(phase, term, sources_all, meanwhile=None):
        def copy(q):
            return remote(
                rs_out.at[phase, q], rs_in.at[phase, r],
                far_send.at[0], line_recv.at[0], (b, q),
            )

        def send():
            def visit(step):
                first = group(NEAR - 1 - step) * NEAR
                for i in range(NEAR):
                    rs_out[phase, first + i] = term(first + i)
                for i in range(NEAR):
                    q = first + turned_by(i, NEAR)

                    @pl.when(q != r)
                    def _():
                        copy(q).start()

            loop(NEAR, visit)
            rs_in[phase, r] = rs_out[phase, r]

        def left():
            await_sent(rs_out.at[phase, pl.ds(0, LINE - 1)], far_send.at[0])

        def gated(action):
            if sources_all:
                action()
            else:
                pl.when(active)(action)

        gated(send)
        settle()
        if meanwhile is not None:
            meanwhile()

        def arrive(count):
            return lambda: await_arrivals(rs_in.at[phase, pl.ds(0, count)], line_recv.at[0])

        if sources_all:
            arrive(LINE - 1)()
        else:
            pl.when(low_plane)(arrive(LINE - 1))
            pl.when(jnp.logical_and(b == 1, r >= HALF))(arrive(HALF - 1))
            pl.when(jnp.logical_and(b == 1, low_line))(arrive(HALF))
        pending.append(lambda: gated(left))
        upper = tree_sum([rs_in[phase, q] for q in range(HALF, LINE)])
        if sources_all:
            return upper + tree_sum([rs_in[phase, q] for q in range(HALF)])
        ag[phase, r] = upper

        @pl.when(low_plane)
        def _():
            ag[phase, r] += tree_sum([rs_in[phase, q] for q in range(HALF)])

        return ag[phase, r]

    def gather(phase, mine, width, use, rounded=False):
        if rounded:
            held = ag_low.at[phase // 2]
            held[r] = packed(mine)
        else:
            held = ag.at[phase]
            held[r] = mine

        def copy(q):
            return remote(
                held.at[r], held.at[r],
                far_send.at[1], group_recv.at[phase % 2, z], (b, q),
            )

        def send(step):
            first = group(NEAR - 1 - step) * NEAR
            for i in range(NEAR):
                q = first + turned_by(i, NEAR)

                @pl.when(q != r)
                def _():
                    copy(q).start()

        loop(NEAR, send)
        settle()
        if phase == 0:
            split(1, aux)

        def visit(j, carry):
            first = group(j) * NEAR
            def arrive(count):
                return lambda: await_arrivals(
                    held.at[pl.ds(first, count)], group_recv.at[phase % 2, group(j)]
                )

            pl.when(j == 0)(arrive(NEAR - 1))
            pl.when(j > 0)(arrive(NEAR))
            for i in range(NEAR):
                low = unpacked(held[first + i]) if rounded else stacked(held[first + i])
                carry = carry + use(first + i, low)
            return carry

        lines = PAD if rounded else 2 * PAD
        total = lax.fori_loop(0, NEAR, visit, jnp.zeros((lines, width), jnp.float32))

        def left():
            await_sent(held.at[pl.ds(0, LINE - 1)], far_send.at[1])

        pending.append(left)
        return total if rounded else fold(total)

    def scalars(phase):
        rows = [ag[phase, q] for q in range(LINE)]
        return tree_sum(rows)[PAD - 1 :]

    def scalars_rounded(phase):
        rows = [ag_low[phase // 2, q].astype(jnp.float32) for q in range(LINE)]
        row = tree_sum(rows)[PAD - 1 : PAD]
        return tree_sum([to_column(row, k * PAD) for k in range(3)])

    def swap(own, landing, index, meanwhile=None):
        copy = remote(own, landing, one_send.at[index], one_recv.at[index], (across, r))
        copy.start()
        settle()
        result = meanwhile() if meanwhile is not None else None
        copy.wait_recv()
        pending.append(copy.wait_send)
        return result

    def factor_rows(factor):
        def use(q, low):
            return dot(low, factor[0, spot(q, chunk), :], STRAIGHT) + dot(
                low, factor[1, spot(q, chunk), :], STRAIGHT
            )

        return use

    def factor_chunk(factor, low):
        def term(q):
            return fold(
                dot(low, factor[0, spot(q, chunk), :], FLIPPED)
                + dot(low, factor[1, spot(q, chunk), :], FLIPPED)
            )

        return term

    def turn(it, product):
        w_own[it] = product
        base = b * HALF

        def inside(q):
            return remote(
                w_own.at[it], w_in.at[it, r - base],
                far_send.at[0], turn_recv.at[r - base], (b, q),
            )

        def outside(q):
            return remote(
                w_own.at[it], w_cross.at[it, r - HALF],
                far_send.at[0], turn_recv.at[r], (1, q),
            )

        def relay(t):
            return remote(
                w_in.at[it, t], w_in.at[it, t], far_send.at[0], turn_recv.at[t], (b, mate)
            )

        def near(act):
            def visit(i):
                q = base + turned_by(i, HALF)

                @pl.when(q != r)
                def _():
                    act(inside(q))

            return lambda: loop(HALF, visit)

        def far(act):
            return lambda: loop(HALF // 2, lambda m: act(inside(HALF + lax.rem(2 * m + r, HALF))))

        def over(act):
            return lambda: loop(HALF, lambda i: act(outside(HALF + turned_by(i, HALF))))

        holder = jnp.logical_and(r >= base, r < base + HALF)
        first_low = jnp.logical_and(low_plane, low_line)
        first_high = jnp.logical_and(low_plane, r >= HALF)

        @pl.when(holder)
        def _():
            w_in[it, r - base] = w_own[it]

        def start(copy):
            copy.start()

        pl.when(first_low)(far(start))
        pl.when(holder)(near(start))
        pl.when(first_high)(over(start))
        settle()

        def arrival(t):
            remote(
                w_own.at[it], w_in.at[it, t], far_send.at[0], turn_recv.at[t], (b, r)
            ).wait_recv()

        @pl.when(first_high)
        def _():
            def visit(m):
                arrival(2 * m + c)
                relay(2 * m + c).start()

            loop(HALF // 2, visit)

        p_own[it] = jnp.zeros(p_own.shape[1:], jnp.float32)

        @pl.when(active)
        def _():
            def ready(t):
                direct = jnp.logical_and(holder, base + t != r)
                relayed = jnp.logical_and(first_high, lax.rem(t, 2) != c)

                @pl.when(jnp.logical_or(direct, relayed))
                def _():
                    arrival(t)

                @pl.when(b == 1)
                def _():
                    remote(
                        w_own.at[it], w_cross.at[it, t],
                        far_send.at[0], turn_recv.at[HALF + t], (b, r),
                    ).wait_recv()
                    w_in[it, t] += w_cross[it, t]

            def visit(i, carry):
                both = [
                    2 * lax.rem(2 * i + k, HALF // 2) + lax.rem(c + 2 * i // (HALF // 2), 2)
                    for k in range(2)
                ]
                for t in both:
                    ready(t)
                for t in both:
                    low = stacked(w_in[it, t])
                    rows = spot(t, cols)
                    carry = carry + dot(low, aux[0, rows, :], STRAIGHT)
                    carry = carry + dot(low, aux[1, rows, :], STRAIGHT)
                return carry

            total = lax.fori_loop(0, HALF // 2, visit, jnp.zeros((2 * PAD, cols), jnp.float32))
            p_own[it] = fold(total)

        def left(count):
            return lambda: await_sent(f_in.at[it, pl.ds(0, count)], far_send.at[0])

        def all_left():
            pl.when(first_low)(left(HALF - 1 + HALF // 2))
            pl.when(first_high)(left(HALF + HALF // 2))
            pl.when(jnp.logical_and(b == 1, r >= HALF))(left(HALF - 1))

        pending.append(all_left)

    def spread(it, vector):
        first_part = (z == 2 * b).astype(jnp.int32)
        low = stacked(vector)
        term = factor_chunk(aux, low)

        def deliver(t):
            here = b * HALF + t

            def copy(plane):
                return remote(
                    f_out.at[it, t], f_in.at[it, r], far_send.at[1], line_recv.at[1], (plane, here)
                )

            @pl.when(here != r)
            def _():
                copy(b).start()

            @pl.when(here == r)
            def _():
                f_in[it, r] = f_out[it, t]

            @pl.when(b == 1)
            def _():
                copy(0).start()

        first_low = jnp.logical_and(low_plane, low_line)
        first_high = jnp.logical_and(low_plane, r >= HALF)
        second = jnp.logical_and(b == 1, r >= HALF)

        @pl.when(first_high)
        def _():
            def mated(step):
                return remote(
                    c_out.at[it, step], c_in.at[it, step],
                    mate_send.at[0], mate_recv.at[step], (b, mate),
                )

            def theirs(step):
                for i in range(2):
                    c_out[it, step, i] = term(2 * (2 * step + i) + 1 - c)
                mated(step).start()

            def ours(step):
                kept = [term(2 * (2 * step + i) + c) for i in range(2)]
                mated(step).wait_recv()
                for i in range(2):
                    far_out[it, 2 * step + i] = kept[i] + c_in[it, step, i]
                for i in range(2):
                    t = 2 * step + turned_by(i, 2)
                    remote(
                        far_out.at[it, t], far_in.at[it, r - HALF],
                        far_send.at[1], line_recv.at[1], (0, t),
                    ).start()

            loop(NEAR, theirs)
            loop(NEAR, ours)

        @pl.when(jnp.logical_or(first_low, second))
        def _():
            def visit(step):
                part = lax.rem(first_part + step // 2, 2)
                first = part * NEAR + 2 * lax.rem(step + r // 2, 2)
                for i in range(2):
                    for side in range(2):
                        columns = slice(side * chunk, (side + 1) * chunk)
                        f_out[it, first + i, :, columns] = term(2 * (first + i) + side)
                for i in range(2):
                    deliver(first + turned_by(i, 2))

            loop(NEAR, visit)

        settle()

        def left(count):
            return lambda: await_sent(f_in.at[it, pl.ds(0, count)], far_send.at[1])

        def arrive(count):
            return lambda: await_arrivals(f_in.at[it, pl.ds(0, count)], line_recv.at[1])

        def all_left():
            pl.when(first_low)(left(HALF - 1))
            pl.when(first_high)(left(HALF // 2))
            pl.when(first_high)(lambda: await_sent(c_out.at[it], mate_send.at[0]))
            pl.when(second)(left(2 * HALF - 1))

        pending.append(all_left)
        pl.when(first_low)(arrive(HALF - 1 + HALF // 2))
        pl.when(first_high)(arrive(HALF))
        pl.when(second)(arrive(HALF - 1))

        @pl.when(r >= HALF)
        def _():
            f_vec[it] = tree_sum([f_in[it, q] for q in range(HALF, LINE)])

        @pl.when(first_low)
        def _():
            near = tree_sum([f_in[it, q] for q in range(HALF)])
            sides = [tree_sum([far_in[it, q] for q in range(side, HALF, 2)]) for side in range(2)]
            f_vec[it] = near + jnp.concatenate(sides, axis=1)

    def onto_centres(low):
        return lambda q: dot(low, km[q], STRAIGHT)

    def onto_rows(q, low):
        return dot(low, km[q], FLIPPED)

    f_vec[0] = jnp.zeros(f_vec.shape[1:], jnp.float32)
    f_vec[1] = jnp.zeros(f_vec.shape[1:], jnp.float32)
    split(0, tri)
    pl.semaphore_wait(ready, NEAR - 1)
    for share in shares:
        share.wait_recv()
        pending.append(share.wait_send)
    mine, other = tgt[...], tgt_in[...]
    targets = jnp.concatenate(
        [jnp.where(low_plane, mine, other), jnp.where(low_plane, other, mine)], axis=1
    ).astype(jnp.bfloat16)
    other_norm = square_norm(feat_in)

    def first_term(q):
        build(feat_in, other_norm, cn[q][:1], across, q)
        return dot(targets, km[q], STRAIGHT)

    start = scatter(0, first_term, True) / count_all
    turned = gather(0, start, cols, factor_rows(tri))
    turn(0, turned)
    swap(p_own.at[0], p_in.at[0], 2)
    residual = p_own[0] + p_in[0]
    r_vec[...] = residual
    spread(0, residual)
    kept = {}

    def square(value):
        return row_sum(value * value)

    def first_wait():
        kept["norm"] = rows_of(three_parts(square(r_vec[...])), chunk)
        find_places()

    mine = scatter(1, factor_chunk(tri, stacked(f_vec[0])), False, first_wait)
    g_own[...] = mine
    image = gather(1, with_last(mine, kept["norm"]), 2 * own_rows, onto_rows, True)
    e_own[0] = image
    norm_first = swap(e_own.at[0], e_in.at[0], 3, lambda: scalars_rounded(1))
    e_vec[...] = e_own[0] + e_in[0]

    def second_wait():
        kept["ridge"] = jnp.where(low_plane, ridge_weight, 0.0) * square(f_vec[0])

    low = e_vec[...].astype(jnp.bfloat16)
    gram = scatter(2, onto_centres(low), True, second_wait) / count_all
    curve = to_lanes(row_sum(gram * g_own[...]) + kept["ridge"], chunk)
    turned = gather(2, with_last(gram, curve), cols, factor_rows(tri))
    holds = jnp.logical_or(b == 1, low_line)
    turn(1, jnp.where(holds, turned + ridge_weight * f_vec[0], turned))
    p_own[1, PAD - 1 :, :chunk] = scalars(2)
    swap(p_own.at[1], p_in.at[1], 2)
    both = p_own[1] + p_in[1]
    step_first = ratio(norm_first, to_column(both[PAD - 1 :]))
    residual = r_vec[...] - step_first * both
    r_vec[...] = residual
    spread(1, residual)

    def third_wait():
        kept["norm"] = rows_of(three_parts(square(r_vec[...])), chunk)
        products = [square(f_vec[1]), row_sum(f_vec[1] * f_vec[0]), square(f_vec[0])]
        kept["ridge"] = rows_of(products, 2 * own_rows)

    mine = scatter(3, factor_chunk(tri, stacked(f_vec[1])), False, third_wait)
    image = gather(3, with_last(mine, kept["norm"]), 2 * own_rows, onto_rows, True)
    e_own[1] = with_last(image, kept["ridge"])
    norm_next = swap(e_own.at[1], e_in.at[1], 3, lambda: scalars_rounded(3))
    weight = ratio(norm_next, norm_first)
    exact = e_own[1] + e_in[1] + weight * e_vec[...]
    low = exact.astype(jnp.bfloat16).astype(jnp.float32)
    row = jnp.where(low_plane, e_own[1, PAD - 1 :, :], e_in[1, PAD - 1 :, :])
    newer, mixed, older = [to_column(row, k * PAD) for k in range(3)]
    ridge = ridge_weight * (newer + 2.0 * weight * mixed + weight * weight * older)
    curve = row_sum(low * exact) / count_all + ridge

    wide = LANES // 4
    settle()
    e_own[1] = exact
    ours = spot(b, own_rows)
    pieces = jnp.concatenate(
        [stacked(e_own[1, :, ours]), stacked(step_first * e_vec[:, ours])], axis=0
    )

    def move(q):
        return remote(
            m_out.at[q], m_in.at[r], far_send.at[0], line_recv.at[0], (b, q)
        )

    curve_row = to_lanes(curve, LANES)
    last = lax.broadcasted_iota(jnp.int32, (PAD, LANES), 0) == PAD - 1

    def put(step):
        first = group(NEAR - 1 - step) * NEAR
        both = dot(pieces, place[:, spot(first // NEAR, NEAR * LANES)], STRAIGHT)
        second, early = fold(both[: 2 * PAD]), fold(both[2 * PAD :])
        for i in range(NEAR):
            lanes = slice(i * LANES, (i + 1) * LANES)
            tile = second[:, lanes] + pltpu.roll(early[:, lanes], wide, 1)
            m_out[first + i] = jnp.where(last, curve_row, tile)
        for i in range(NEAR):
            q = first + turned_by(i, NEAR)

            @pl.when(q != r)
            def _():
                move(q).start()

    loop(NEAR, put)
    m_in[r] = m_out[r]
    settle()

    await_arrivals(m_in.at[pl.ds(0, LINE - 1)], line_recv.at[0])
    tiles = [m_in[q] for q in range(LINE)]
    step_next = ratio(norm_next, to_column(tree_sum(tiles)[PAD - 1 :]))
    band = lax.broadcasted_iota(jnp.int32, (PAD, LANES), 1) // wide
    for four in range(LINE // 4):
        total = None
        for i in range(4):
            tile = tiles[four * 4 + i]
            value = pltpu.roll(tile, LANES - wide, 1) + step_next * tile
            if i > 0:
                value = pltpu.roll(value, i * wide, 1)
            total = value if total is None else jnp.where(band == i, value, total)
        out[:, four * LANES : (four + 1) * LANES] = total[:CLASSES]

    await_sent(m_out.at[pl.ds(0, LINE - 1)], far_send.at[0])


def fused(features, labels, destination, centres, tri_inverse, aux_inverse):
    own_rows, width = features.shape
    rows, cols = tri_inverse.shape
    chunk = rows // LINE
    slots = LINE * max(2, 2 * own_rows // LINE)

    def floats(*shape):
        return pltpu.VMEM(shape, jnp.float32)

    def halves(*shape):
        return pltpu.VMEM(shape, jnp.bfloat16)

    scratch = [
        halves(own_rows, width),
        pltpu.VMEM((1, own_rows), jnp.int32),
        halves(rows, width),
        pltpu.VMEM((1, own_rows), jnp.int32),
        floats(2, rows, cols),
        halves(2, rows, cols),
        halves(2, rows, cols),
        halves(LINE, PLANES * own_rows, chunk),
        floats(LINE, PAD, chunk),
        halves(own_rows, LINE * LANES),
        halves(own_rows, width),
        floats(PAD, own_rows),
        floats(PAD, own_rows),
        floats(4, LINE, PAD, chunk),
        floats(4, LINE, PAD, chunk),
        floats(4, LINE, PAD, chunk),
        halves(2, LINE, 2 * PAD, chunk // 2),
        floats(2, PAD, cols),
        floats(2, HALF, PAD, cols),
        floats(2, HALF, PAD, cols),
        floats(2, PAD, cols),
        floats(2, PAD, cols),
        floats(PAD, cols),
        floats(PAD, chunk),
        floats(2, HALF, PAD, cols),
        floats(2, LINE, PAD, cols),
        floats(2, PAD, cols),
        floats(2, NEAR, 2, PAD, chunk),
        floats(2, NEAR, 2, PAD, chunk),
        floats(2, HALF, PAD, chunk),
        floats(2, HALF, PAD, chunk),
        floats(2, PAD, PLANES * own_rows),
        floats(2, PAD, PLANES * own_rows),
        floats(PAD, PLANES * own_rows),
        floats(LINE, PAD, LANES),
        floats(LINE, PAD, LANES),
        dma((6,)),
        dma((2,)),
        dma((2,)),
        dma((2, LINE // NEAR)),
        dma((LINE,)),
        dma((1,)),
        dma((NEAR,)),
        pltpu.SemaphoreType.REGULAR,
        dma((4,)),
        dma((4,)),
    ]
    whole = pl.BlockSpec(memory_space=pltpu.VMEM)
    away = pl.BlockSpec(memory_space=pltpu.MemorySpace.HBM)
    return pl.pallas_call(
        functools.partial(fused_kernel, float(own_rows * PLANES * LINE), 2.0 / width),
        out_shape=jax.ShapeDtypeStruct((CLASSES, slots), jnp.float32),
        in_specs=[away] * 6,
        out_specs=whole,
        scratch_shapes=scratch,
        compiler_params=pltpu.CompilerParams(
            collective_id=0, has_side_effects=True, vmem_limit_bytes=56 * 1024 * 1024
        ),
    )(
        features,
        labels[None, :],
        centres,
        destination.reshape(1, own_rows),
        tri_inverse,
        aux_inverse,
    )


def exact_product(dims, vector, block):
    parts = jnp.concatenate(three_parts(vector), axis=0).astype(jnp.bfloat16)
    total = None
    for part in reversed(block):
        product = dot(parts, part.astype(jnp.bfloat16), dims)
        product = product[2 * PAD :] + product[PAD : 2 * PAD] + product[:PAD]
        total = product if total is None else total + product
    return total


def forward_kernel(u_ref, block_ref, o_ref):
    o_ref[...] = exact_product(FLIPPED, u_ref[...], three_parts(block_ref[...]))


def backward_kernel(u_ref, block_ref, o_ref):
    product = exact_product(STRAIGHT, u_ref[...], three_parts(block_ref[...]))

    @pl.when(pl.program_id(0) == 0)
    def _():
        o_ref[...] = product

    @pl.when(pl.program_id(0) > 0)
    def _():
        o_ref[...] += product


STEP = 512

def factor_forward(block, vector):
    rows, cols = block.shape
    return pl.pallas_call(
        forward_kernel,
        grid=(rows // STEP,),
        in_specs=[
            pl.BlockSpec((PAD, cols), lambda i: (0, 0)),
            pl.BlockSpec((STEP, cols), lambda i: (i, 0)),
        ],
        out_specs=pl.BlockSpec((PAD, STEP), lambda i: (0, i)),
        out_shape=jax.ShapeDtypeStruct((PAD, rows), jnp.float32),
    )(vector, block)


def factor_backward(block, vector):
    rows, cols = block.shape
    return pl.pallas_call(
        backward_kernel,
        grid=(rows // STEP,),
        in_specs=[
            pl.BlockSpec((PAD, STEP), lambda i: (0, i)),
            pl.BlockSpec((STEP, cols), lambda i: (i, 0)),
        ],
        out_specs=pl.BlockSpec((PAD, cols), lambda i: (0, 0)),
        out_shape=jax.ShapeDtypeStruct((PAD, cols), jnp.float32),
    )(vector, block)


def square_norms(rows_x):
    return jnp.einsum("nd,nd->n", rows_x, rows_x, preferred_element_type=jnp.float32)


def plane_sum(x):
    return lax.psum(x, "rows")


def joint_sum(kind, nb, nr, block, *operands):
    x = operands[0]
    if kind == "plane":
        out = plane_sum(x)
        lines = jnp.arange(PAD, dtype=jnp.int32)[:, None]
        return out, factor_backward(block, jnp.where(lines < CLASSES, out, 0.0))
    if kind == "turn":
        width = x.shape[1] * nr // nb
        full = lax.all_gather(lax.psum(x, "blk") + operands[1], "rows", axis=1, tiled=True)
        out = lax.dynamic_slice_in_dim(full, lax.axis_index("blk") * width, width, 1)
        return out, factor_backward(block, out)
    if kind == "slice":
        size = x.shape[1] * nb // nr
        full = lax.all_gather(lax.psum(x, "rows"), "blk", axis=1, tiled=True)
        out = lax.dynamic_slice_in_dim(full, lax.axis_index("rows") * size, size, 1)
    else:
        out = operands[1] + operands[2] * lax.psum(x, "blk")
    return out, factor_forward(block, out)


def to_low(values):
    return lax.reduce_precision(values, 8, 7).astype(jnp.bfloat16)


def with_row(vector, scalars):
    return vector + jnp.pad(scalars[None, :], ((PAD - 1, 0), (0, vector.shape[1] - PAD)))


def on_device(nb, nr, features, labels, destination, centres, tri_inverse, aux_inverse):
    own_rows, width = features.shape
    capacity = max(2, 2 * own_rows // nr)
    scale = 2.0 / width
    count_all = float(own_rows * nb * nr)
    b = lax.axis_index("blk")
    class_rows = jnp.arange(PAD, dtype=jnp.int32)[:, None]
    real = class_rows < CLASSES

    tags = jnp.pad(labels.astype(jnp.bfloat16), (0, -own_rows % (16 * width)))
    tags = tags.reshape(-1, width)
    shared = lax.all_gather(jnp.concatenate([features, tags], axis=0), "blk", axis=0)
    rows_x = shared[:, :own_rows].reshape(nb * own_rows, width)
    tags = shared[:, own_rows:].reshape(nb, -1)[:, :own_rows].reshape(nb * own_rows)
    centre_norm = square_norms(centres)
    rows_norm = square_norms(rows_x)
    inner = lax.dot_general(
        rows_x, centres, (((1,), (1,)), ((), ())), preferred_element_type=jnp.float32
    )
    kmat = jnp.exp(-(rows_norm[:, None] + centre_norm[None, :] - 2.0 * inner) * scale).astype(
        jnp.bfloat16
    )
    hits = tags.astype(jnp.float32)[None, :] == class_rows.astype(jnp.float32)
    targets = jnp.where(real, jnp.where(hits, 1.0, -1.0), 0.0).astype(jnp.bfloat16)

    def clean(vector):
        return jnp.where(real, vector, 0.0)

    def onto_rows(low):
        return lax.dot_general(
            low, kmat, (((1,), (1,)), ((), ())), preferred_element_type=jnp.float32
        )

    def images(second):
        high = to_low(second)
        rest = second - high.astype(jnp.float32)
        mid = to_low(rest)
        low = to_low(rest - mid.astype(jnp.float32))
        three = onto_rows(jnp.concatenate([high, mid, low], axis=0))
        both = jnp.concatenate([three[:PAD], three[PAD : 2 * PAD] + three[2 * PAD :]], axis=0)
        both = lax.psum(both, "blk")
        image = to_low(both[:PAD])
        exact = both[:PAD] + both[PAD:]
        curve = jnp.sum(image.astype(jnp.float32) * exact, axis=1) / count_all
        return image, curve

    def ratio(above, below):
        return jnp.where(real, (above / below)[:, None], 0.0)

    def normal(vector):
        return jnp.sum(vector * vector, axis=1)

    start = jnp.dot(targets, kmat, preferred_element_type=jnp.float32) / count_all
    start = joint_sum("plane", nb, nr, tri_inverse, start)[1]
    start = joint_sum("turn", nb, nr, aux_inverse, start, jnp.zeros_like(start))[1]
    zeros = jnp.zeros_like(start)
    rhs, start = joint_sum("pair", nb, nr, aux_inverse, start, zeros, zeros + 1.0)
    first, start = joint_sum("slice", nb, nr, tri_inverse, start)
    joined = plane_sum(with_row(start, normal(rhs)))
    norm_first = joined[PAD - 1, :PAD]
    second = clean(joined)
    image, curve = images(second)
    curve = curve + ridge_weight * normal(first)
    gram = jnp.dot(image, kmat, preferred_element_type=jnp.float32) / count_all
    joined, turned = joint_sum("plane", nb, nr, tri_inverse, with_row(gram, curve))
    step_first = ratio(norm_first, joined[PAD - 1, :PAD])
    turned = joint_sum("turn", nb, nr, aux_inverse, turned, ridge_weight * first)[1]
    residual, start = joint_sum("pair", nb, nr, aux_inverse, turned, rhs, zeros - step_first)
    first_next, start = joint_sum("slice", nb, nr, tri_inverse, start)
    joined = plane_sum(with_row(start, normal(residual)))
    norm_next = joined[PAD - 1, :PAD]
    turn_weight = ratio(norm_next, norm_first)
    first_next = first_next + turn_weight * first
    second_next = clean(joined) + turn_weight * second
    image, curve = images(second_next)
    curve = curve + ridge_weight * normal(first_next)
    curve = lax.psum(jnp.pad(curve[:, None], ((0, 0), (0, 127))), "rows")[:, 0]
    step_next = ratio(norm_next, curve)
    coefficients = step_first * second + step_next * second_next
    scores = lax.psum(onto_rows(to_low(coefficients)), "blk")
    scores = lax.dynamic_slice_in_dim(scores, b * own_rows, own_rows, 1)

    target = destination[:, 0]
    row_ids = jnp.arange(own_rows, dtype=jnp.int32)
    same = (target[:, None] == target[None, :]) & (row_ids[None, :] < row_ids[:, None])
    before = jnp.sum(same.astype(jnp.int32), axis=1)
    slots = nr * capacity
    spread = (
        (target * capacity + before)[:, None] == jnp.arange(slots, dtype=jnp.int32)[None, :]
    ).astype(jnp.float32)
    placed = jnp.dot(scores, spread, precision=highest, preferred_element_type=jnp.float32)
    placed = placed.reshape(PAD, nr, capacity).transpose(1, 0, 2)
    lanes = -capacity % 128
    placed = jnp.pad(placed, ((0, 0), (0, 0), (0, lanes)))
    moved = lax.all_to_all(placed, "rows", split_axis=0, concat_axis=0, tiled=True)
    moved = moved[:, :CLASSES, :capacity]
    return moved.transpose(1, 0, 2).reshape(CLASSES, slots)


def solution(mesh):
    nb, nr = mesh.shape["blk"], mesh.shape["rows"]
    body = fused if (nb, nr) == (PLANES, LINE) else functools.partial(on_device, nb, nr)
    return jax.shard_map(
        body,
        mesh=mesh,
        in_specs=(
            P(("blk", "rows"), None),
            P(("blk", "rows")),
            P(("blk", "rows"), None),
            P("blk", None),
            P("blk", "rows"),
            P("blk", "rows"),
        ),
        out_specs=P(None, ("blk", "rows")),
        check_vma=False,
    )
```

```python
import functools

import jax
import jax.numpy as jnp
from jax import lax
from jax.experimental import pallas as pl
from jax.experimental.pallas import tpu as pltpu
from jax.sharding import PartitionSpec as P

CLASSES = 7
PAD = 8
LANES = 128
MESH = pl.DeviceIdType.MESH
ridge_weight = 0.1
highest = lax.Precision.HIGHEST

PLANES = 2
LINE = 16
HALF = LINE // 2
NEAR = 4
FLIPPED = (((1,), (1,)), ((), ()))
STRAIGHT = (((1,), (0,)), ((), ()))

dma = pltpu.SemaphoreType.DMA


def spot(index, chunk):
    return pl.ds(pl.multiple_of(index * chunk, chunk), chunk)


def dot(left, right, dims):
    return lax.dot_general(left, right, dims, preferred_element_type=jnp.float32)


def stacked(vector):
    high = vector.astype(jnp.bfloat16).astype(jnp.float32)
    return jnp.concatenate([high, vector - high], axis=0).astype(jnp.bfloat16)


def fold(product):
    return product[:PAD] + product[PAD:]


def tree_sum(terms):
    while len(terms) > 1:
        pairs = [terms[i] + terms[i + 1] for i in range(0, len(terms) - 1, 2)]
        terms = pairs + terms[len(pairs) * 2 :]
    return terms[0]


def diagonal(width, first):
    sub = lax.broadcasted_iota(jnp.int32, (PAD, width), 0)
    lane = lax.broadcasted_iota(jnp.int32, (PAD, width), 1)
    return sub + first == lane


def to_lanes(column, width, first=0):
    spread = jnp.where(diagonal(width, first), column, 0.0)
    return jnp.sum(spread, axis=0, keepdims=True)


def to_column(row, first=0):
    spread = jnp.where(diagonal(row.shape[1], first), row, 0.0)
    return jnp.sum(spread, axis=1, keepdims=True)


def three_parts(x):
    high = x.astype(jnp.bfloat16).astype(jnp.float32)
    rest = x - high
    mid = rest.astype(jnp.bfloat16).astype(jnp.float32)
    return high, mid, rest - mid


def with_last(vector, row):
    lines = lax.broadcasted_iota(jnp.int32, vector.shape, 0)
    return jnp.where(lines == PAD - 1, row, vector)


def rows_of(columns, width):
    return tree_sum([to_lanes(column, width, k * PAD) for k, column in enumerate(columns)])


def packed(vector):
    half = vector.shape[1] // 2
    return jnp.concatenate([vector[:, :half], vector[:, half:]], axis=0).astype(jnp.bfloat16)


def unpacked(tile):
    wide = tile.astype(jnp.float32)
    return jnp.concatenate([wide[:PAD], wide[PAD:]], axis=1).astype(jnp.bfloat16)


def ratio(above, below):
    lines = lax.broadcasted_iota(jnp.int32, above.shape, 0)
    return jnp.where(lines < CLASSES, above / below, 0.0)


def row_sum(values):
    return jnp.sum(values, axis=1, keepdims=True)


def fused_kernel(count_all, scale, *refs):
    arrays, out, scratch = refs[:6], refs[6], refs[7:]
    (
        feat, label, cent, dest, stage, tri, aux, km, cn, place, feat_in, tgt, tgt_in,
        rs_out, rs_in, ag, ag_low, w_own, w_in, w_cross, p_own, p_in, r_vec, g_own,
        f_out, f_in, f_vec, c_out, c_in, far_out, far_in, e_own, e_in, e_vec, m_out, m_in,
        load_sem, far_send, line_recv, group_recv, turn_recv, mate_send, mate_recv, ready, one_send, one_recv,
    ) = scratch
    b, r = lax.axis_index("blk"), lax.axis_index("rows")
    z, c = r // NEAR, lax.rem(r, 2)
    mate = r + 1 - 2 * c
    across = 1 - b
    chunk = ag.shape[3]
    own_rows = feat.shape[0]
    cols = tri.shape[2]
    low_plane, low_line = b == 0, r < HALF
    active = jnp.logical_or(low_plane, r >= HALF)
    pending = []

    def settle():
        for action in pending:
            action()
        pending.clear()

    def remote(source, target, send_sem, recv_sem, device):
        return pltpu.make_async_remote_copy(
            src_ref=source, dst_ref=target, send_sem=send_sem, recv_sem=recv_sem,
            device_id=device, device_id_type=MESH,
        )

    def await_arrivals(like, sem):
        remote(like, like, sem, sem, (b, r)).wait_recv()

    def await_sent(like, sem):
        remote(like, like, sem, sem, (b, r)).wait_send()

    def loop(count, body):
        def step(i, carry):
            body(i)
            return carry

        lax.fori_loop(0, count, step, 0)

    def turned_by(i, count):
        return lax.rem(r + i, count)

    def farthest(step):
        inner = jnp.logical_and(z > 0, z < NEAR - 1)
        ahead = jnp.logical_and(inner, step < 2)
        return group(jnp.where(ahead, 2 + step, NEAR - 1 - step))

    def group(j):
        return lax.rem(z + j, 2) + 2 * lax.rem(z // 2 + j // 2, 2)

    barrier = pltpu.get_barrier_semaphore()

    def hello(k):
        pl.semaphore_signal(
            barrier, inc=1, device_id=(b, lax.rem(r + k * NEAR, LINE)), device_id_type=MESH
        )

    def beside(k):
        return (b, z * NEAR + lax.rem(r + k, NEAR))

    pl.semaphore_signal(barrier, inc=1, device_id=(across, r), device_id_type=MESH)
    for k in range(1, NEAR):
        hello(k)
        pl.semaphore_signal(barrier, inc=1, device_id=beside(k), device_id_type=MESH)
    into = (feat, label, cent, dest, stage.at[0], stage.at[1])
    loads = [
        pltpu.make_async_copy(source, target, load_sem.at[i])
        for i, (source, target) in enumerate(zip(arrays, into))
    ]
    for load in loads:
        load.start()
    for load in loads[:4]:
        load.wait()
    loads = loads[4:]

    class_rows = lax.broadcasted_iota(jnp.int32, (PAD, own_rows), 0)
    hits = jnp.where(label[...] == class_rows, 1.0, -1.0)
    tgt[...] = jnp.where(class_rows < CLASSES, hits, 0.0)

    def squares_of_centres(q):
        values = cent[spot(q, chunk), :].astype(jnp.float32)
        values = values * values
        high = values.astype(jnp.bfloat16)
        low = (values - high.astype(jnp.float32)).astype(jnp.bfloat16)
        ones = jnp.ones((PAD, values.shape[1]), jnp.bfloat16)
        return (dot(ones, high, FLIPPED) + dot(ones, low, FLIPPED))[:1] * scale

    def square_norm(source):
        values = source[...].astype(jnp.float32)
        return row_sum(values * values) * scale

    def build(source, norm, norms, half, q):
        inner = dot(source[...], cent[spot(q, chunk), :], FLIPPED)
        power = inner * (2.0 * scale) - norm - norms
        km[q, spot(half, own_rows), :] = jnp.exp(power).astype(jnp.bfloat16)

    own_norm = square_norm(feat)

    def own_half(q):
        for i in range(NEAR):
            norms = squares_of_centres(q * NEAR + i)
            cn[q * NEAR + i] = jnp.broadcast_to(norms, (PAD, chunk))
            build(feat, own_norm, norms, b, q * NEAR + i)

    loop(LINE // NEAR, own_half)
    pl.semaphore_wait(barrier, 2 * NEAR - 1)
    shares = [
        remote(feat, feat_in, one_send.at[0], one_recv.at[0], (across, r)),
        remote(tgt, tgt_in, one_send.at[1], one_recv.at[1], (across, r)),
    ]
    for share in shares:
        share.start()
    for k in range(1, NEAR):
        pl.semaphore_signal(ready, inc=1, device_id=beside(k), device_id_type=MESH)

    def split(index, target):
        loads[index].wait()

        def visit(i):
            piece = spot(i, chunk)
            values = stage[index, piece, :]
            high = values.astype(jnp.bfloat16)
            target[0, piece, :] = high
            target[1, piece, :] = (values - high.astype(jnp.float32)).astype(jnp.bfloat16)

        loop(LINE, visit)

    def find_places():
        to_row = dest[...].astype(jnp.float32)
        sub = lax.broadcasted_iota(jnp.int32, (own_rows, own_rows), 0)
        lane = lax.broadcasted_iota(jnp.int32, (own_rows, own_rows), 1)
        to = row_sum(jnp.where(sub == lane, to_row, 0.0))
        same = jnp.logical_and(to == to_row, lane < sub)
        before = row_sum(jnp.where(same, 1.0, 0.0))
        position = to * LANES + before

        def visit(q):
            lanes = lax.broadcasted_iota(jnp.int32, (own_rows, own_rows), 1) + q * own_rows
            hit = jnp.where(lanes.astype(jnp.float32) == position, 1.0, 0.0)
            place[:, spot(q, own_rows)] = hit.astype(jnp.bfloat16)

        loop(place.shape[1] // own_rows, visit)

    def scatter(phase, term, sources_all, meanwhile=None):
        def copy(q):
            return remote(
                rs_out.at[phase, q], rs_in.at[phase, r],
                far_send.at[0], line_recv.at[0], (b, q),
            )

        def send():
            def visit(step):
                first = farthest(step) * NEAR
                for i in range(NEAR):
                    rs_out[phase, first + i] = term(first + i)
                for i in range(NEAR):
                    q = first + turned_by(i, NEAR)

                    @pl.when(q != r)
                    def _():
                        copy(q).start()

            loop(NEAR, visit)
            rs_in[phase, r] = rs_out[phase, r]

        def left():
            await_sent(rs_out.at[phase, pl.ds(0, LINE - 1)], far_send.at[0])

        def gated(action):
            if sources_all:
                action()
            else:
                pl.when(active)(action)

        gated(send)
        settle()
        if meanwhile is not None:
            meanwhile()

        def arrive(count):
            return lambda: await_arrivals(rs_in.at[phase, pl.ds(0, count)], line_recv.at[0])

        if sources_all:
            arrive(LINE - 1)()
        else:
            pl.when(low_plane)(arrive(LINE - 1))
            pl.when(jnp.logical_and(b == 1, r >= HALF))(arrive(HALF - 1))
            pl.when(jnp.logical_and(b == 1, low_line))(arrive(HALF))
        pending.append(lambda: gated(left))
        upper = tree_sum([rs_in[phase, q] for q in range(HALF, LINE)])
        if sources_all:
            return upper + tree_sum([rs_in[phase, q] for q in range(HALF)])
        ag[phase, r] = upper

        @pl.when(low_plane)
        def _():
            ag[phase, r] += tree_sum([rs_in[phase, q] for q in range(HALF)])

        return ag[phase, r]

    def gather(phase, mine, width, use, rounded=False):
        if rounded:
            held = ag_low.at[phase // 2]
            held[r] = packed(mine)
        else:
            held = ag.at[phase]
            held[r] = mine

        def copy(q):
            return remote(
                held.at[r], held.at[r],
                far_send.at[1], group_recv.at[phase % 2, z], (b, q),
            )

        def send(step):
            first = farthest(step) * NEAR
            for i in range(NEAR):
                q = first + turned_by(i, NEAR)

                @pl.when(q != r)
                def _():
                    copy(q).start()

        loop(NEAR, send)
        settle()
        if phase == 0:
            split(1, aux)

        def visit(j, carry):
            first = group(j) * NEAR
            def arrive(count):
                return lambda: await_arrivals(
                    held.at[pl.ds(first, count)], group_recv.at[phase % 2, group(j)]
                )

            pl.when(j == 0)(arrive(NEAR - 1))
            pl.when(j > 0)(arrive(NEAR))
            for i in range(NEAR):
                low = unpacked(held[first + i]) if rounded else stacked(held[first + i])
                carry = carry + use(first + i, low)
            return carry

        lines = PAD if rounded else 2 * PAD
        total = lax.fori_loop(0, NEAR, visit, jnp.zeros((lines, width), jnp.float32))

        def left():
            await_sent(held.at[pl.ds(0, LINE - 1)], far_send.at[1])

        pending.append(left)
        return total if rounded else fold(total)

    def scalars(phase):
        rows = [ag[phase, q] for q in range(LINE)]
        return tree_sum(rows)[PAD - 1 :]

    def scalars_rounded(phase):
        rows = [ag_low[phase // 2, q].astype(jnp.float32) for q in range(LINE)]
        row = tree_sum(rows)[PAD - 1 : PAD]
        return tree_sum([to_column(row, k * PAD) for k in range(3)])

    def swap(own, landing, index, meanwhile=None):
        copy = remote(own, landing, one_send.at[index], one_recv.at[index], (across, r))
        copy.start()
        settle()
        result = meanwhile() if meanwhile is not None else None
        copy.wait_recv()
        pending.append(copy.wait_send)
        return result

    def factor_rows(factor):
        def use(q, low):
            return dot(low, factor[0, spot(q, chunk), :], STRAIGHT) + dot(
                low, factor[1, spot(q, chunk), :], STRAIGHT
            )

        return use

    def factor_chunk(factor, low):
        def term(q):
            return fold(
                dot(low, factor[0, spot(q, chunk), :], FLIPPED)
                + dot(low, factor[1, spot(q, chunk), :], FLIPPED)
            )

        return term

    def turn(it, product):
        w_own[it] = product
        base = b * HALF

        def inside(q):
            return remote(
                w_own.at[it], w_in.at[it, r - base],
                far_send.at[0], turn_recv.at[r - base], (b, q),
            )

        def outside(q):
            return remote(
                w_own.at[it], w_cross.at[it, r - HALF],
                far_send.at[0], turn_recv.at[r], (1, q),
            )

        def relay(t):
            return remote(
                w_in.at[it, t], w_in.at[it, t], far_send.at[0], turn_recv.at[t], (b, mate)
            )

        def near(act):
            def visit(i):
                q = base + turned_by(i, HALF)

                @pl.when(q != r)
                def _():
                    act(inside(q))

            return lambda: loop(HALF, visit)

        def far(act):
            return lambda: loop(HALF // 2, lambda m: act(inside(HALF + lax.rem(2 * m + r, HALF))))

        def over(act):
            return lambda: loop(HALF, lambda i: act(outside(HALF + turned_by(i, HALF))))

        holder = jnp.logical_and(r >= base, r < base + HALF)
        first_low = jnp.logical_and(low_plane, low_line)
        first_high = jnp.logical_and(low_plane, r >= HALF)

        @pl.when(holder)
        def _():
            w_in[it, r - base] = w_own[it]

        def start(copy):
            copy.start()

        pl.when(first_low)(far(start))
        pl.when(holder)(near(start))
        pl.when(first_high)(over(start))
        settle()

        def arrival(t):
            remote(
                w_own.at[it], w_in.at[it, t], far_send.at[0], turn_recv.at[t], (b, r)
            ).wait_recv()

        @pl.when(first_high)
        def _():
            def visit(m):
                arrival(2 * m + c)
                relay(2 * m + c).start()

            loop(HALF // 2, visit)

        p_own[it] = jnp.zeros(p_own.shape[1:], jnp.float32)

        @pl.when(active)
        def _():
            def ready(t):
                direct = jnp.logical_and(holder, base + t != r)
                relayed = jnp.logical_and(first_high, lax.rem(t, 2) != c)

                @pl.when(jnp.logical_or(direct, relayed))
                def _():
                    arrival(t)

                @pl.when(b == 1)
                def _():
                    remote(
                        w_own.at[it], w_cross.at[it, t],
                        far_send.at[0], turn_recv.at[HALF + t], (b, r),
                    ).wait_recv()
                    w_in[it, t] += w_cross[it, t]

            def visit(i, carry):
                both = [
                    2 * lax.rem(2 * i + k, HALF // 2) + lax.rem(c + 2 * i // (HALF // 2), 2)
                    for k in range(2)
                ]
                for t in both:
                    ready(t)
                for t in both:
                    low = stacked(w_in[it, t])
                    rows = spot(t, cols)
                    carry = carry + dot(low, aux[0, rows, :], STRAIGHT)
                    carry = carry + dot(low, aux[1, rows, :], STRAIGHT)
                return carry

            total = lax.fori_loop(0, HALF // 2, visit, jnp.zeros((2 * PAD, cols), jnp.float32))
            p_own[it] = fold(total)

        def left(count):
            return lambda: await_sent(f_in.at[it, pl.ds(0, count)], far_send.at[0])

        def all_left():
            pl.when(first_low)(left(HALF - 1 + HALF // 2))
            pl.when(first_high)(left(HALF + HALF // 2))
            pl.when(jnp.logical_and(b == 1, r >= HALF))(left(HALF - 1))

        pending.append(all_left)

    def spread(it, vector):
        first_part = (z == 2 * b).astype(jnp.int32)
        low = stacked(vector)
        term = factor_chunk(aux, low)

        def deliver(t):
            here = b * HALF + t

            def copy(plane):
                return remote(
                    f_out.at[it, t], f_in.at[it, r], far_send.at[1], line_recv.at[1], (plane, here)
                )

            @pl.when(here != r)
            def _():
                copy(b).start()

            @pl.when(here == r)
            def _():
                f_in[it, r] = f_out[it, t]

            @pl.when(b == 1)
            def _():
                copy(0).start()

        first_low = jnp.logical_and(low_plane, low_line)
        first_high = jnp.logical_and(low_plane, r >= HALF)
        second = jnp.logical_and(b == 1, r >= HALF)

        @pl.when(first_high)
        def _():
            def mated(step):
                return remote(
                    c_out.at[it, step], c_in.at[it, step],
                    mate_send.at[0], mate_recv.at[step], (b, mate),
                )

            def theirs(step):
                for i in range(2):
                    c_out[it, step, i] = term(2 * (2 * step + i) + 1 - c)
                mated(step).start()

            def ours(step):
                kept = [term(2 * (2 * step + i) + c) for i in range(2)]
                mated(step).wait_recv()
                for i in range(2):
                    far_out[it, 2 * step + i] = kept[i] + c_in[it, step, i]
                for i in range(2):
                    t = 2 * step + turned_by(i, 2)
                    remote(
                        far_out.at[it, t], far_in.at[it, r - HALF],
                        far_send.at[1], line_recv.at[1], (0, t),
                    ).start()

            loop(NEAR, theirs)
            loop(NEAR, ours)

        @pl.when(jnp.logical_or(first_low, second))
        def _():
            def visit(step):
                part = lax.rem(first_part + step // 2, 2)
                first = part * NEAR + 2 * lax.rem(step + r // 2, 2)
                for i in range(2):
                    for side in range(2):
                        columns = slice(side * chunk, (side + 1) * chunk)
                        f_out[it, first + i, :, columns] = term(2 * (first + i) + side)
                for i in range(2):
                    deliver(first + turned_by(i, 2))

            loop(NEAR, visit)

        settle()

        def left(count):
            return lambda: await_sent(f_in.at[it, pl.ds(0, count)], far_send.at[1])

        def arrive(count):
            return lambda: await_arrivals(f_in.at[it, pl.ds(0, count)], line_recv.at[1])

        def all_left():
            pl.when(first_low)(left(HALF - 1))
            pl.when(first_high)(left(HALF // 2))
            pl.when(first_high)(lambda: await_sent(c_out.at[it], mate_send.at[0]))
            pl.when(second)(left(2 * HALF - 1))

        pending.append(all_left)
        pl.when(first_low)(arrive(HALF - 1 + HALF // 2))
        pl.when(first_high)(arrive(HALF))
        pl.when(second)(arrive(HALF - 1))

        @pl.when(r >= HALF)
        def _():
            f_vec[it] = tree_sum([f_in[it, q] for q in range(HALF, LINE)])

        @pl.when(first_low)
        def _():
            near = tree_sum([f_in[it, q] for q in range(HALF)])
            sides = [tree_sum([far_in[it, q] for q in range(side, HALF, 2)]) for side in range(2)]
            f_vec[it] = near + jnp.concatenate(sides, axis=1)

    def onto_centres(low):
        return lambda q: dot(low, km[q], STRAIGHT)

    def onto_rows(q, low):
        return dot(low, km[q], FLIPPED)

    f_vec[0] = jnp.zeros(f_vec.shape[1:], jnp.float32)
    f_vec[1] = jnp.zeros(f_vec.shape[1:], jnp.float32)
    split(0, tri)
    pl.semaphore_wait(ready, NEAR - 1)
    for share in shares:
        share.wait_recv()
        pending.append(share.wait_send)
    mine, other = tgt[...], tgt_in[...]
    targets = jnp.concatenate(
        [jnp.where(low_plane, mine, other), jnp.where(low_plane, other, mine)], axis=1
    ).astype(jnp.bfloat16)
    other_norm = square_norm(feat_in)

    def first_term(q):
        build(feat_in, other_norm, cn[q][:1], across, q)
        return dot(targets, km[q], STRAIGHT)

    start = scatter(0, first_term, True) / count_all
    turned = gather(0, start, cols, factor_rows(tri))
    turn(0, turned)
    swap(p_own.at[0], p_in.at[0], 2)
    residual = p_own[0] + p_in[0]
    r_vec[...] = residual
    spread(0, residual)
    kept = {}

    def square(value):
        return row_sum(value * value)

    def first_wait():
        kept["norm"] = rows_of(three_parts(square(r_vec[...])), chunk)
        find_places()

    mine = scatter(1, factor_chunk(tri, stacked(f_vec[0])), False, first_wait)
    g_own[...] = mine
    image = gather(1, with_last(mine, kept["norm"]), 2 * own_rows, onto_rows, True)
    e_own[0] = image
    norm_first = swap(e_own.at[0], e_in.at[0], 3, lambda: scalars_rounded(1))
    e_vec[...] = e_own[0] + e_in[0]

    def second_wait():
        kept["ridge"] = jnp.where(low_plane, ridge_weight, 0.0) * square(f_vec[0])

    low = e_vec[...].astype(jnp.bfloat16)
    gram = scatter(2, onto_centres(low), True, second_wait) / count_all
    curve = to_lanes(row_sum(gram * g_own[...]) + kept["ridge"], chunk)
    turned = gather(2, with_last(gram, curve), cols, factor_rows(tri))
    holds = jnp.logical_or(b == 1, low_line)
    turn(1, jnp.where(holds, turned + ridge_weight * f_vec[0], turned))
    p_own[1, PAD - 1 :, :chunk] = scalars(2)
    swap(p_own.at[1], p_in.at[1], 2)
    both = p_own[1] + p_in[1]
    step_first = ratio(norm_first, to_column(both[PAD - 1 :]))
    residual = r_vec[...] - step_first * both
    r_vec[...] = residual
    spread(1, residual)

    def third_wait():
        kept["norm"] = rows_of(three_parts(square(r_vec[...])), chunk)
        products = [square(f_vec[1]), row_sum(f_vec[1] * f_vec[0]), square(f_vec[0])]
        kept["ridge"] = rows_of(products, 2 * own_rows)

    mine = scatter(3, factor_chunk(tri, stacked(f_vec[1])), False, third_wait)
    image = gather(3, with_last(mine, kept["norm"]), 2 * own_rows, onto_rows, True)
    e_own[1] = with_last(image, kept["ridge"])
    norm_next = swap(e_own.at[1], e_in.at[1], 3, lambda: scalars_rounded(3))
    weight = ratio(norm_next, norm_first)
    exact = e_own[1] + e_in[1] + weight * e_vec[...]
    low = exact.astype(jnp.bfloat16).astype(jnp.float32)
    row = jnp.where(low_plane, e_own[1, PAD - 1 :, :], e_in[1, PAD - 1 :, :])
    newer, mixed, older = [to_column(row, k * PAD) for k in range(3)]
    ridge = ridge_weight * (newer + 2.0 * weight * mixed + weight * weight * older)
    curve = row_sum(low * exact) / count_all + ridge

    wide = LANES // 4
    settle()
    e_own[1] = exact
    ours = spot(b, own_rows)
    pieces = jnp.concatenate(
        [stacked(e_own[1, :, ours]), stacked(step_first * e_vec[:, ours])], axis=0
    )

    def move(q):
        return remote(
            m_out.at[q], m_in.at[r], far_send.at[0], line_recv.at[0], (b, q)
        )

    curve_row = to_lanes(curve, LANES)
    last = lax.broadcasted_iota(jnp.int32, (PAD, LANES), 0) == PAD - 1

    def put(step):
        first = farthest(step) * NEAR
        both = dot(pieces, place[:, spot(first // NEAR, NEAR * LANES)], STRAIGHT)
        second, early = fold(both[: 2 * PAD]), fold(both[2 * PAD :])
        for i in range(NEAR):
            lanes = slice(i * LANES, (i + 1) * LANES)
            tile = second[:, lanes] + pltpu.roll(early[:, lanes], wide, 1)
            m_out[first + i] = jnp.where(last, curve_row, tile)
        for i in range(NEAR):
            q = first + turned_by(i, NEAR)

            @pl.when(q != r)
            def _():
                move(q).start()

    loop(NEAR, put)
    m_in[r] = m_out[r]
    settle()

    await_arrivals(m_in.at[pl.ds(0, LINE - 1)], line_recv.at[0])
    tiles = [m_in[q] for q in range(LINE)]
    step_next = ratio(norm_next, to_column(tree_sum(tiles)[PAD - 1 :]))
    band = lax.broadcasted_iota(jnp.int32, (PAD, LANES), 1) // wide
    for four in range(LINE // 4):
        parts = [None, None]
        for i in range(4):
            tile = tiles[four * 4 + i]
            for k, value in enumerate((step_next * tile, tile)):
                shift = (i - k) % 4 * wide
                value = pltpu.roll(value, shift, 1) if shift else value
                parts[k] = value if i == 0 else jnp.where(band == i, value, parts[k])
        for k in range(2):
            out[k, :, four * LANES : (four + 1) * LANES] = parts[k]

    await_sent(m_out.at[pl.ds(0, LINE - 1)], far_send.at[0])


def fused(features, labels, destination, centres, tri_inverse, aux_inverse):
    own_rows, width = features.shape
    rows, cols = tri_inverse.shape
    chunk = rows // LINE
    slots = LINE * max(2, 2 * own_rows // LINE)

    def floats(*shape):
        return pltpu.VMEM(shape, jnp.float32)

    def halves(*shape):
        return pltpu.VMEM(shape, jnp.bfloat16)

    scratch = [
        halves(own_rows, width),
        pltpu.VMEM((1, own_rows), jnp.int32),
        halves(rows, width),
        pltpu.VMEM((1, own_rows), jnp.int32),
        floats(2, rows, cols),
        halves(2, rows, cols),
        halves(2, rows, cols),
        halves(LINE, PLANES * own_rows, chunk),
        floats(LINE, PAD, chunk),
        halves(own_rows, LINE * LANES),
        halves(own_rows, width),
        floats(PAD, own_rows),
        floats(PAD, own_rows),
        floats(4, LINE, PAD, chunk),
        floats(4, LINE, PAD, chunk),
        floats(4, LINE, PAD, chunk),
        halves(2, LINE, 2 * PAD, chunk // 2),
        floats(2, PAD, cols),
        floats(2, HALF, PAD, cols),
        floats(2, HALF, PAD, cols),
        floats(2, PAD, cols),
        floats(2, PAD, cols),
        floats(PAD, cols),
        floats(PAD, chunk),
        floats(2, HALF, PAD, cols),
        floats(2, LINE, PAD, cols),
        floats(2, PAD, cols),
        floats(2, NEAR, 2, PAD, chunk),
        floats(2, NEAR, 2, PAD, chunk),
        floats(2, HALF, PAD, chunk),
        floats(2, HALF, PAD, chunk),
        floats(2, PAD, PLANES * own_rows),
        floats(2, PAD, PLANES * own_rows),
        floats(PAD, PLANES * own_rows),
        floats(LINE, PAD, LANES),
        floats(LINE, PAD, LANES),
        dma((6,)),
        dma((2,)),
        dma((2,)),
        dma((2, LINE // NEAR)),
        dma((LINE,)),
        dma((1,)),
        dma((NEAR,)),
        pltpu.SemaphoreType.REGULAR,
        dma((4,)),
        dma((4,)),
    ]
    whole = pl.BlockSpec(memory_space=pltpu.VMEM)
    away = pl.BlockSpec(memory_space=pltpu.MemorySpace.HBM)
    second, early = pl.pallas_call(
        functools.partial(fused_kernel, float(own_rows * PLANES * LINE), 2.0 / width),
        out_shape=jax.ShapeDtypeStruct((2, PAD, slots), jnp.float32),
        in_specs=[away] * 6,
        out_specs=whole,
        scratch_shapes=scratch,
        compiler_params=pltpu.CompilerParams(
            collective_id=0, has_side_effects=True, vmem_limit_bytes=56 * 1024 * 1024
        ),
    )(
        features,
        labels[None, :],
        centres,
        destination.reshape(1, own_rows),
        tri_inverse,
        aux_inverse,
    )
    return early[:CLASSES] + second[:CLASSES]


def exact_product(dims, vector, block):
    parts = jnp.concatenate(three_parts(vector), axis=0).astype(jnp.bfloat16)
    total = None
    for part in reversed(block):
        product = dot(parts, part.astype(jnp.bfloat16), dims)
        product = product[2 * PAD :] + product[PAD : 2 * PAD] + product[:PAD]
        total = product if total is None else total + product
    return total


def forward_kernel(u_ref, block_ref, o_ref):
    o_ref[...] = exact_product(FLIPPED, u_ref[...], three_parts(block_ref[...]))


def backward_kernel(u_ref, block_ref, o_ref):
    product = exact_product(STRAIGHT, u_ref[...], three_parts(block_ref[...]))

    @pl.when(pl.program_id(0) == 0)
    def _():
        o_ref[...] = product

    @pl.when(pl.program_id(0) > 0)
    def _():
        o_ref[...] += product


STEP = 512

def factor_forward(block, vector):
    rows, cols = block.shape
    return pl.pallas_call(
        forward_kernel,
        grid=(rows // STEP,),
        in_specs=[
            pl.BlockSpec((PAD, cols), lambda i: (0, 0)),
            pl.BlockSpec((STEP, cols), lambda i: (i, 0)),
        ],
        out_specs=pl.BlockSpec((PAD, STEP), lambda i: (0, i)),
        out_shape=jax.ShapeDtypeStruct((PAD, rows), jnp.float32),
    )(vector, block)


def factor_backward(block, vector):
    rows, cols = block.shape
    return pl.pallas_call(
        backward_kernel,
        grid=(rows // STEP,),
        in_specs=[
            pl.BlockSpec((PAD, STEP), lambda i: (0, i)),
            pl.BlockSpec((STEP, cols), lambda i: (i, 0)),
        ],
        out_specs=pl.BlockSpec((PAD, cols), lambda i: (0, 0)),
        out_shape=jax.ShapeDtypeStruct((PAD, cols), jnp.float32),
    )(vector, block)


def square_norms(rows_x):
    return jnp.einsum("nd,nd->n", rows_x, rows_x, preferred_element_type=jnp.float32)


def plane_sum(x):
    return lax.psum(x, "rows")


def joint_sum(kind, nb, nr, block, *operands):
    x = operands[0]
    if kind == "plane":
        out = plane_sum(x)
        lines = jnp.arange(PAD, dtype=jnp.int32)[:, None]
        return out, factor_backward(block, jnp.where(lines < CLASSES, out, 0.0))
    if kind == "turn":
        width = x.shape[1] * nr // nb
        full = lax.all_gather(lax.psum(x, "blk") + operands[1], "rows", axis=1, tiled=True)
        out = lax.dynamic_slice_in_dim(full, lax.axis_index("blk") * width, width, 1)
        return out, factor_backward(block, out)
    if kind == "slice":
        size = x.shape[1] * nb // nr
        full = lax.all_gather(lax.psum(x, "rows"), "blk", axis=1, tiled=True)
        out = lax.dynamic_slice_in_dim(full, lax.axis_index("rows") * size, size, 1)
    else:
        out = operands[1] + operands[2] * lax.psum(x, "blk")
    return out, factor_forward(block, out)


def to_low(values):
    return lax.reduce_precision(values, 8, 7).astype(jnp.bfloat16)


def with_row(vector, scalars):
    return vector + jnp.pad(scalars[None, :], ((PAD - 1, 0), (0, vector.shape[1] - PAD)))


def on_device(nb, nr, features, labels, destination, centres, tri_inverse, aux_inverse):
    own_rows, width = features.shape
    capacity = max(2, 2 * own_rows // nr)
    scale = 2.0 / width
    count_all = float(own_rows * nb * nr)
    b = lax.axis_index("blk")
    class_rows = jnp.arange(PAD, dtype=jnp.int32)[:, None]
    real = class_rows < CLASSES

    tags = jnp.pad(labels.astype(jnp.bfloat16), (0, -own_rows % (16 * width)))
    tags = tags.reshape(-1, width)
    shared = lax.all_gather(jnp.concatenate([features, tags], axis=0), "blk", axis=0)
    rows_x = shared[:, :own_rows].reshape(nb * own_rows, width)
    tags = shared[:, own_rows:].reshape(nb, -1)[:, :own_rows].reshape(nb * own_rows)
    centre_norm = square_norms(centres)
    rows_norm = square_norms(rows_x)
    inner = lax.dot_general(
        rows_x, centres, (((1,), (1,)), ((), ())), preferred_element_type=jnp.float32
    )
    kmat = jnp.exp(-(rows_norm[:, None] + centre_norm[None, :] - 2.0 * inner) * scale).astype(
        jnp.bfloat16
    )
    hits = tags.astype(jnp.float32)[None, :] == class_rows.astype(jnp.float32)
    targets = jnp.where(real, jnp.where(hits, 1.0, -1.0), 0.0).astype(jnp.bfloat16)

    def clean(vector):
        return jnp.where(real, vector, 0.0)

    def onto_rows(low):
        return lax.dot_general(
            low, kmat, (((1,), (1,)), ((), ())), preferred_element_type=jnp.float32
        )

    def images(second):
        high = to_low(second)
        rest = second - high.astype(jnp.float32)
        mid = to_low(rest)
        low = to_low(rest - mid.astype(jnp.float32))
        three = onto_rows(jnp.concatenate([high, mid, low], axis=0))
        both = jnp.concatenate([three[:PAD], three[PAD : 2 * PAD] + three[2 * PAD :]], axis=0)
        both = lax.psum(both, "blk")
        image = to_low(both[:PAD])
        exact = both[:PAD] + both[PAD:]
        curve = jnp.sum(image.astype(jnp.float32) * exact, axis=1) / count_all
        return image, curve

    def ratio(above, below):
        return jnp.where(real, (above / below)[:, None], 0.0)

    def normal(vector):
        return jnp.sum(vector * vector, axis=1)

    start = jnp.dot(targets, kmat, preferred_element_type=jnp.float32) / count_all
    start = joint_sum("plane", nb, nr, tri_inverse, start)[1]
    start = joint_sum("turn", nb, nr, aux_inverse, start, jnp.zeros_like(start))[1]
    zeros = jnp.zeros_like(start)
    rhs, start = joint_sum("pair", nb, nr, aux_inverse, start, zeros, zeros + 1.0)
    first, start = joint_sum("slice", nb, nr, tri_inverse, start)
    joined = plane_sum(with_row(start, normal(rhs)))
    norm_first = joined[PAD - 1, :PAD]
    second = clean(joined)
    image, curve = images(second)
    curve = curve + ridge_weight * normal(first)
    gram = jnp.dot(image, kmat, preferred_element_type=jnp.float32) / count_all
    joined, turned = joint_sum("plane", nb, nr, tri_inverse, with_row(gram, curve))
    step_first = ratio(norm_first, joined[PAD - 1, :PAD])
    turned = joint_sum("turn", nb, nr, aux_inverse, turned, ridge_weight * first)[1]
    residual, start = joint_sum("pair", nb, nr, aux_inverse, turned, rhs, zeros - step_first)
    first_next, start = joint_sum("slice", nb, nr, tri_inverse, start)
    joined = plane_sum(with_row(start, normal(residual)))
    norm_next = joined[PAD - 1, :PAD]
    turn_weight = ratio(norm_next, norm_first)
    first_next = first_next + turn_weight * first
    second_next = clean(joined) + turn_weight * second
    image, curve = images(second_next)
    curve = curve + ridge_weight * normal(first_next)
    curve = lax.psum(jnp.pad(curve[:, None], ((0, 0), (0, 127))), "rows")[:, 0]
    step_next = ratio(norm_next, curve)
    coefficients = step_first * second + step_next * second_next
    scores = lax.psum(onto_rows(to_low(coefficients)), "blk")
    scores = lax.dynamic_slice_in_dim(scores, b * own_rows, own_rows, 1)

    target = destination[:, 0]
    row_ids = jnp.arange(own_rows, dtype=jnp.int32)
    same = (target[:, None] == target[None, :]) & (row_ids[None, :] < row_ids[:, None])
    before = jnp.sum(same.astype(jnp.int32), axis=1)
    slots = nr * capacity
    spread = (
        (target * capacity + before)[:, None] == jnp.arange(slots, dtype=jnp.int32)[None, :]
    ).astype(jnp.float32)
    placed = jnp.dot(scores, spread, precision=highest, preferred_element_type=jnp.float32)
    placed = placed.reshape(PAD, nr, capacity).transpose(1, 0, 2)
    lanes = -capacity % 128
    placed = jnp.pad(placed, ((0, 0), (0, 0), (0, lanes)))
    moved = lax.all_to_all(placed, "rows", split_axis=0, concat_axis=0, tiled=True)
    moved = moved[:, :CLASSES, :capacity]
    return moved.transpose(1, 0, 2).reshape(CLASSES, slots)


def solution(mesh):
    nb, nr = mesh.shape["blk"], mesh.shape["rows"]
    body = fused if (nb, nr) == (PLANES, LINE) else functools.partial(on_device, nb, nr)
    return jax.shard_map(
        body,
        mesh=mesh,
        in_specs=(
            P(("blk", "rows"), None),
            P(("blk", "rows")),
            P(("blk", "rows"), None),
            P("blk", None),
            P("blk", "rows"),
            P("blk", "rows"),
        ),
        out_specs=P(None, ("blk", "rows")),
        check_vma=False,
    )
```

```python
import functools

import jax
import jax.numpy as jnp
from jax import lax
from jax.experimental import pallas as pl
from jax.experimental.pallas import tpu as pltpu
from jax.sharding import PartitionSpec as P

CLASSES = 7
PAD = 8
LANES = 128
MESH = pl.DeviceIdType.MESH
ridge_weight = 0.1
highest = lax.Precision.HIGHEST

PLANES = 2
LINE = 16
HALF = LINE // 2
NEAR = 4
FLIPPED = (((1,), (1,)), ((), ()))
STRAIGHT = (((1,), (0,)), ((), ()))

dma = pltpu.SemaphoreType.DMA


def spot(index, chunk):
    return pl.ds(pl.multiple_of(index * chunk, chunk), chunk)


def dot(left, right, dims):
    return lax.dot_general(left, right, dims, preferred_element_type=jnp.float32)


def stacked(vector):
    high = vector.astype(jnp.bfloat16).astype(jnp.float32)
    return jnp.concatenate([high, vector - high], axis=0).astype(jnp.bfloat16)


def fold(product):
    return product[:PAD] + product[PAD:]


def tree_sum(terms):
    while len(terms) > 1:
        pairs = [terms[i] + terms[i + 1] for i in range(0, len(terms) - 1, 2)]
        terms = pairs + terms[len(pairs) * 2 :]
    return terms[0]


def diagonal(width, first):
    sub = lax.broadcasted_iota(jnp.int32, (PAD, width), 0)
    lane = lax.broadcasted_iota(jnp.int32, (PAD, width), 1)
    return sub + first == lane


def to_lanes(column, width, first=0):
    spread = jnp.where(diagonal(width, first), column, 0.0)
    return jnp.sum(spread, axis=0, keepdims=True)


def to_column(row, first=0):
    spread = jnp.where(diagonal(row.shape[1], first), row, 0.0)
    return jnp.sum(spread, axis=1, keepdims=True)


def three_parts(x):
    high = x.astype(jnp.bfloat16).astype(jnp.float32)
    rest = x - high
    mid = rest.astype(jnp.bfloat16).astype(jnp.float32)
    return high, mid, rest - mid


def with_last(vector, row):
    lines = lax.broadcasted_iota(jnp.int32, vector.shape, 0)
    return jnp.where(lines == PAD - 1, row, vector)


def rows_of(columns, width):
    return tree_sum([to_lanes(column, width, k * PAD) for k, column in enumerate(columns)])


def packed(vector):
    half = vector.shape[1] // 2
    return jnp.concatenate([vector[:, :half], vector[:, half:]], axis=0).astype(jnp.bfloat16)


def unpacked(tile):
    wide = tile.astype(jnp.float32)
    return jnp.concatenate([wide[:PAD], wide[PAD:]], axis=1).astype(jnp.bfloat16)


def ratio(above, below):
    lines = lax.broadcasted_iota(jnp.int32, above.shape, 0)
    return jnp.where(lines < CLASSES, above / below, 0.0)


def row_sum(values):
    return jnp.sum(values, axis=1, keepdims=True)


def fused_kernel(count_all, scale, *refs):
    arrays, out, scratch = refs[:6], refs[6], refs[7:]
    (
        feat, label, cent, dest, stage, tri, aux, km, cn, place, feat_in, tgt, tgt_in,
        rs_out, rs_in, ag, ag_low, w_own, w_in, w_cross, p_own, p_in, r_vec, g_own,
        f_out, f_in, f_vec, c_out, c_in, far_out, far_in, e_own, e_in, e_vec, m_out, m_in,
        load_sem, far_send, line_recv, group_recv, turn_recv, mate_send, mate_recv, ready, one_send, one_recv,
    ) = scratch
    b, r = lax.axis_index("blk"), lax.axis_index("rows")
    z, c = r // NEAR, lax.rem(r, 2)
    mate = r + 1 - 2 * c
    across = 1 - b
    chunk = ag.shape[3]
    own_rows = feat.shape[0]
    cols = tri.shape[2]
    low_plane, low_line = b == 0, r < HALF
    active = jnp.logical_or(low_plane, r >= HALF)
    pending = []

    def settle():
        for action in pending:
            action()
        pending.clear()

    def remote(source, target, send_sem, recv_sem, device):
        return pltpu.make_async_remote_copy(
            src_ref=source, dst_ref=target, send_sem=send_sem, recv_sem=recv_sem,
            device_id=device, device_id_type=MESH,
        )

    def await_arrivals(like, sem):
        remote(like, like, sem, sem, (b, r)).wait_recv()

    def await_sent(like, sem):
        remote(like, like, sem, sem, (b, r)).wait_send()

    def loop(count, body):
        def step(i, carry):
            body(i)
            return carry

        lax.fori_loop(0, count, step, 0)

    def turned_by(i, count):
        return lax.rem(r + i, count)

    def farthest(step):
        inner = jnp.logical_and(z > 0, z < NEAR - 1)
        ahead = jnp.logical_and(inner, step < 2)
        return group(jnp.where(ahead, 2 + step, NEAR - 1 - step))

    def group(j):
        return lax.rem(z + j, 2) + 2 * lax.rem(z // 2 + j // 2, 2)

    barrier = pltpu.get_barrier_semaphore()

    def hello(k):
        pl.semaphore_signal(
            barrier, inc=1, device_id=(b, lax.rem(r + k * NEAR, LINE)), device_id_type=MESH
        )

    def beside(k):
        return (b, z * NEAR + lax.rem(r + k, NEAR))

    pl.semaphore_signal(barrier, inc=1, device_id=(across, r), device_id_type=MESH)
    for k in range(1, NEAR):
        hello(k)
        pl.semaphore_signal(barrier, inc=1, device_id=beside(k), device_id_type=MESH)
    into = (feat, label, cent, dest, stage.at[0], stage.at[1])
    loads = [
        pltpu.make_async_copy(source, target, load_sem.at[i])
        for i, (source, target) in enumerate(zip(arrays, into))
    ]
    for load in loads:
        load.start()
    for load in loads[:4]:
        load.wait()
    loads = loads[4:]

    class_rows = lax.broadcasted_iota(jnp.int32, (PAD, own_rows), 0)
    hits = jnp.where(label[...] == class_rows, 1.0, -1.0)
    tgt[...] = jnp.where(class_rows < CLASSES, hits, 0.0)

    def squares_of_centres(q):
        values = cent[spot(q, chunk), :].astype(jnp.float32)
        values = values * values
        high = values.astype(jnp.bfloat16)
        low = (values - high.astype(jnp.float32)).astype(jnp.bfloat16)
        ones = jnp.ones((PAD, values.shape[1]), jnp.bfloat16)
        return (dot(ones, high, FLIPPED) + dot(ones, low, FLIPPED))[:1] * scale

    def square_norm(source):
        values = source[...].astype(jnp.float32)
        return row_sum(values * values) * scale

    def build(source, norm, norms, half, q):
        inner = dot(source[...], cent[spot(q, chunk), :], FLIPPED)
        power = inner * (2.0 * scale) - norm - norms
        km[q, spot(half, own_rows), :] = jnp.exp(power).astype(jnp.bfloat16)

    own_norm = square_norm(feat)

    def own_half(q):
        for i in range(NEAR):
            norms = squares_of_centres(q * NEAR + i)
            cn[q * NEAR + i] = jnp.broadcast_to(norms, (PAD, chunk))
            build(feat, own_norm, norms, b, q * NEAR + i)

    loop(LINE // NEAR, own_half)
    pl.semaphore_wait(barrier, 2 * NEAR - 1)
    shares = [
        remote(feat, feat_in, one_send.at[0], one_recv.at[0], (across, r)),
        remote(tgt, tgt_in, one_send.at[1], one_recv.at[1], (across, r)),
    ]
    for share in shares:
        share.start()
    for k in range(1, NEAR):
        pl.semaphore_signal(ready, inc=1, device_id=beside(k), device_id_type=MESH)

    def split(index, target):
        loads[index].wait()

        def visit(i):
            piece = spot(i, chunk)
            values = stage[index, piece, :]
            high = values.astype(jnp.bfloat16)
            target[0, piece, :] = high
            target[1, piece, :] = (values - high.astype(jnp.float32)).astype(jnp.bfloat16)

        loop(LINE, visit)

    def find_places():
        to_row = dest[...].astype(jnp.float32)
        sub = lax.broadcasted_iota(jnp.int32, (own_rows, own_rows), 0)
        lane = lax.broadcasted_iota(jnp.int32, (own_rows, own_rows), 1)
        to = row_sum(jnp.where(sub == lane, to_row, 0.0))
        same = jnp.logical_and(to == to_row, lane < sub)
        before = row_sum(jnp.where(same, 1.0, 0.0))
        position = to * LANES + before

        def visit(q):
            lanes = lax.broadcasted_iota(jnp.int32, (own_rows, own_rows), 1) + q * own_rows
            hit = jnp.where(lanes.astype(jnp.float32) == position, 1.0, 0.0)
            place[:, spot(q, own_rows)] = hit.astype(jnp.bfloat16)

        loop(place.shape[1] // own_rows, visit)

    def scatter(phase, term, sources_all, meanwhile=None):
        def copy(q):
            return remote(
                rs_out.at[phase, q], rs_in.at[phase, r],
                far_send.at[0], line_recv.at[0], (b, q),
            )

        def send():
            def visit(step):
                first = farthest(step) * NEAR
                for i in range(NEAR):
                    rs_out[phase, first + i] = term(first + i)
                for i in range(NEAR):
                    q = first + turned_by(i, NEAR)

                    @pl.when(q != r)
                    def _():
                        copy(q).start()

            loop(NEAR, visit)
            rs_in[phase, r] = rs_out[phase, r]

        def left():
            await_sent(rs_out.at[phase, pl.ds(0, LINE - 1)], far_send.at[0])

        def gated(action):
            if sources_all:
                action()
            else:
                pl.when(active)(action)

        gated(send)
        settle()
        if meanwhile is not None:
            meanwhile()

        def arrive(count):
            return lambda: await_arrivals(rs_in.at[phase, pl.ds(0, count)], line_recv.at[0])

        if sources_all:
            arrive(LINE - 1)()
        else:
            pl.when(low_plane)(arrive(LINE - 1))
            pl.when(jnp.logical_and(b == 1, r >= HALF))(arrive(HALF - 1))
            pl.when(jnp.logical_and(b == 1, low_line))(arrive(HALF))
        pending.append(lambda: gated(left))
        upper = tree_sum([rs_in[phase, q] for q in range(HALF, LINE)])
        if sources_all:
            return upper + tree_sum([rs_in[phase, q] for q in range(HALF)])
        ag[phase, r] = upper

        @pl.when(low_plane)
        def _():
            ag[phase, r] += tree_sum([rs_in[phase, q] for q in range(HALF)])

        return ag[phase, r]

    def gather(phase, mine, width, use, rounded=False):
        if rounded:
            held = ag_low.at[phase // 2]
            held[r] = packed(mine)
        else:
            held = ag.at[phase]
            held[r] = mine

        def copy(q):
            return remote(
                held.at[r], held.at[r],
                far_send.at[1], group_recv.at[phase % 2, z], (b, q),
            )

        def send(step):
            first = farthest(step) * NEAR
            for i in range(NEAR):
                q = first + turned_by(i, NEAR)

                @pl.when(q != r)
                def _():
                    copy(q).start()

        loop(NEAR, send)
        settle()
        if phase == 0:
            split(1, aux)

        def visit(j, carry):
            first = group(j) * NEAR
            def arrive(count):
                return lambda: await_arrivals(
                    held.at[pl.ds(first, count)], group_recv.at[phase % 2, group(j)]
                )

            pl.when(j == 0)(arrive(NEAR - 1))
            pl.when(j > 0)(arrive(NEAR))
            for i in range(NEAR):
                low = unpacked(held[first + i]) if rounded else stacked(held[first + i])
                carry = carry + use(first + i, low)
            return carry

        lines = PAD if rounded else 2 * PAD
        total = lax.fori_loop(0, NEAR, visit, jnp.zeros((lines, width), jnp.float32))

        def left():
            await_sent(held.at[pl.ds(0, LINE - 1)], far_send.at[1])

        pending.append(left)
        return total if rounded else fold(total)

    def scalars(phase):
        rows = [ag[phase, q] for q in range(LINE)]
        return tree_sum(rows)[PAD - 1 :]

    def scalars_rounded(phase):
        rows = [ag_low[phase // 2, q].astype(jnp.float32) for q in range(LINE)]
        row = tree_sum(rows)[PAD - 1 : PAD]
        return tree_sum([to_column(row, k * PAD) for k in range(3)])

    def swap(own, landing, index, meanwhile=None):
        copy = remote(own, landing, one_send.at[index], one_recv.at[index], (across, r))
        copy.start()
        settle()
        result = meanwhile() if meanwhile is not None else None
        copy.wait_recv()
        pending.append(copy.wait_send)
        return result

    def factor_rows(factor):
        def use(q, low):
            return dot(low, factor[0, spot(q, chunk), :], STRAIGHT) + dot(
                low, factor[1, spot(q, chunk), :], STRAIGHT
            )

        return use

    def factor_chunk(factor, low):
        def term(q):
            return fold(
                dot(low, factor[0, spot(q, chunk), :], FLIPPED)
                + dot(low, factor[1, spot(q, chunk), :], FLIPPED)
            )

        return term

    def turn(it, product):
        w_own[it] = product
        base = b * HALF

        def inside(q):
            return remote(
                w_own.at[it], w_in.at[it, r - base],
                far_send.at[0], turn_recv.at[r - base], (b, q),
            )

        def outside(q):
            return remote(
                w_own.at[it], w_cross.at[it, r - HALF],
                far_send.at[0], turn_recv.at[r], (1, q),
            )

        def relay(t):
            return remote(
                w_in.at[it, t], w_in.at[it, t], far_send.at[0], turn_recv.at[t], (b, mate)
            )

        def near(act):
            def visit(i):
                q = base + turned_by(i, HALF)

                @pl.when(q != r)
                def _():
                    act(inside(q))

            return lambda: loop(HALF, visit)

        def far(act):
            return lambda: loop(HALF // 2, lambda m: act(inside(HALF + lax.rem(2 * m + r, HALF))))

        def over(act):
            return lambda: loop(HALF, lambda i: act(outside(HALF + turned_by(i, HALF))))

        holder = jnp.logical_and(r >= base, r < base + HALF)
        first_low = jnp.logical_and(low_plane, low_line)
        first_high = jnp.logical_and(low_plane, r >= HALF)

        @pl.when(holder)
        def _():
            w_in[it, r - base] = w_own[it]

        def start(copy):
            copy.start()

        pl.when(first_low)(far(start))
        pl.when(holder)(near(start))
        pl.when(first_high)(over(start))
        settle()

        def arrival(t):
            remote(
                w_own.at[it], w_in.at[it, t], far_send.at[0], turn_recv.at[t], (b, r)
            ).wait_recv()

        @pl.when(first_high)
        def _():
            def visit(m):
                arrival(2 * m + c)
                relay(2 * m + c).start()

            loop(HALF // 2, visit)

        p_own[it] = jnp.zeros(p_own.shape[1:], jnp.float32)

        @pl.when(active)
        def _():
            def ready(t):
                direct = jnp.logical_and(holder, base + t != r)
                relayed = jnp.logical_and(first_high, lax.rem(t, 2) != c)

                @pl.when(jnp.logical_or(direct, relayed))
                def _():
                    arrival(t)

                @pl.when(b == 1)
                def _():
                    remote(
                        w_own.at[it], w_cross.at[it, t],
                        far_send.at[0], turn_recv.at[HALF + t], (b, r),
                    ).wait_recv()
                    w_in[it, t] += w_cross[it, t]

            def visit(i, carry):
                both = [
                    2 * lax.rem(2 * i + k, HALF // 2) + lax.rem(c + 2 * i // (HALF // 2), 2)
                    for k in range(2)
                ]
                for t in both:
                    ready(t)
                for t in both:
                    low = stacked(w_in[it, t])
                    rows = spot(t, cols)
                    carry = carry + dot(low, aux[0, rows, :], STRAIGHT)
                    carry = carry + dot(low, aux[1, rows, :], STRAIGHT)
                return carry

            total = lax.fori_loop(0, HALF // 2, visit, jnp.zeros((2 * PAD, cols), jnp.float32))
            p_own[it] = fold(total)

        def left(count):
            return lambda: await_sent(f_in.at[it, pl.ds(0, count)], far_send.at[0])

        def all_left():
            pl.when(first_low)(left(HALF - 1 + HALF // 2))
            pl.when(first_high)(left(HALF + HALF // 2))
            pl.when(jnp.logical_and(b == 1, r >= HALF))(left(HALF - 1))

        pending.append(all_left)

    def spread(it, vector):
        first_part = (z == 2 * b).astype(jnp.int32)
        low = stacked(vector)
        term = factor_chunk(aux, low)

        def deliver(t):
            here = b * HALF + t

            def copy(plane):
                return remote(
                    f_out.at[it, t], f_in.at[it, r], far_send.at[1], line_recv.at[1], (plane, here)
                )

            @pl.when(here != r)
            def _():
                copy(b).start()

            @pl.when(here == r)
            def _():
                f_in[it, r] = f_out[it, t]

            @pl.when(b == 1)
            def _():
                copy(0).start()

        first_low = jnp.logical_and(low_plane, low_line)
        first_high = jnp.logical_and(low_plane, r >= HALF)
        second = jnp.logical_and(b == 1, r >= HALF)

        @pl.when(first_high)
        def _():
            def mated(step):
                return remote(
                    c_out.at[it, step], c_in.at[it, step],
                    mate_send.at[0], mate_recv.at[step], (b, mate),
                )

            def theirs(step):
                for i in range(2):
                    c_out[it, step, i] = term(2 * (2 * step + i) + 1 - c)
                mated(step).start()

            def ours(step):
                kept = [term(2 * (2 * step + i) + c) for i in range(2)]
                mated(step).wait_recv()
                for i in range(2):
                    far_out[it, 2 * step + i] = kept[i] + c_in[it, step, i]
                for i in range(2):
                    t = 2 * step + turned_by(i, 2)
                    remote(
                        far_out.at[it, t], far_in.at[it, r - HALF],
                        far_send.at[1], line_recv.at[1], (0, t),
                    ).start()

            for step in range(NEAR):
                theirs(step)
            for step in range(NEAR):
                ours(step)

        @pl.when(jnp.logical_or(first_low, second))
        def _():
            def visit(step):
                part = lax.rem(first_part + step // 2, 2)
                first = part * NEAR + 2 * lax.rem(step + r // 2, 2)
                for i in range(2):
                    for side in range(2):
                        columns = slice(side * chunk, (side + 1) * chunk)
                        f_out[it, first + i, :, columns] = term(2 * (first + i) + side)
                for i in range(2):
                    deliver(first + turned_by(i, 2))

            loop(NEAR, visit)

        settle()

        def left(count):
            return lambda: await_sent(f_in.at[it, pl.ds(0, count)], far_send.at[1])

        def arrive(count):
            return lambda: await_arrivals(f_in.at[it, pl.ds(0, count)], line_recv.at[1])

        def all_left():
            pl.when(first_low)(left(HALF - 1))
            pl.when(first_high)(left(HALF // 2))
            pl.when(first_high)(lambda: await_sent(c_out.at[it], mate_send.at[0]))
            pl.when(second)(left(2 * HALF - 1))

        pending.append(all_left)
        pl.when(first_low)(arrive(HALF - 1 + HALF // 2))
        pl.when(first_high)(arrive(HALF))
        pl.when(second)(arrive(HALF - 1))

        @pl.when(r >= HALF)
        def _():
            f_vec[it] = tree_sum([f_in[it, q] for q in range(HALF, LINE)])

        @pl.when(first_low)
        def _():
            near = tree_sum([f_in[it, q] for q in range(HALF)])
            sides = [tree_sum([far_in[it, q] for q in range(side, HALF, 2)]) for side in range(2)]
            f_vec[it] = near + jnp.concatenate(sides, axis=1)

    def onto_centres(low):
        return lambda q: dot(low, km[q], STRAIGHT)

    def onto_rows(q, low):
        return dot(low, km[q], FLIPPED)

    f_vec[0] = jnp.zeros(f_vec.shape[1:], jnp.float32)
    f_vec[1] = jnp.zeros(f_vec.shape[1:], jnp.float32)
    split(0, tri)
    pl.semaphore_wait(ready, NEAR - 1)
    for share in shares:
        share.wait_recv()
        pending.append(share.wait_send)
    mine, other = tgt[...], tgt_in[...]
    targets = jnp.concatenate(
        [jnp.where(low_plane, mine, other), jnp.where(low_plane, other, mine)], axis=1
    ).astype(jnp.bfloat16)
    other_norm = square_norm(feat_in)

    def first_term(q):
        build(feat_in, other_norm, cn[q][:1], across, q)
        return dot(targets, km[q], STRAIGHT)

    start = scatter(0, first_term, True) / count_all
    turned = gather(0, start, cols, factor_rows(tri))
    turn(0, turned)
    swap(p_own.at[0], p_in.at[0], 2)
    residual = p_own[0] + p_in[0]
    r_vec[...] = residual
    spread(0, residual)
    kept = {}

    def square(value):
        return row_sum(value * value)

    def first_wait():
        kept["norm"] = rows_of(three_parts(square(r_vec[...])), chunk)
        find_places()

    mine = scatter(1, factor_chunk(tri, stacked(f_vec[0])), False, first_wait)
    g_own[...] = mine
    image = gather(1, with_last(mine, kept["norm"]), 2 * own_rows, onto_rows, True)
    e_own[0] = image
    norm_first = swap(e_own.at[0], e_in.at[0], 3, lambda: scalars_rounded(1))
    e_vec[...] = e_own[0] + e_in[0]

    def second_wait():
        kept["ridge"] = jnp.where(low_plane, ridge_weight, 0.0) * square(f_vec[0])

    low = e_vec[...].astype(jnp.bfloat16)
    gram = scatter(2, onto_centres(low), True, second_wait) / count_all
    curve = to_lanes(row_sum(gram * g_own[...]) + kept["ridge"], chunk)
    turned = gather(2, with_last(gram, curve), cols, factor_rows(tri))
    holds = jnp.logical_or(b == 1, low_line)
    turn(1, jnp.where(holds, turned + ridge_weight * f_vec[0], turned))
    p_own[1, PAD - 1 :, :chunk] = scalars(2)
    swap(p_own.at[1], p_in.at[1], 2)
    both = p_own[1] + p_in[1]
    step_first = ratio(norm_first, to_column(both[PAD - 1 :]))
    residual = r_vec[...] - step_first * both
    r_vec[...] = residual
    spread(1, residual)

    def third_wait():
        kept["norm"] = rows_of(three_parts(square(r_vec[...])), chunk)
        products = [square(f_vec[1]), row_sum(f_vec[1] * f_vec[0]), square(f_vec[0])]
        kept["ridge"] = rows_of(products, 2 * own_rows)

    mine = scatter(3, factor_chunk(tri, stacked(f_vec[1])), False, third_wait)
    image = gather(3, with_last(mine, kept["norm"]), 2 * own_rows, onto_rows, True)
    e_own[1] = with_last(image, kept["ridge"])
    norm_next = swap(e_own.at[1], e_in.at[1], 3, lambda: scalars_rounded(3))
    weight = ratio(norm_next, norm_first)
    exact = e_own[1] + e_in[1] + weight * e_vec[...]
    low = exact.astype(jnp.bfloat16).astype(jnp.float32)
    row = jnp.where(low_plane, e_own[1, PAD - 1 :, :], e_in[1, PAD - 1 :, :])
    newer, mixed, older = [to_column(row, k * PAD) for k in range(3)]
    ridge = ridge_weight * (newer + 2.0 * weight * mixed + weight * weight * older)
    curve = row_sum(low * exact) / count_all + ridge

    wide = LANES // 4
    settle()
    e_own[1] = exact
    ours = spot(b, own_rows)
    pieces = jnp.concatenate(
        [stacked(e_own[1, :, ours]), stacked(step_first * e_vec[:, ours])], axis=0
    )

    def move(q):
        return remote(
            m_out.at[q], m_in.at[r], far_send.at[0], line_recv.at[0], (b, q)
        )

    curve_row = to_lanes(curve, LANES)
    last = lax.broadcasted_iota(jnp.int32, (PAD, LANES), 0) == PAD - 1

    def put(step):
        first = farthest(step) * NEAR
        both = dot(pieces, place[:, spot(first // NEAR, NEAR * LANES)], STRAIGHT)
        second, early = fold(both[: 2 * PAD]), fold(both[2 * PAD :])
        for i in range(NEAR):
            lanes = slice(i * LANES, (i + 1) * LANES)
            tile = second[:, lanes] + pltpu.roll(early[:, lanes], wide, 1)
            m_out[first + i] = jnp.where(last, curve_row, tile)
        for i in range(NEAR):
            q = first + turned_by(i, NEAR)

            @pl.when(q != r)
            def _():
                move(q).start()

    loop(NEAR, put)
    m_in[r] = m_out[r]
    settle()

    await_arrivals(m_in.at[pl.ds(0, LINE - 1)], line_recv.at[0])
    tiles = [m_in[q] for q in range(LINE)]
    step_next = ratio(norm_next, to_column(tree_sum(tiles)[PAD - 1 :]))
    band = lax.broadcasted_iota(jnp.int32, (PAD, LANES), 1) // wide
    for four in range(LINE // 4):
        parts = [None, None]
        for i in range(4):
            tile = tiles[four * 4 + i]
            for k, value in enumerate((step_next * tile, tile)):
                shift = (i - k) % 4 * wide
                value = pltpu.roll(value, shift, 1) if shift else value
                parts[k] = value if i == 0 else jnp.where(band == i, value, parts[k])
        for k in range(2):
            out[k, :, four * LANES : (four + 1) * LANES] = parts[k]

    await_sent(m_out.at[pl.ds(0, LINE - 1)], far_send.at[0])


def fused(features, labels, destination, centres, tri_inverse, aux_inverse):
    own_rows, width = features.shape
    rows, cols = tri_inverse.shape
    chunk = rows // LINE
    slots = LINE * max(2, 2 * own_rows // LINE)

    def floats(*shape):
        return pltpu.VMEM(shape, jnp.float32)

    def halves(*shape):
        return pltpu.VMEM(shape, jnp.bfloat16)

    scratch = [
        halves(own_rows, width),
        pltpu.VMEM((1, own_rows), jnp.int32),
        halves(rows, width),
        pltpu.VMEM((1, own_rows), jnp.int32),
        floats(2, rows, cols),
        halves(2, rows, cols),
        halves(2, rows, cols),
        halves(LINE, PLANES * own_rows, chunk),
        floats(LINE, PAD, chunk),
        halves(own_rows, LINE * LANES),
        halves(own_rows, width),
        floats(PAD, own_rows),
        floats(PAD, own_rows),
        floats(4, LINE, PAD, chunk),
        floats(4, LINE, PAD, chunk),
        floats(4, LINE, PAD, chunk),
        halves(2, LINE, 2 * PAD, chunk // 2),
        floats(2, PAD, cols),
        floats(2, HALF, PAD, cols),
        floats(2, HALF, PAD, cols),
        floats(2, PAD, cols),
        floats(2, PAD, cols),
        floats(PAD, cols),
        floats(PAD, chunk),
        floats(2, HALF, PAD, cols),
        floats(2, LINE, PAD, cols),
        floats(2, PAD, cols),
        floats(2, NEAR, 2, PAD, chunk),
        floats(2, NEAR, 2, PAD, chunk),
        floats(2, HALF, PAD, chunk),
        floats(2, HALF, PAD, chunk),
        floats(2, PAD, PLANES * own_rows),
        floats(2, PAD, PLANES * own_rows),
        floats(PAD, PLANES * own_rows),
        floats(LINE, PAD, LANES),
        floats(LINE, PAD, LANES),
        dma((6,)),
        dma((2,)),
        dma((2,)),
        dma((2, LINE // NEAR)),
        dma((LINE,)),
        dma((1,)),
        dma((NEAR,)),
        pltpu.SemaphoreType.REGULAR,
        dma((4,)),
        dma((4,)),
    ]
    whole = pl.BlockSpec(memory_space=pltpu.VMEM)
    away = pl.BlockSpec(memory_space=pltpu.MemorySpace.HBM)
    second, early = pl.pallas_call(
        functools.partial(fused_kernel, float(own_rows * PLANES * LINE), 2.0 / width),
        out_shape=jax.ShapeDtypeStruct((2, PAD, slots), jnp.float32),
        in_specs=[away] * 6,
        out_specs=whole,
        scratch_shapes=scratch,
        compiler_params=pltpu.CompilerParams(
            collective_id=0, has_side_effects=True, vmem_limit_bytes=56 * 1024 * 1024
        ),
    )(
        features,
        labels[None, :],
        centres,
        destination.reshape(1, own_rows),
        tri_inverse,
        aux_inverse,
    )
    return early[:CLASSES] + second[:CLASSES]


def exact_product(dims, vector, block):
    parts = jnp.concatenate(three_parts(vector), axis=0).astype(jnp.bfloat16)
    total = None
    for part in reversed(block):
        product = dot(parts, part.astype(jnp.bfloat16), dims)
        product = product[2 * PAD :] + product[PAD : 2 * PAD] + product[:PAD]
        total = product if total is None else total + product
    return total


def forward_kernel(u_ref, block_ref, o_ref):
    o_ref[...] = exact_product(FLIPPED, u_ref[...], three_parts(block_ref[...]))


def backward_kernel(u_ref, block_ref, o_ref):
    product = exact_product(STRAIGHT, u_ref[...], three_parts(block_ref[...]))

    @pl.when(pl.program_id(0) == 0)
    def _():
        o_ref[...] = product

    @pl.when(pl.program_id(0) > 0)
    def _():
        o_ref[...] += product


STEP = 512

def factor_forward(block, vector):
    rows, cols = block.shape
    return pl.pallas_call(
        forward_kernel,
        grid=(rows // STEP,),
        in_specs=[
            pl.BlockSpec((PAD, cols), lambda i: (0, 0)),
            pl.BlockSpec((STEP, cols), lambda i: (i, 0)),
        ],
        out_specs=pl.BlockSpec((PAD, STEP), lambda i: (0, i)),
        out_shape=jax.ShapeDtypeStruct((PAD, rows), jnp.float32),
    )(vector, block)


def factor_backward(block, vector):
    rows, cols = block.shape
    return pl.pallas_call(
        backward_kernel,
        grid=(rows // STEP,),
        in_specs=[
            pl.BlockSpec((PAD, STEP), lambda i: (0, i)),
            pl.BlockSpec((STEP, cols), lambda i: (i, 0)),
        ],
        out_specs=pl.BlockSpec((PAD, cols), lambda i: (0, 0)),
        out_shape=jax.ShapeDtypeStruct((PAD, cols), jnp.float32),
    )(vector, block)


def square_norms(rows_x):
    return jnp.einsum("nd,nd->n", rows_x, rows_x, preferred_element_type=jnp.float32)


def plane_sum(x):
    return lax.psum(x, "rows")


def joint_sum(kind, nb, nr, block, *operands):
    x = operands[0]
    if kind == "plane":
        out = plane_sum(x)
        lines = jnp.arange(PAD, dtype=jnp.int32)[:, None]
        return out, factor_backward(block, jnp.where(lines < CLASSES, out, 0.0))
    if kind == "turn":
        width = x.shape[1] * nr // nb
        full = lax.all_gather(lax.psum(x, "blk") + operands[1], "rows", axis=1, tiled=True)
        out = lax.dynamic_slice_in_dim(full, lax.axis_index("blk") * width, width, 1)
        return out, factor_backward(block, out)
    if kind == "slice":
        size = x.shape[1] * nb // nr
        full = lax.all_gather(lax.psum(x, "rows"), "blk", axis=1, tiled=True)
        out = lax.dynamic_slice_in_dim(full, lax.axis_index("rows") * size, size, 1)
    else:
        out = operands[1] + operands[2] * lax.psum(x, "blk")
    return out, factor_forward(block, out)


def to_low(values):
    return lax.reduce_precision(values, 8, 7).astype(jnp.bfloat16)


def with_row(vector, scalars):
    return vector + jnp.pad(scalars[None, :], ((PAD - 1, 0), (0, vector.shape[1] - PAD)))


def on_device(nb, nr, features, labels, destination, centres, tri_inverse, aux_inverse):
    own_rows, width = features.shape
    capacity = max(2, 2 * own_rows // nr)
    scale = 2.0 / width
    count_all = float(own_rows * nb * nr)
    b = lax.axis_index("blk")
    class_rows = jnp.arange(PAD, dtype=jnp.int32)[:, None]
    real = class_rows < CLASSES

    tags = jnp.pad(labels.astype(jnp.bfloat16), (0, -own_rows % (16 * width)))
    tags = tags.reshape(-1, width)
    shared = lax.all_gather(jnp.concatenate([features, tags], axis=0), "blk", axis=0)
    rows_x = shared[:, :own_rows].reshape(nb * own_rows, width)
    tags = shared[:, own_rows:].reshape(nb, -1)[:, :own_rows].reshape(nb * own_rows)
    centre_norm = square_norms(centres)
    rows_norm = square_norms(rows_x)
    inner = lax.dot_general(
        rows_x, centres, (((1,), (1,)), ((), ())), preferred_element_type=jnp.float32
    )
    kmat = jnp.exp(-(rows_norm[:, None] + centre_norm[None, :] - 2.0 * inner) * scale).astype(
        jnp.bfloat16
    )
    hits = tags.astype(jnp.float32)[None, :] == class_rows.astype(jnp.float32)
    targets = jnp.where(real, jnp.where(hits, 1.0, -1.0), 0.0).astype(jnp.bfloat16)

    def clean(vector):
        return jnp.where(real, vector, 0.0)

    def onto_rows(low):
        return lax.dot_general(
            low, kmat, (((1,), (1,)), ((), ())), preferred_element_type=jnp.float32
        )

    def images(second):
        high = to_low(second)
        rest = second - high.astype(jnp.float32)
        mid = to_low(rest)
        low = to_low(rest - mid.astype(jnp.float32))
        three = onto_rows(jnp.concatenate([high, mid, low], axis=0))
        both = jnp.concatenate([three[:PAD], three[PAD : 2 * PAD] + three[2 * PAD :]], axis=0)
        both = lax.psum(both, "blk")
        image = to_low(both[:PAD])
        exact = both[:PAD] + both[PAD:]
        curve = jnp.sum(image.astype(jnp.float32) * exact, axis=1) / count_all
        return image, curve

    def ratio(above, below):
        return jnp.where(real, (above / below)[:, None], 0.0)

    def normal(vector):
        return jnp.sum(vector * vector, axis=1)

    start = jnp.dot(targets, kmat, preferred_element_type=jnp.float32) / count_all
    start = joint_sum("plane", nb, nr, tri_inverse, start)[1]
    start = joint_sum("turn", nb, nr, aux_inverse, start, jnp.zeros_like(start))[1]
    zeros = jnp.zeros_like(start)
    rhs, start = joint_sum("pair", nb, nr, aux_inverse, start, zeros, zeros + 1.0)
    first, start = joint_sum("slice", nb, nr, tri_inverse, start)
    joined = plane_sum(with_row(start, normal(rhs)))
    norm_first = joined[PAD - 1, :PAD]
    second = clean(joined)
    image, curve = images(second)
    curve = curve + ridge_weight * normal(first)
    gram = jnp.dot(image, kmat, preferred_element_type=jnp.float32) / count_all
    joined, turned = joint_sum("plane", nb, nr, tri_inverse, with_row(gram, curve))
    step_first = ratio(norm_first, joined[PAD - 1, :PAD])
    turned = joint_sum("turn", nb, nr, aux_inverse, turned, ridge_weight * first)[1]
    residual, start = joint_sum("pair", nb, nr, aux_inverse, turned, rhs, zeros - step_first)
    first_next, start = joint_sum("slice", nb, nr, tri_inverse, start)
    joined = plane_sum(with_row(start, normal(residual)))
    norm_next = joined[PAD - 1, :PAD]
    turn_weight = ratio(norm_next, norm_first)
    first_next = first_next + turn_weight * first
    second_next = clean(joined) + turn_weight * second
    image, curve = images(second_next)
    curve = curve + ridge_weight * normal(first_next)
    curve = lax.psum(jnp.pad(curve[:, None], ((0, 0), (0, 127))), "rows")[:, 0]
    step_next = ratio(norm_next, curve)
    coefficients = step_first * second + step_next * second_next
    scores = lax.psum(onto_rows(to_low(coefficients)), "blk")
    scores = lax.dynamic_slice_in_dim(scores, b * own_rows, own_rows, 1)

    target = destination[:, 0]
    row_ids = jnp.arange(own_rows, dtype=jnp.int32)
    same = (target[:, None] == target[None, :]) & (row_ids[None, :] < row_ids[:, None])
    before = jnp.sum(same.astype(jnp.int32), axis=1)
    slots = nr * capacity
    spread = (
        (target * capacity + before)[:, None] == jnp.arange(slots, dtype=jnp.int32)[None, :]
    ).astype(jnp.float32)
    placed = jnp.dot(scores, spread, precision=highest, preferred_element_type=jnp.float32)
    placed = placed.reshape(PAD, nr, capacity).transpose(1, 0, 2)
    lanes = -capacity % 128
    placed = jnp.pad(placed, ((0, 0), (0, 0), (0, lanes)))
    moved = lax.all_to_all(placed, "rows", split_axis=0, concat_axis=0, tiled=True)
    moved = moved[:, :CLASSES, :capacity]
    return moved.transpose(1, 0, 2).reshape(CLASSES, slots)


def solution(mesh):
    nb, nr = mesh.shape["blk"], mesh.shape["rows"]
    body = fused if (nb, nr) == (PLANES, LINE) else functools.partial(on_device, nb, nr)
    return jax.shard_map(
        body,
        mesh=mesh,
        in_specs=(
            P(("blk", "rows"), None),
            P(("blk", "rows")),
            P(("blk", "rows"), None),
            P("blk", None),
            P("blk", "rows"),
            P("blk", "rows"),
        ),
        out_specs=P(None, ("blk", "rows")),
        check_vma=False,
    )
```
